256 devices in a mesh: grp: 8 (over y, x_lo), brick: 32 (over z, x_hi, core).
Axes of the slice: x: 4 (x_hi: 2, x_lo: 2; x = x_hi * 2 + x_lo), y: 4, z: 8, core: 2. Of those that a mesh axis runs over, the one named last changes fastest.
Arguments:
- positions: float32 [3, 8388608], P(None, ('grp', 'brick')), may hold values from -4 to 4
- charges: float32 [8388608], P(('grp', 'brick')), may hold values from -5 to 5
- cluster_fill: int32 [65536], P(('grp', 'brick')), may hold values from 1 to 128, as said below
- cluster_cell: int32 [65536], P(('grp', 'brick')), may hold values from 0 to 131071
- send_index: int32 [1792, 32], P(('grp', 'brick')), may hold values from 0 to 255
- send_count: int32 [256, 7], P(('grp', 'brick')), may hold values from 1 to 32, as said below
- pair_local: int32 [262144], P(('grp', 'brick')), may hold values from 0 to 255
- pair_dir: int32 [262144], P(('grp', 'brick')), may hold values from 0 to 6, as said below
- pair_slot: int32 [262144], P(('grp', 'brick')), may hold values from 0 to 31
- ion_density: float32 [128, 1024, 256], P('grp', 'brick'), may hold values from 0.2 to 2
- potential_prev: float32 [128, 1024, 256], P('grp', 'brick'), may hold values from -6 to 6
- screening: float32 [128, 1024, 256], P('grp', 'brick'), may hold values from 0.05 to 0.5
Outputs:
- forces: float32 [3, 8388608], P(None, ('grp', 'brick'))
- potential: float32 [128, 1024, 256], P('grp', 'brick')
- ion_next: float32 [128, 1024, 256], P('grp', 'brick')
The draws below stay inside these ranges and needn't reach their ends.
Inputs may be any that keep to these rules, and one draw needn't show every extreme that they name: `cluster_fill`: live particles of a cluster; later slots are padding; some cluster is full. `send_count`: every device sends 32 live slots in some direction. `send_index`: local cluster indices; row e * 7 + k lists what device e sends to the device at minus the offset of direction k. `pair_local`: local cluster indices. `pair_dir`: a direction never names a device outside the room. `pair_slot`: slot indices; a slot at or past the sender's count carries no charge. `cluster_cell`: cell indices within a device's block.
All inputs are finite; a program needn't handle non-finite values.
Results may differ from the reference program's by a relative error of at most 0.0001.
Values sent between devices are 32-bit elements; how exact they have to be, the bound alone decides.
A program may use at most 192 MiB of HBM per device.

```python
import math
import jax
import jax.numpy as jnp
from jax import lax

CL_DEV = 256
PSIZE = 128
DIRS = 7
SLOTS = 32
PAIRS_DEV = 1024
GX = 16
GY = 32
GZ = 256
SWEEPS = 4
NX = 128
NY = 1024
CLUSTERS = 65536
PARTICLES = 8388608
PAIRS = 262144
N_GRP = 8
N_BRICK = 32
DEVICES = 256


def draw_cluster_fill(key, part):
    fill = jax.random.randint(key, (DEVICES * CL_DEV,), 1, PSIZE + 1, dtype=jnp.int32)
    return fill.at[0].set(PSIZE)


def draw_send_count(key, part):
    key_count, key_pick = jax.random.split(key)
    counts = jax.random.randint(key_count, (DEVICES, DIRS), 1, SLOTS + 1, dtype=jnp.int32)
    pick = jax.random.randint(key_pick, (DEVICES, 1), 0, DIRS, dtype=jnp.int32)
    columns = jnp.arange(DIRS, dtype=jnp.int32)[None, :]
    return jnp.where(columns == pick, SLOTS, counts)


def draw_pair_dir(key, part):
    raw = jax.random.randint(key, (DEVICES * PAIRS_DEV,), 0, DIRS, dtype=jnp.int32)
    device = jnp.arange(DEVICES * PAIRS_DEV, dtype=jnp.int32) // PAIRS_DEV
    slab = device // N_BRICK
    column = device % N_BRICK
    step_g = jnp.where(raw == 5, -1, jnp.where(raw == 6, 1, 0))
    step_b = jnp.where(raw == 1, -1, jnp.where(raw == 2, 1, jnp.where(raw == 3, -2, jnp.where(raw == 4, 2, 0))))
    valid = (slab + step_g >= 0) & (slab + step_g < N_GRP) & (column + step_b >= 0) & (column + step_b < N_BRICK)
    return jnp.where(valid, raw, 0).astype(jnp.int32)


def touch_ends(values, own_key, smallest, largest):
    longest = values.shape.index(max(values.shape))
    spots = []
    for shift in (0, 1):
        where = [jax.random.randint(jax.random.fold_in(own_key, axis), (), 0, length) for axis, length in enumerate(values.shape)]
        where[longest] = (where[longest] + shift) % values.shape[longest]
        spots.append(tuple(where))
    return values.at[spots[0]].set(smallest).at[spots[1]].set(largest)


def steps_of(key, extent, shards, smallest, high):
    gain, own = 1.0, jax.random.fold_in(key, 6)
    for dim, parts in shards:
        heights = jnp.exp(jax.random.uniform(jax.random.fold_in(own, dim), (parts,), jnp.float32, smallest / len(shards), high / len(shards)))
        gain = gain * jnp.repeat(heights, extent[dim] // parts).reshape([-1 if axis == dim else 1 for axis in range(len(extent))])
    return gain


def bell_draw(key, dims, deviation, limit, cuts=(), held_as=jnp.bfloat16):
    factor_of = steps_of(key, dims, cuts, -0.22, 0.18) if cuts else 1.0
    drawn = jax.random.normal(key, dims, jnp.float32) * deviation * factor_of
    return jnp.minimum(jnp.maximum(drawn, -limit), limit).astype(held_as)


def setup_inputs(seed: int = 0) -> dict:
    key_list = jax.random.split(jax.random.key(seed), 13)
    return {
        "positions": bell_draw(key_list[0], (3, PARTICLES), 1.0, 4.0, ((1, 256),), jnp.float32),
        "charges": bell_draw(key_list[1], (PARTICLES,), 1.0, 5.0, ((0, 256),), jnp.float32),
        "cluster_fill": draw_cluster_fill(jax.random.fold_in(key_list[12], 71), 0),
        "cluster_cell": touch_ends(jax.random.randint(key_list[3], (CLUSTERS,), 0, GX * GY * GZ), jax.random.fold_in(key_list[3], 1), 0, (GX * GY * GZ) - 1).astype(jnp.int32),
        "send_index": touch_ends(jax.random.randint(key_list[4], (DEVICES * DIRS, SLOTS), 0, CL_DEV), jax.random.fold_in(key_list[4], 1), 0, CL_DEV - 1).astype(jnp.int32),
        "send_count": draw_send_count(jax.random.fold_in(key_list[12], 71), 0),
        "pair_local": touch_ends(jax.random.randint(key_list[6], (PAIRS,), 0, CL_DEV), jax.random.fold_in(key_list[6], 1), 0, CL_DEV - 1).astype(jnp.int32),
        "pair_dir": draw_pair_dir(jax.random.fold_in(key_list[12], 71), 0),
        "pair_slot": touch_ends(jax.random.randint(key_list[8], (PAIRS,), 0, SLOTS), jax.random.fold_in(key_list[8], 1), 0, SLOTS - 1).astype(jnp.int32),
        "ion_density": jnp.clip(jnp.exp(math.log(2.0) - 2.3025851 * jax.random.uniform(key_list[9], (NX, NY, GZ), jnp.float32) ** steps_of(key_list[9], (NX, NY, GZ), ((0, 8), (1, 32)), -0.2, 0.2)), 0.2, 2.0),
        "potential_prev": bell_draw(key_list[10], (NX, NY, GZ), 1.0, 6.0, ((0, 8), (1, 32)), jnp.float32),
        "screening": jnp.clip(jnp.exp(math.log(0.5) - 2.3025851 * jax.random.uniform(key_list[11], (NX, NY, GZ), jnp.float32) ** steps_of(key_list[11], (NX, NY, GZ), ((0, 8), (1, 32)), -0.2, 0.2)), 0.05, 0.5),
    }


coulomb_scale = 0.02
softening = 0.1
field_scale = 0.5
deposit_scale = 0.2
lowest_eig = 0.01
highest_eig = 1.99
mobility = 0.3
diffusion = 0.2
time_step = 0.2

def offsets_of(dirs):
    step_g = jnp.where(dirs == 5, -1, jnp.where(dirs == 6, 1, 0)).astype(jnp.int32)
    step_b = jnp.where(dirs == 1, -1, jnp.where(dirs == 2, 1, jnp.where(dirs == 3, -2, jnp.where(dirs == 4, 2, 0)))).astype(jnp.int32)
    return (step_g, step_b)

def stencil_core(padded, center, screen):
    beside = padded[2:, 1:-1, 1:-1] + padded[:-2, 1:-1, 1:-1]
    beside = beside + padded[1:-1, 2:, 1:-1] + padded[1:-1, :-2, 1:-1]
    beside = beside + padded[1:-1, 1:-1, 2:] + padded[1:-1, 1:-1, :-2]
    return (6.0 + screen) * center - beside

def operate_plain(field, screen):
    return stencil_core(jnp.pad(field, 1), field, screen)

def chebyshev(start, rhs, screen):
    middle = 0.5 * (highest_eig + lowest_eig)
    spread = 0.5 * (highest_eig - lowest_eig)
    ratio_ms = middle / spread
    weight_now = 1.0 / ratio_ms
    inverse = 1.0 / (6.0 + screen)
    solution = start
    resid = rhs - operate_plain(solution, screen)
    update = inverse * resid / middle
    for turn in range(SWEEPS):
        solution = solution + update
        if turn + 1 < SWEEPS:
            resid = resid - operate_plain(update, screen)
            weight_next = 1.0 / (2.0 * ratio_ms - weight_now)
            update = weight_next * weight_now * update + 2.0 * weight_next / spread * (inverse * resid)
            weight_now = weight_next
    return solution

def tile_forces(own, other):
    diff = own[:, :3, :, None] - other[:, :3, None, :]
    dist = lax.optimization_barrier(jnp.sum(diff * diff, axis=1)) + softening
    weight = coulomb_scale * own[:, 3, :, None] * other[:, 3, None, :] / (dist * jnp.sqrt(dist))
    pull = diff * weight[:, None]
    return (lax.optimization_barrier(jnp.sum(pull, axis=3)), lax.optimization_barrier(jnp.sum(pull, axis=2)))

def face_div(pot, ions, axis):
    inner = [slice(1, -1), slice(1, -1), slice(1, -1)]
    inner[axis] = slice(None)
    pot = pot[tuple(inner)]
    ions = ions[tuple(inner)]

    def upper(arr):
        return lax.slice_in_dim(arr, 1, arr.shape[axis], axis=axis)

    def lower(arr):
        return lax.slice_in_dim(arr, 0, arr.shape[axis] - 1, axis=axis)
    speed = -mobility * (upper(pot) - lower(pot))
    flux = jnp.maximum(speed, 0.0) * lower(ions) + jnp.minimum(speed, 0.0) * upper(ions) - diffusion * (upper(ions) - lower(ions))
    return upper(flux) - lower(flux)

def field_of(padded):
    along_x = -(padded[2:, 1:-1, 1:-1] - padded[:-2, 1:-1, 1:-1]) * 0.5
    along_y = -(padded[1:-1, 2:, 1:-1] - padded[1:-1, :-2, 1:-1]) * 0.5
    along_z = -(padded[1:-1, 1:-1, 2:] - padded[1:-1, 1:-1, :-2]) * 0.5
    return jnp.stack([along_x, along_y, along_z])

def reference(positions, charges, cluster_fill, cluster_cell, send_index, send_count, pair_local, pair_dir, pair_slot, ion_density, potential_prev, screening):
    total = cluster_fill.shape[0]
    lanes = jnp.arange(PSIZE, dtype=jnp.int32)
    qmask = charges.reshape(total, PSIZE) * (lanes[None, :] < cluster_fill[:, None]).astype(jnp.float32)
    cluster_data = jnp.concatenate([positions.reshape(3, total, PSIZE).transpose(1, 0, 2), qmask[:, None, :]], axis=1)
    cluster_ids = jnp.arange(total, dtype=jnp.int32)
    owner = cluster_ids // CL_DEV
    grp_of = owner // N_BRICK
    brick_of = owner % N_BRICK
    cell_i = cluster_cell // (GY * GZ)
    cell_j = cluster_cell // GZ % GY
    cell_k = cluster_cell % GZ
    width_y = GY * N_BRICK
    flat = ((grp_of * GX + cell_i) * width_y + brick_of * GY + cell_j) * GZ + cell_k
    length_x = GX * N_GRP
    deposit = jnp.zeros(length_x * width_y * GZ, jnp.float32).at[flat].add(lax.optimization_barrier(jnp.sum(qmask, axis=1))).reshape(length_x, width_y, GZ)
    rhs = ion_density + deposit_scale * deposit
    pair_ids = jnp.arange(pair_local.shape[0], dtype=jnp.int32)
    device = pair_ids // PAIRS_DEV
    step_g, step_b = offsets_of(pair_dir)
    source = (device // N_BRICK + step_g) * N_BRICK + device % N_BRICK + step_b
    partner = source * CL_DEV + send_index[source * DIRS + pair_dir, pair_slot]
    alive = (pair_slot < send_count[source, pair_dir]).astype(jnp.float32)
    own_ids = device * CL_DEV + pair_local
    block = math.gcd(pair_local.shape[0], 256)

    def visit(accum, items):
        own_rows, other_rows, live_rows = items
        own = cluster_data[own_rows]
        other = cluster_data[other_rows]
        other = jnp.concatenate([other[:, :3], (other[:, 3] * live_rows[:, None])[:, None]], axis=1)
        pull_own, pull_other = tile_forces(own, other)
        accum = accum.at[own_rows].add(pull_own).at[other_rows].add(-pull_other)
        return (accum, None)
    coulomb, _ = lax.scan(visit, jnp.zeros((total, 3, PSIZE), jnp.float32), (own_ids.reshape(-1, block), partner.reshape(-1, block), alive.reshape(-1, block)))
    potential = chebyshev(potential_prev, rhs, screening)
    padded_pot = jnp.pad(potential, 1)
    padded_ion = jnp.pad(ion_density, 1)
    ion_next = ion_density - time_step * (face_div(padded_pot, padded_ion, 0) + face_div(padded_pot, padded_ion, 1) + face_div(padded_pot, padded_ion, 2))
    ecell = field_of(padded_pot).reshape(3, -1)[:, flat]
    forces = coulomb.transpose(1, 0, 2) + field_scale * qmask[None] * ecell[:, :, None]
    return (forces.reshape(3, -1), potential, ion_next)
```

```python
import functools

import jax
import jax.numpy as jnp
from jax import lax
from jax.experimental import pallas as pl
from jax.experimental.pallas import tpu as pltpu
from jax.sharding import PartitionSpec as P

F32, BF16, I32 = jnp.float32, jnp.bfloat16, jnp.int32
SWEEPS = 4
ROUNDS = SWEEPS + 1
coulomb_scale = 0.02
softening = 0.1
field_scale = 0.5
deposit_scale = 0.2
lowest_eig = 0.01
highest_eig = 1.99
mobility = 0.3
diffusion = 0.2
time_step = 0.2
OFFSETS = ((0, 0), (0, -1), (0, 1), (0, -2), (0, 2), (-1, 0), (1, 0))
MESH = pl.DeviceIdType.MESH
PAIRS_AT_ONCE = 8
GROUPS = 2
TOP = 8


def split3(v):
    high = v.astype(BF16).astype(F32)
    rest = v - high
    mid = rest.astype(BF16).astype(F32)
    return high, mid, (rest - mid).astype(BF16).astype(F32)


def dot(a, b, dims=((1,), (0,))):
    return lax.dot_general(a, b, (dims, ((), ())), preferred_element_type=F32)


def select_rows(chooser, data, dims=((1,), (0,)), parts=3):
    pieces = split3(data)[:parts]
    total = dot(chooser, pieces[0].astype(BF16), dims)
    for piece in pieces[1:]:
        total = total + dot(chooser, piece.astype(BF16), dims)
    return total


def neighbour(step_g, step_b, groups, bricks):
    g = lax.axis_index("grp")
    b = lax.axis_index("brick")
    return (lax.rem(g + step_g + groups, groups), lax.rem(b + step_b + bricks, bricks))


def greet(groups, bricks):
    barrier = pltpu.get_barrier_semaphore()
    for step in OFFSETS[1:]:
        pl.semaphore_signal(
            barrier, inc=1, device_id=neighbour(*step, groups, bricks), device_id_type=MESH
        )
    return barrier


def slot_row(index_ref):
    return jnp.concatenate([index_ref[k : k + 1, :] for k in range(index_ref.shape[0])], axis=1)


def column(row):
    return jnp.transpose(jnp.broadcast_to(row, (128, 128)))


def columns(values):
    vals = values.astype(F32)
    return jnp.concatenate([column(vals[i : i + 1, :]) for i in range(vals.shape[0])], axis=0)


def neighbours_sum(pad, i):
    rows = pad.shape[1] - 16
    centre = pad[i + 1, TOP : TOP + rows, :]
    total = pad[i + 2, TOP : TOP + rows, :] + pad[i, TOP : TOP + rows, :]
    total = total + pad[i + 1, TOP + 1 : TOP + rows + 1, :] + pad[i + 1, TOP - 1 : TOP + rows - 1, :]
    above, below = z_shifts(centre)
    return centre, total + above + below


def z_shifts(v):
    depth = v.shape[1]
    lane = lax.broadcasted_iota(I32, v.shape, 1)
    above = jnp.where(lane == depth - 1, 0.0, pltpu.roll(v, depth - 1, 1))
    below = jnp.where(lane == 0, 0.0, pltpu.roll(v, 1, 1))
    return above, below


def face_flux(pot_low, pot_high, ion_low, ion_high):
    speed = -mobility * (pot_high - pot_low)
    return (
        jnp.maximum(speed, 0.0) * ion_low
        + jnp.minimum(speed, 0.0) * ion_high
        - diffusion * (ion_high - ion_low)
    )


def field_kernel(
    groups,
    bricks,
    count_ref,
    pos_ref,
    charge_ref,
    fill_ref,
    cell_ref,
    index_ref,
    ion_ref,
    prev_ref,
    screen_ref,
    data_ref,
    arrived_ref,
    push_ref,
    pot_ref,
    next_ref,
    out_rows,
    in_rows,
    x_in,
    y_out,
    y_in,
    x_first,
    ion_pad,
    pad,
    resid,
    efield,
    row_send,
    row_recv,
    halo_send,
    halo_recv,
):
    clusters = charge_ref.shape[0]
    nx, ny, nz = ion_ref.shape
    g = lax.axis_index("grp")
    b = lax.axis_index("brick")
    barrier = greet(groups, bricks)

    fill_col = columns(fill_ref[...])
    lane = lax.broadcasted_iota(I32, (clusters, 128), 1).astype(F32)
    charge = charge_ref[...] * jnp.where(lane < fill_col, 1.0, 0.0)
    for d in range(3):
        data_ref[:, d * 128 : (d + 1) * 128] = pos_ref[:, d, :]
    data_ref[:, 384:512] = charge
    slots = index_ref.shape[1]
    wanted = slot_row(index_ref)
    total_slots = wanted.shape[1]
    chooser = jnp.where(
        lax.broadcasted_iota(I32, (clusters, total_slots), 0) == wanted, 1.0, 0.0
    ).astype(BF16)
    out_rows[...] = select_rows(chooser, data_ref[...], ((0,), (0,)))
    slot_id = lax.broadcasted_iota(I32, (slots, 128), 0)
    for k in range(len(OFFSETS)):
        live = jnp.where(slot_id < count_ref[0, k], 1.0, 0.0)
        out_rows[k * slots : (k + 1) * slots, 384:512] = (
            out_rows[k * slots : (k + 1) * slots, 384:512] * live
        )
    for i in range(nx):
        pad[0, i + 1, TOP : TOP + ny, :] = prev_ref[i]
        ion_pad[i + 1, TOP : TOP + ny, :] = ion_ref[i]
    y_out[0, 0, 0] = prev_ref[:, 0, :]
    y_out[0, 1, 0] = prev_ref[:, ny - 1, :]
    y_out[0, 0, 1] = ion_ref[:, 0, :]
    y_out[0, 1, 1] = ion_ref[:, ny - 1, :]
    for f, ref in enumerate((prev_ref, ion_ref)):
        x_first[0, f] = ref[0]
        x_first[1, f] = ref[nx - 1]
    pl.semaphore_wait(barrier, len(OFFSETS) - 1)

    def halo_copies(turn):
        held = turn % 2
        copies = []
        for side in range(2):
            step = 2 * side - 1
            if turn == 0:
                src, dst = x_first.at[side], x_in.at[0, 1 - side]
                ysrc, ydst = y_out.at[0, side], y_in.at[0, 1 - side]
            else:
                src = pad.at[held, 1 if side == 0 else nx, pl.ds(TOP, ny), :]
                dst = x_in.at[turn, 1 - side, 0]
                ysrc, ydst = y_out.at[turn, side, 0], y_in.at[turn, 1 - side, 0]
            copies.append(
                pltpu.make_async_remote_copy(
                    src_ref=src,
                    dst_ref=dst,
                    send_sem=halo_send.at[turn, side],
                    recv_sem=halo_recv.at[turn, 1 - side],
                    device_id=neighbour(step, 0, groups, bricks),
                    device_id_type=MESH,
                )
            )
            copies.append(
                pltpu.make_async_remote_copy(
                    src_ref=ysrc,
                    dst_ref=ydst,
                    send_sem=halo_send.at[turn, 2 + side],
                    recv_sem=halo_recv.at[turn, 3 - side],
                    device_id=neighbour(0, step, groups, bricks),
                    device_id_type=MESH,
                )
            )
        return copies

    def start_halos(turn):
        held = turn % 2
        if turn:
            y_out[turn, 0, 0] = pad[held, 1 : nx + 1, TOP, :]
            y_out[turn, 1, 0] = pad[held, 1 : nx + 1, TOP + ny - 1, :]
        copies = halo_copies(turn)
        for copy in copies:
            copy.start()
        return copies

    inside = (
        jnp.where(g > 0, 1.0, 0.0),
        jnp.where(g < groups - 1, 1.0, 0.0),
        jnp.where(b > 0, 1.0, 0.0),
        jnp.where(b < bricks - 1, 1.0, 0.0),
    )

    def place(target, turn, field):
        target[0, TOP : TOP + ny, :] = x_in[turn, 0, field] * inside[0]
        target[nx + 1, TOP : TOP + ny, :] = x_in[turn, 1, field] * inside[1]
        target[1 : nx + 1, TOP - 1, :] = y_in[turn, 0, field] * inside[2]
        target[1 : nx + 1, TOP + ny, :] = y_in[turn, 1, field] * inside[3]

    halos = start_halos(0)
    sends = []
    for k in range(1, len(OFFSETS)):
        step_g, step_b = OFFSETS[k]
        copy = pltpu.make_async_remote_copy(
            src_ref=out_rows.at[pl.ds(k * slots, slots), :],
            dst_ref=in_rows.at[pl.ds((k - 1) * slots, slots), :],
            send_sem=row_send.at[k - 1],
            recv_sem=row_recv.at[k - 1],
            device_id=neighbour(-step_g, -step_b, groups, bricks),
            device_id_type=MESH,
        )
        copy.start()
        sends.append(copy)

    cell = cell_ref[...]
    row_of = cell // nz
    row_line = jnp.concatenate([row_of[i : i + 1, :] for i in range(row_of.shape[0])], axis=1)
    into = jnp.where(
        lax.broadcasted_iota(I32, (nx * ny, clusters), 0) == row_line, 1.0, 0.0
    ).astype(BF16)
    k_col = columns(cell - row_of * nz)
    k_col = jnp.concatenate([k_col, k_col], axis=1)
    at_depth = jnp.where(
        lax.broadcasted_iota(I32, (clusters, nz), 1).astype(F32) == k_col, 1.0, 0.0
    )
    deposit = select_rows(into, at_depth * jnp.sum(charge, axis=1, keepdims=True))
    resid[...] = ion_ref[...] + deposit_scale * deposit.reshape(nx, ny, nz)

    middle = 0.5 * (highest_eig + lowest_eig)
    spread = 0.5 * (highest_eig - lowest_eig)
    ratio_ms = middle / spread
    weight_now = 1.0 / ratio_ms
    for copy in halos:
        copy.wait()
    place(pad.at[0], 0, 0)
    place(ion_pad, 0, 1)

    def first(i, carry):
        centre, around = neighbours_sum(pad.at[0], i)
        diag = 6.0 + screen_ref[i]
        rest = resid[i] - (diag * centre - around)
        resid[i] = rest
        update = rest / diag / middle
        pad[1, i + 1, TOP : TOP + ny, :] = update
        pot_ref[i] = centre + update
        return carry

    lax.fori_loop(0, nx, first, 0, unroll=2)
    for turn in range(1, SWEEPS):
        halos = start_halos(turn)
        weight_next = 1.0 / (2.0 * ratio_ms - weight_now)
        last = turn == SWEEPS - 1
        for copy in halos:
            copy.wait()
        held = turn % 2
        place(pad.at[held], turn, 0)

        def sweep(i, carry, held=held, weight_next=weight_next, weight_now=weight_now, last=last):
            centre, around = neighbours_sum(pad.at[held], i)
            diag = 6.0 + screen_ref[i]
            rest = resid[i] - (diag * centre - around)
            resid[i] = rest
            update = weight_next * weight_now * centre + 2.0 * weight_next / spread * (rest / diag)
            done = pot_ref[i] + update
            pot_ref[i] = done
            pad[1 - held, i + 1, TOP : TOP + ny, :] = done if last else update
            return carry

        lax.fori_loop(0, nx, sweep, 0, unroll=2)
        weight_now = weight_next
    halos = start_halos(SWEEPS)
    for copy in halos:
        copy.wait()
    pot = pad.at[SWEEPS % 2]
    place(pot, SWEEPS, 0)

    def finish(i, carry):
        lo, hi = TOP, TOP + ny
        p, n = pot[i + 1, lo:hi, :], ion_pad[i + 1, lo:hi, :]
        px = (pot[i, lo:hi, :], pot[i + 2, lo:hi, :])
        py = (pot[i + 1, lo - 1 : hi - 1, :], pot[i + 1, lo + 1 : hi + 1, :])
        ix = (ion_pad[i, lo:hi, :], ion_pad[i + 2, lo:hi, :])
        iy = (ion_pad[i + 1, lo - 1 : hi - 1, :], ion_pad[i + 1, lo + 1 : hi + 1, :])
        pz = z_shifts(p)[::-1]
        iz = z_shifts(n)[::-1]
        out = jnp.zeros_like(p)
        for d, (ps, ns) in enumerate(((px, ix), (py, iy), (pz, iz))):
            out = out + (face_flux(p, ps[1], n, ns[1]) - face_flux(ps[0], p, ns[0], n))
            efield[d, pl.ds(pl.multiple_of(i * ny, ny), ny), :] = -(ps[1] - ps[0]) * 0.5
        next_ref[i] = n - time_step * out
        return carry

    lax.fori_loop(0, nx, finish, 0)
    for d in range(3):
        seen = select_rows(into, efield[d], ((0,), (0,)))
        here = jnp.sum(seen * at_depth, axis=1, keepdims=True)
        push_ref[:, d * 128 : (d + 1) * 128] = field_scale * data_ref[:, 384:512] * here
    for copy in sends:
        copy.wait()
    arrived_ref[0:slots, :] = out_rows[0:slots, :]
    arrived_ref[slots:, :] = in_rows[...]


def features(data_ref, feat, vals, own):
    spots = [data_ref[:, d * 128 : (d + 1) * 128] for d in range(3)]
    charge = data_ref[:, 384:512]
    square = jnp.zeros_like(charge)
    for d in range(3):
        high, mid, low = split3(spots[d])
        rows = (high, high, mid, mid, high, low) if own else (high, mid, high, mid, low, high)
        for f, row in enumerate(rows):
            feat[:, 6 * d + f, :] = -2.0 * row if own else row
        square = square + spots[d] * spots[d]
    if own:
        square = square + softening
    one = jnp.ones_like(square)
    for f, row in enumerate(split3(square)):
        feat[:, (18 if own else 21) + f, :] = row
        feat[:, (21 if own else 18) + f, :] = one
    for c, val in enumerate((charge, charge * spots[0], charge * spots[1], charge * spots[2])):
        for f, row in enumerate(split3(val)):
            vals[:, 4 * f + c, :] = row
    for f in range(12, 16):
        vals[:, f, :] = jnp.zeros_like(charge)


def tile_sums(own_ids, part_ids, own_feat, own_vals, part_feat, part_vals):
    left = jnp.concatenate([own_feat[o] for o in own_ids], axis=0).astype(BF16)
    blank = jnp.zeros((24, 128), F32)
    count = len(own_ids)
    right = jnp.concatenate(
        [
            jnp.concatenate([part_feat[r] if i == j else blank for i in range(count)], axis=0).astype(BF16)
            for j, r in enumerate(part_ids)
        ],
        axis=1,
    )
    dist = dot(left, right, ((0,), (0,)))
    sums = []
    for j in range(count):
        root = lax.rsqrt(dist[:, j * 128 : (j + 1) * 128])
        u = root * root * root
        high = u.astype(BF16)
        low = (u - high.astype(F32)).astype(BF16)
        mine = own_vals[own_ids[j]].astype(BF16)
        theirs = part_vals[part_ids[j]].astype(BF16)
        on_part = dot(jnp.concatenate([mine, mine], axis=1), jnp.concatenate([high, low], axis=0))
        on_own = dot(
            jnp.concatenate([theirs, theirs], axis=1),
            jnp.concatenate([high, low], axis=1),
            ((1,), (1,)),
        )
        sums.append((on_own, on_part))
    return sums


def pair_kernel(
    local_ref,
    dir_ref,
    slot_ref,
    data_ref,
    arrived_ref,
    own_ref,
    part_ref,
    own_feat,
    own_vals,
    part_feat,
    part_vals,
    own_acc,
    part_acc,
):
    features(data_ref, own_feat, own_vals, True)
    features(arrived_ref, part_feat, part_vals, False)
    own_acc[...] = jnp.zeros_like(own_acc)
    part_acc[...] = jnp.zeros_like(part_acc)
    slots = arrived_ref.shape[0] // len(OFFSETS)
    step = PAIRS_AT_ONCE * GROUPS

    @pl.loop(0, local_ref.shape[0] // step)
    def _(turn):
        done = []
        for group in range(GROUPS):
            base = turn * step + group * PAIRS_AT_ONCE
            own_ids = [local_ref[base + j] for j in range(PAIRS_AT_ONCE)]
            part_ids = [
                dir_ref[base + j] * slots + slot_ref[base + j] for j in range(PAIRS_AT_ONCE)
            ]
            done.append(
                (own_ids, part_ids, tile_sums(own_ids, part_ids, own_feat, own_vals, part_feat, part_vals))
            )
        for own_ids, part_ids, sums in done:
            for j, (on_own, on_part) in enumerate(sums):
                own_acc[own_ids[j]] += on_own
                part_acc[part_ids[j]] += on_part

    for acc, out in ((own_acc, own_ref), (part_acc, part_ref)):
        for c in range(4):
            out[:, c * 128 : (c + 1) * 128] = acc[:, c, :] + (acc[:, 4 + c, :] + acc[:, 8 + c, :])


def return_kernel(
    groups,
    bricks,
    count_ref,
    index_ref,
    data_ref,
    own_ref,
    part_ref,
    push_ref,
    out_ref,
    back,
    row_send,
    row_recv,
):
    clusters = data_ref.shape[0]
    slots = index_ref.shape[1]
    barrier = greet(groups, bricks)
    pl.semaphore_wait(barrier, len(OFFSETS) - 1)
    copies = []
    for k in range(1, len(OFFSETS)):
        copy = pltpu.make_async_remote_copy(
            src_ref=part_ref.at[pl.ds(k * slots, slots), :],
            dst_ref=back.at[pl.ds(k * slots, slots), :],
            send_sem=row_send.at[k - 1],
            recv_sem=row_recv.at[k - 1],
            device_id=neighbour(*OFFSETS[k], groups, bricks),
            device_id_type=MESH,
        )
        copy.start()
        copies.append(copy)
    back[0:slots, :] = part_ref[0:slots, :]
    wanted = slot_row(index_ref)
    total_slots = wanted.shape[1]
    spot = lax.broadcasted_iota(I32, (1, slots), 1)
    live = jnp.concatenate(
        [jnp.where(spot < count_ref[0, k], 1.0, 0.0) for k in range(len(OFFSETS))], axis=1
    )
    chooser = jnp.where(
        lax.broadcasted_iota(I32, (clusters, total_slots), 0) == wanted,
        jnp.broadcast_to(live, (clusters, total_slots)),
        0.0,
    ).astype(BF16)
    for copy in copies:
        copy.wait()
    sums = own_ref[...] + select_rows(chooser, back[...])
    charge = coulomb_scale * data_ref[:, 384:512]
    for d in range(3):
        pull = data_ref[:, d * 128 : (d + 1) * 128] * sums[:, 0:128] - sums[:, (d + 1) * 128 : (d + 2) * 128]
        out_ref[:, d, :] = charge * pull + push_ref[:, d * 128 : (d + 1) * 128]


def shards(
    groups,
    bricks,
    positions,
    charges,
    cluster_fill,
    cluster_cell,
    send_index,
    send_count,
    pair_local,
    pair_dir,
    pair_slot,
    ion_density,
    potential_prev,
    screening,
):
    clusters = cluster_fill.shape[0]
    psize = charges.shape[0] // clusters
    dirs, slots = send_index.shape
    nx, ny, nz = ion_density.shape
    placed = positions.reshape(3, clusters, psize).transpose(1, 0, 2)
    vmem = pl.BlockSpec(memory_space=pltpu.VMEM)
    smem = pl.BlockSpec(memory_space=pltpu.SMEM)
    shape = lambda *dims: jax.ShapeDtypeStruct(dims, F32)
    data, arrived, push, potential, ion_next = pl.pallas_call(
        functools.partial(field_kernel, groups, bricks),
        out_shape=(
            shape(clusters, 4 * psize),
            shape(dirs * slots, 4 * psize),
            shape(clusters, 3 * psize),
            shape(nx, ny, nz),
            shape(nx, ny, nz),
        ),
        in_specs=[smem] + [vmem] * 8,
        out_specs=[vmem] * 5,
        scratch_shapes=[
            pltpu.VMEM((dirs * slots, 4 * psize), F32),
            pltpu.VMEM(((dirs - 1) * slots, 4 * psize), F32),
            pltpu.VMEM((ROUNDS, 2, 2, ny, nz), F32),
            pltpu.VMEM((ROUNDS, 2, 2, nx, nz), F32),
            pltpu.VMEM((ROUNDS, 2, 2, nx, nz), F32),
            pltpu.VMEM((2, 2, ny, nz), F32),
            pltpu.VMEM((nx + 2, ny + 16, nz), F32),
            pltpu.VMEM((2, nx + 2, ny + 16, nz), F32),
            pltpu.VMEM((nx, ny, nz), F32),
            pltpu.VMEM((3, nx * ny, nz), F32),
            pltpu.SemaphoreType.DMA((dirs - 1,)),
            pltpu.SemaphoreType.DMA((dirs - 1,)),
            pltpu.SemaphoreType.DMA((ROUNDS, 4)),
            pltpu.SemaphoreType.DMA((ROUNDS, 4)),
        ],
        compiler_params=pltpu.CompilerParams(
            collective_id=0, has_side_effects=True, vmem_limit_bytes=48 << 20
        ),
        name="field",
    )(
        send_count,
        placed,
        charges.reshape(clusters, psize),
        cluster_fill.reshape(clusters // 128, 128),
        cluster_cell.reshape(clusters // 128, 128),
        send_index,
        ion_density,
        potential_prev,
        screening,
    )
    own_sums, part_sums = pl.pallas_call(
        pair_kernel,
        out_shape=(shape(clusters, 4 * psize), shape(dirs * slots, 4 * psize)),
        in_specs=[smem] * 3 + [vmem] * 2,
        out_specs=[vmem] * 2,
        scratch_shapes=[
            pltpu.VMEM((clusters, 24, psize), F32),
            pltpu.VMEM((clusters, 16, psize), F32),
            pltpu.VMEM((dirs * slots, 24, psize), F32),
            pltpu.VMEM((dirs * slots, 16, psize), F32),
            pltpu.VMEM((clusters, 16, psize), F32),
            pltpu.VMEM((dirs * slots, 16, psize), F32),
        ],
        compiler_params=pltpu.CompilerParams(vmem_limit_bytes=48 << 20),
        name="pairs",
    )(pair_local, pair_dir, pair_slot, data, arrived)
    forces = pl.pallas_call(
        functools.partial(return_kernel, groups, bricks),
        out_shape=shape(clusters, 3, psize),
        in_specs=[smem] + [vmem] * 5,
        out_specs=vmem,
        scratch_shapes=[
            pltpu.VMEM((dirs * slots, 4 * psize), F32),
            pltpu.SemaphoreType.DMA((dirs - 1,)),
            pltpu.SemaphoreType.DMA((dirs - 1,)),
        ],
        compiler_params=pltpu.CompilerParams(
            collective_id=1, has_side_effects=True, vmem_limit_bytes=48 << 20
        ),
        name="forces",
    )(send_count, send_index, data, own_sums, part_sums, push)
    return (forces.transpose(1, 0, 2).reshape(3, -1), potential, ion_next)


def solution(mesh):
    in_specs = (
        P(None, ("grp", "brick")),
        P(("grp", "brick")),
        P(("grp", "brick")),
        P(("grp", "brick")),
        P(("grp", "brick"), None),
        P(("grp", "brick"), None),
        P(("grp", "brick")),
        P(("grp", "brick")),
        P(("grp", "brick")),
        P("grp", "brick", None),
        P("grp", "brick", None),
        P("grp", "brick", None),
    )
    out_specs = (P(None, ("grp", "brick")), P("grp", "brick", None), P("grp", "brick", None))
    body = functools.partial(shards, mesh.shape["grp"], mesh.shape["brick"])
    return jax.shard_map(body, mesh=mesh, in_specs=in_specs, out_specs=out_specs, check_vma=False)
```

```python
import functools

import jax
import jax.numpy as jnp
from jax import lax
from jax.experimental import pallas as pl
from jax.experimental.pallas import tpu as pltpu
from jax.sharding import PartitionSpec as P

F32, BF16, I32 = jnp.float32, jnp.bfloat16, jnp.int32
SWEEPS = 4
EARLY = 3
coulomb_scale = 0.02
softening = 0.1
field_scale = 0.5
deposit_scale = 0.2
lowest_eig = 0.01
highest_eig = 1.99
mobility = 0.3
diffusion = 0.2
time_step = 0.2
OFFSETS = ((0, 0), (0, -1), (0, 1), (0, -2), (0, 2), (-1, 0), (1, 0))
MESH = pl.DeviceIdType.MESH
PAIRS_AT_ONCE = 8
GROUPS = 4
TOP = 8


def split3(v):
    high = v.astype(BF16).astype(F32)
    rest = v - high
    mid = rest.astype(BF16).astype(F32)
    return high, mid, (rest - mid).astype(BF16).astype(F32)


def dot(a, b, dims=((1,), (0,))):
    return lax.dot_general(a, b, (dims, ((), ())), preferred_element_type=F32)


def select_rows(chooser, data, dims=((1,), (0,)), parts=3):
    pieces = split3(data)[:parts]
    total = dot(chooser, pieces[0].astype(BF16), dims)
    for piece in pieces[1:]:
        total = total + dot(chooser, piece.astype(BF16), dims)
    return total


def neighbour(step_g, step_b, groups, bricks):
    g = lax.axis_index("grp")
    b = lax.axis_index("brick")
    return (lax.rem(g + step_g + groups, groups), lax.rem(b + step_b + bricks, bricks))


def greet(groups, bricks):
    barrier = pltpu.get_barrier_semaphore()
    for step in OFFSETS[1:]:
        pl.semaphore_signal(
            barrier, inc=1, device_id=neighbour(*step, groups, bricks), device_id_type=MESH
        )
    return barrier


def slot_row(index_ref):
    return jnp.concatenate([index_ref[k : k + 1, :] for k in range(index_ref.shape[0])], axis=1)


def column(row):
    return jnp.transpose(jnp.broadcast_to(row, (128, 128)))


def columns(values):
    vals = values.astype(F32)
    return jnp.concatenate([column(vals[i : i + 1, :]) for i in range(vals.shape[0])], axis=0)


def neighbours_sum(pad, i):
    rows = pad.shape[1] - 16
    centre = pad[i + 1, TOP : TOP + rows, :]
    total = pad[i + 2, TOP : TOP + rows, :] + pad[i, TOP : TOP + rows, :]
    total = total + pad[i + 1, TOP + 1 : TOP + rows + 1, :] + pad[i + 1, TOP - 1 : TOP + rows - 1, :]
    above, below = z_shifts(centre)
    return centre, total + above + below


def z_shifts(v):
    depth = v.shape[1]
    lane = lax.broadcasted_iota(I32, v.shape, 1)
    above = jnp.where(lane == depth - 1, 0.0, pltpu.roll(v, depth - 1, 1))
    below = jnp.where(lane == 0, 0.0, pltpu.roll(v, 1, 1))
    return above, below


def face_flux(pot_low, pot_high, ion_low, ion_high):
    speed = -mobility * (pot_high - pot_low)
    return (
        jnp.maximum(speed, 0.0) * ion_low
        + jnp.minimum(speed, 0.0) * ion_high
        - diffusion * (ion_high - ion_low)
    )


def inside_flags(groups, bricks):
    g = lax.axis_index("grp")
    b = lax.axis_index("brick")
    return (
        jnp.where(g > 0, 1.0, 0.0),
        jnp.where(g < groups - 1, 1.0, 0.0),
        jnp.where(b > 0, 1.0, 0.0),
        jnp.where(b < bricks - 1, 1.0, 0.0),
    )


def start_halos(fields, turn, x_out, x_in, y_out, y_in, send, recv, groups, bricks):
    nx, ny = fields[0].shape[0] - 2, fields[0].shape[1] - 2 * TOP
    for f, field in enumerate(fields):
        y_out[turn, 0, f] = field[1 : nx + 1, TOP, :]
        y_out[turn, 1, f] = field[1 : nx + 1, TOP + ny - 1, :]
        x_out[turn, 0, f] = field[1, TOP : TOP + ny, :]
        x_out[turn, 1, f] = field[nx, TOP : TOP + ny, :]
    count = len(fields)
    copies = []
    for side in range(2):
        step = 2 * side - 1
        for axis, (out, into) in enumerate(((x_out, x_in), (y_out, y_in))):
            copy = pltpu.make_async_remote_copy(
                src_ref=out.at[turn, side, pl.ds(0, count)],
                dst_ref=into.at[turn, 1 - side, pl.ds(0, count)],
                send_sem=send.at[turn, 2 * axis + side],
                recv_sem=recv.at[turn, 2 * axis + 1 - side],
                device_id=neighbour(step * (1 - axis), step * axis, groups, bricks),
                device_id_type=MESH,
            )
            copy.start()
            copies.append(copy)
    return copies


def finish_halos(copies, fields, turn, x_in, y_in, inside):
    for copy in copies:
        copy.wait()
    nx, ny = fields[0].shape[0] - 2, fields[0].shape[1] - 2 * TOP
    for f, field in enumerate(fields):
        field[0, TOP : TOP + ny, :] = x_in[turn, 0, f] * inside[0]
        field[nx + 1, TOP : TOP + ny, :] = x_in[turn, 1, f] * inside[1]
        field[1 : nx + 1, TOP - 1, :] = y_in[turn, 0, f] * inside[2]
        field[1 : nx + 1, TOP + ny, :] = y_in[turn, 1, f] * inside[3]


def send_rows(source, target, towards, send, recv, groups, bricks):
    slots = source.shape[0] // len(OFFSETS)
    copies = []
    for k in range(1, len(OFFSETS)):
        step_g, step_b = OFFSETS[k]
        copy = pltpu.make_async_remote_copy(
            src_ref=source.at[pl.ds(k * slots, slots), :],
            dst_ref=target.at[pl.ds(k * slots, slots), :],
            send_sem=send.at[k - 1],
            recv_sem=recv.at[k - 1],
            device_id=neighbour(towards * step_g, towards * step_b, groups, bricks),
            device_id_type=MESH,
        )
        copy.start()
        copies.append(copy)
    return copies


def weights():
    middle = 0.5 * (highest_eig + lowest_eig)
    spread = 0.5 * (highest_eig - lowest_eig)
    ratio_ms = middle / spread
    now = 1.0 / ratio_ms
    table = [(0.0, 1.0 / middle)]
    for _ in range(SWEEPS - 1):
        after = 1.0 / (2.0 * ratio_ms - now)
        table.append((after * now, 2.0 * after / spread))
        now = after
    return table


def sweep(turn, held, other, resid, screen, total):
    keep, gain = weights()[turn]
    nx, ny, nz = resid.shape

    def plane(i, carry):
        centre, around = neighbours_sum(held, i)
        diag = 6.0 + screen[i]
        rest = resid[i] - (diag * centre - around)
        resid[i] = rest
        update = gain * (rest / diag)
        if turn:
            update = keep * centre + update
            total[i] = total[i] + update
        else:
            total[i] = centre + update
        other[i + 1, TOP : TOP + ny, :] = update
        return carry

    lax.fori_loop(0, nx, plane, 0, unroll=2)


def cell_tables(cell_ref, nx, ny, nz):
    cell = cell_ref[...]
    clusters = cell.shape[0] * cell.shape[1]
    row_of = cell // nz
    row_line = jnp.concatenate([row_of[i : i + 1, :] for i in range(cell.shape[0])], axis=1)
    into = jnp.where(
        lax.broadcasted_iota(I32, (nx * ny, clusters), 0) == row_line, 1.0, 0.0
    ).astype(BF16)
    k_col = columns(cell - row_of * nz)
    k_col = jnp.concatenate([k_col, k_col], axis=1)
    at_depth = jnp.where(
        lax.broadcasted_iota(I32, (clusters, nz), 1).astype(F32) == k_col, 1.0, 0.0
    )
    return into, at_depth


def send_kernel(
    groups,
    bricks,
    count_ref,
    pos_hbm,
    charge_hbm,
    fill_hbm,
    cell_hbm,
    index_hbm,
    ion_hbm,
    prev_hbm,
    screen_hbm,
    data_ref,
    arrived_ref,
    update_ref,
    resid_ref,
    total_ref,
    pos,
    charges,
    fill,
    cells,
    index,
    screen,
    out_rows,
    in_rows,
    x_out,
    x_in,
    y_out,
    y_in,
    pad,
    load,
    row_send,
    row_recv,
    halo_send,
    halo_recv,
):
    nx, ny, nz = ion_hbm.shape
    loads = [
        pltpu.make_async_copy(src, dst, load.at[i])
        for i, (src, dst) in enumerate(
            (
                (index_hbm, index),
                (fill_hbm, fill),
                (cell_hbm, cells),
                (prev_hbm, pad.at[0, pl.ds(1, nx), pl.ds(TOP, ny), :]),
                (pos_hbm, pos),
                (charge_hbm, charges),
                (ion_hbm, resid_ref),
                (screen_hbm, screen),
            )
        )
    ]
    for copy in loads:
        copy.start()
    barrier = greet(groups, bricks)
    inside = inside_flags(groups, bricks)
    for copy in loads[:4]:
        copy.wait()
    exchange = (x_out, x_in, y_out, y_in, halo_send, halo_recv, groups, bricks)
    clusters = charges.shape[0]
    slots = index.shape[1]
    wanted = slot_row(index)
    chooser = jnp.where(
        lax.broadcasted_iota(I32, (clusters, wanted.shape[1]), 0) == wanted, 1.0, 0.0
    ).astype(BF16)
    fill_col = columns(fill[...])
    lane = lax.broadcasted_iota(I32, (clusters, 128), 1).astype(F32)
    for copy in loads[4:]:
        copy.wait()
    charge = charges[...] * jnp.where(lane < fill_col, 1.0, 0.0)
    for d in range(3):
        data_ref[:, d * 128 : (d + 1) * 128] = pos[:, d, :]
    data_ref[:, 384:512] = charge
    pl.semaphore_wait(barrier, len(OFFSETS) - 1)
    halos = start_halos([pad.at[0]], 0, *exchange)
    out_rows[...] = select_rows(chooser, data_ref[...], ((0,), (0,)))
    slot_id = lax.broadcasted_iota(I32, (slots, 128), 0)
    for k in range(len(OFFSETS)):
        live = jnp.where(slot_id < count_ref[0, k], 1.0, 0.0)
        out_rows[k * slots : (k + 1) * slots, 384:512] = (
            out_rows[k * slots : (k + 1) * slots, 384:512] * live
        )
    sends = send_rows(out_rows, in_rows, -1, row_send, row_recv, groups, bricks)
    into, at_depth = cell_tables(cells, nx, ny, nz)
    deposit = select_rows(into, at_depth * jnp.sum(charge, axis=1, keepdims=True))
    resid_ref[...] = resid_ref[...] + deposit_scale * deposit.reshape(nx, ny, nz)
    for turn in range(EARLY):
        held, other = pad.at[turn % 2], pad.at[1 - turn % 2]
        if turn:
            halos = start_halos([held], turn, *exchange)
        finish_halos(halos, [held], turn, x_in, y_in, inside)
        sweep(turn, held, other, resid_ref, screen, total_ref)
    update_ref[...] = pad[EARLY % 2, 1 : nx + 1, TOP : TOP + ny, :]
    for copy in sends:
        copy.wait()
    arrived_ref[0:slots, :] = out_rows[0:slots, :]
    arrived_ref[slots:, :] = in_rows[slots:, :]


def return_kernel(
    groups,
    bricks,
    count_ref,
    cell_hbm,
    index_hbm,
    ion_hbm,
    screen_hbm,
    data_ref,
    own_ref,
    part_ref,
    update_ref,
    resid_ref,
    total_ref,
    force_ref,
    pot_ref,
    next_ref,
    cells,
    index,
    screen,
    back,
    resid,
    x_out,
    x_in,
    y_out,
    y_in,
    pad,
    ion,
    efield,
    load,
    row_send,
    row_recv,
    halo_send,
    halo_recv,
):
    nx, ny, nz = ion_hbm.shape
    loads = [
        pltpu.make_async_copy(src, dst, load.at[i])
        for i, (src, dst) in enumerate(
            (
                (ion_hbm, ion.at[pl.ds(1, nx), pl.ds(TOP, ny), :]),
                (screen_hbm, screen),
                (index_hbm, index),
                (cell_hbm, cells),
            )
        )
    ]
    for copy in loads:
        copy.start()
    barrier = greet(groups, bricks)
    inside = inside_flags(groups, bricks)
    pad[EARLY % 2, 1 : nx + 1, TOP : TOP + ny, :] = update_ref[...]
    resid[...] = resid_ref[...]
    pot_ref[...] = total_ref[...]
    for copy in loads:
        copy.wait()
    exchange = (x_out, x_in, y_out, y_in, halo_send, halo_recv, groups, bricks)
    pl.semaphore_wait(barrier, len(OFFSETS) - 1)
    halos = start_halos([pad.at[EARLY % 2], ion], 0, *exchange)
    sends = send_rows(part_ref, back, 1, row_send, row_recv, groups, bricks)
    clusters = data_ref.shape[0]
    slots = index.shape[1]
    back[0:slots, :] = part_ref[0:slots, :]
    wanted = slot_row(index)
    spot = lax.broadcasted_iota(I32, (1, slots), 1)
    live = jnp.concatenate(
        [jnp.where(spot < count_ref[0, k], 1.0, 0.0) for k in range(len(OFFSETS))], axis=1
    )
    chooser = jnp.where(
        lax.broadcasted_iota(I32, (clusters, wanted.shape[1]), 0) == wanted,
        jnp.broadcast_to(live, (clusters, wanted.shape[1])),
        0.0,
    ).astype(BF16)
    into, at_depth = cell_tables(cells, nx, ny, nz)
    for turn in range(EARLY, SWEEPS):
        held, other = pad.at[turn % 2], pad.at[1 - turn % 2]
        fields = [held, ion] if turn == EARLY else [held]
        if turn > EARLY:
            halos = start_halos(fields, turn - EARLY, *exchange)
        finish_halos(halos, fields, turn - EARLY, x_in, y_in, inside)
        sweep(turn, held, other, resid, screen, pot_ref)
    pot = pad.at[SWEEPS % 2]
    pot[1 : nx + 1, TOP : TOP + ny, :] = pot_ref[...]
    halos = start_halos([pot], SWEEPS - EARLY, *exchange)
    finish_halos(halos, [pot], SWEEPS - EARLY, x_in, y_in, inside)

    def finish(i, carry):
        lo, hi = TOP, TOP + ny
        p, n = pot[i + 1, lo:hi, :], ion[i + 1, lo:hi, :]
        px = (pot[i, lo:hi, :], pot[i + 2, lo:hi, :])
        py = (pot[i + 1, lo - 1 : hi - 1, :], pot[i + 1, lo + 1 : hi + 1, :])
        ix = (ion[i, lo:hi, :], ion[i + 2, lo:hi, :])
        iy = (ion[i + 1, lo - 1 : hi - 1, :], ion[i + 1, lo + 1 : hi + 1, :])
        pz = z_shifts(p)[::-1]
        iz = z_shifts(n)[::-1]
        out = jnp.zeros_like(p)
        for d, (ps, ns) in enumerate(((px, ix), (py, iy), (pz, iz))):
            out = out + (face_flux(p, ps[1], n, ns[1]) - face_flux(ps[0], p, ns[0], n))
            efield[d, pl.ds(pl.multiple_of(i * ny, ny), ny), :] = -(ps[1] - ps[0]) * 0.5
        next_ref[i] = n - time_step * out
        return carry

    lax.fori_loop(0, nx, finish, 0)
    push = []
    for d in range(3):
        seen = select_rows(into, efield[d], ((0,), (0,)))
        push.append(field_scale * jnp.sum(seen * at_depth, axis=1, keepdims=True))
    for copy in sends:
        copy.wait()
    sums = own_ref[...] + select_rows(chooser, back[...])
    charge = data_ref[:, 384:512]
    for d in range(3):
        pull = data_ref[:, d * 128 : (d + 1) * 128] * sums[:, 0:128] - sums[:, (d + 1) * 128 : (d + 2) * 128]
        force_ref[:, d, :] = charge * (coulomb_scale * pull + push[d])


def features(data_ref, feat, vals, own):
    spots = [data_ref[:, d * 128 : (d + 1) * 128] for d in range(3)]
    charge = data_ref[:, 384:512]
    square = jnp.zeros_like(charge)
    for d in range(3):
        high, mid, low = split3(spots[d])
        rows = (high, high, mid, mid, high, low) if own else (high, mid, high, mid, low, high)
        for f, row in enumerate(rows):
            feat[:, 6 * d + f, :] = -2.0 * row if own else row
        square = square + spots[d] * spots[d]
    if own:
        square = square + softening
    one = jnp.ones_like(square)
    for f, row in enumerate(split3(square)):
        feat[:, (18 if own else 21) + f, :] = row
        feat[:, (21 if own else 18) + f, :] = one
    for c, val in enumerate((charge, charge * spots[0], charge * spots[1], charge * spots[2])):
        for f, row in enumerate(split3(val)):
            vals[:, 4 * f + c, :] = row
    for f in range(12, 16):
        vals[:, f, :] = jnp.zeros_like(charge)


def tile_sums(own_ids, part_ids, own_feat, own_vals, part_feat, part_vals):
    left = jnp.concatenate([own_feat[o] for o in own_ids], axis=0).astype(BF16)
    blank = jnp.zeros((24, 128), F32)
    count = len(own_ids)
    right = jnp.concatenate(
        [
            jnp.concatenate([part_feat[r] if i == j else blank for i in range(count)], axis=0).astype(BF16)
            for j, r in enumerate(part_ids)
        ],
        axis=1,
    )
    dist = dot(left, right, ((0,), (0,)))
    sums = []
    for j in range(count):
        root = lax.rsqrt(dist[:, j * 128 : (j + 1) * 128])
        u = root * root * root
        high = u.astype(BF16)
        low = (u - high.astype(F32)).astype(BF16)
        mine = own_vals[own_ids[j]].astype(BF16)
        theirs = part_vals[part_ids[j]].astype(BF16)
        on_part = dot(jnp.concatenate([mine, mine], axis=1), jnp.concatenate([high, low], axis=0))
        on_own = dot(
            jnp.concatenate([theirs, theirs], axis=1),
            jnp.concatenate([high, low], axis=1),
            ((1,), (1,)),
        )
        sums.append((on_own, on_part))
    return sums


def pair_kernel(
    local_ref,
    dir_ref,
    slot_ref,
    data_ref,
    arrived_ref,
    own_ref,
    part_ref,
    own_feat,
    own_vals,
    part_feat,
    part_vals,
    own_acc,
    part_acc,
):
    features(data_ref, own_feat, own_vals, True)
    features(arrived_ref, part_feat, part_vals, False)
    own_acc[...] = jnp.zeros_like(own_acc)
    part_acc[...] = jnp.zeros_like(part_acc)
    slots = arrived_ref.shape[0] // len(OFFSETS)
    step = PAIRS_AT_ONCE * GROUPS

    @pl.loop(0, local_ref.shape[0] // step)
    def _(turn):
        done = []
        for group in range(GROUPS):
            base = turn * step + group * PAIRS_AT_ONCE
            own_ids = [local_ref[base + j] for j in range(PAIRS_AT_ONCE)]
            part_ids = [
                dir_ref[base + j] * slots + slot_ref[base + j] for j in range(PAIRS_AT_ONCE)
            ]
            done.append(
                (own_ids, part_ids, tile_sums(own_ids, part_ids, own_feat, own_vals, part_feat, part_vals))
            )
        for own_ids, part_ids, sums in done:
            for j, (on_own, on_part) in enumerate(sums):
                own_acc[own_ids[j]] += on_own
                part_acc[part_ids[j]] += on_part

    for acc, out in ((own_acc, own_ref), (part_acc, part_ref)):
        for c in range(4):
            out[:, c * 128 : (c + 1) * 128] = acc[:, c, :] + (acc[:, 4 + c, :] + acc[:, 8 + c, :])


def shards(
    groups,
    bricks,
    positions,
    charges,
    cluster_fill,
    cluster_cell,
    send_index,
    send_count,
    pair_local,
    pair_dir,
    pair_slot,
    ion_density,
    potential_prev,
    screening,
):
    clusters = cluster_fill.shape[0]
    psize = charges.shape[0] // clusters
    dirs, slots = send_index.shape
    nx, ny, nz = ion_density.shape
    placed = positions.reshape(3, clusters, psize).transpose(1, 0, 2)
    vmem = pl.BlockSpec(memory_space=pltpu.VMEM)
    smem = pl.BlockSpec(memory_space=pltpu.SMEM)
    hbm = pl.BlockSpec(memory_space=pltpu.HBM)
    shape = lambda *dims: jax.ShapeDtypeStruct(dims, F32)
    halo = lambda turns, fields, length: pltpu.VMEM((turns, 2, fields, length, nz), F32)
    block = shape(nx, ny, nz)
    rows = shape(dirs * slots, 4 * psize)
    padded = (nx + 2, ny + 2 * TOP, nz)
    cells = cluster_cell.reshape(clusters // 128, 128)
    late = SWEEPS + 1 - EARLY
    data, arrived, update, resid, total = pl.pallas_call(
        functools.partial(send_kernel, groups, bricks),
        out_shape=(shape(clusters, 4 * psize), rows, block, block, block),
        in_specs=[smem] + [hbm] * 8,
        out_specs=[vmem] * 5,
        scratch_shapes=[
            pltpu.VMEM((clusters, 3, psize), F32),
            pltpu.VMEM((clusters, psize), F32),
            pltpu.VMEM((clusters // 128, 128), I32),
            pltpu.VMEM((clusters // 128, 128), I32),
            pltpu.VMEM((dirs, slots), I32),
            pltpu.VMEM((nx, ny, nz), F32),
            pltpu.VMEM((dirs * slots, 4 * psize), F32),
            pltpu.VMEM((dirs * slots, 4 * psize), F32),
            halo(EARLY, 1, ny),
            halo(EARLY, 1, ny),
            halo(EARLY, 1, nx),
            halo(EARLY, 1, nx),
            pltpu.VMEM((2, *padded), F32),
            pltpu.SemaphoreType.DMA((8,)),
            pltpu.SemaphoreType.DMA((dirs - 1,)),
            pltpu.SemaphoreType.DMA((dirs - 1,)),
            pltpu.SemaphoreType.DMA((EARLY, 4)),
            pltpu.SemaphoreType.DMA((EARLY, 4)),
        ],
        compiler_params=pltpu.CompilerParams(
            collective_id=0, has_side_effects=True, vmem_limit_bytes=40 << 20
        ),
        name="send",
    )(
        send_count,
        placed,
        charges.reshape(clusters, psize),
        cluster_fill.reshape(clusters // 128, 128),
        cells,
        send_index,
        ion_density,
        potential_prev,
        screening,
    )
    own_sums, part_sums = pl.pallas_call(
        pair_kernel,
        out_shape=(shape(clusters, 4 * psize), rows),
        in_specs=[smem] * 3 + [vmem] * 2,
        out_specs=[vmem] * 2,
        scratch_shapes=[
            pltpu.VMEM((clusters, 24, psize), F32),
            pltpu.VMEM((clusters, 16, psize), F32),
            pltpu.VMEM((dirs * slots, 24, psize), F32),
            pltpu.VMEM((dirs * slots, 16, psize), F32),
            pltpu.VMEM((clusters, 16, psize), F32),
            pltpu.VMEM((dirs * slots, 16, psize), F32),
        ],
        compiler_params=pltpu.CompilerParams(vmem_limit_bytes=40 << 20),
        name="pairs",
    )(pair_local, pair_dir, pair_slot, data, arrived)
    forces, potential, ion_next = pl.pallas_call(
        functools.partial(return_kernel, groups, bricks),
        out_shape=(shape(clusters, 3, psize), block, block),
        in_specs=[smem] + [hbm] * 4 + [vmem] * 6,
        out_specs=[vmem] * 3,
        scratch_shapes=[
            pltpu.VMEM((clusters // 128, 128), I32),
            pltpu.VMEM((dirs, slots), I32),
            pltpu.VMEM((nx, ny, nz), F32),
            pltpu.VMEM((dirs * slots, 4 * psize), F32),
            pltpu.VMEM((nx, ny, nz), F32),
            halo(late, 2, ny),
            halo(late, 2, ny),
            halo(late, 2, nx),
            halo(late, 2, nx),
            pltpu.VMEM((2, *padded), F32),
            pltpu.VMEM(padded, F32),
            pltpu.VMEM((3, nx * ny, nz), F32),
            pltpu.SemaphoreType.DMA((4,)),
            pltpu.SemaphoreType.DMA((dirs - 1,)),
            pltpu.SemaphoreType.DMA((dirs - 1,)),
            pltpu.SemaphoreType.DMA((late, 4)),
            pltpu.SemaphoreType.DMA((late, 4)),
        ],
        compiler_params=pltpu.CompilerParams(
            collective_id=1, has_side_effects=True, vmem_limit_bytes=40 << 20
        ),
        name="back",
    )(
        send_count,
        cells,
        send_index,
        ion_density,
        screening,
        data,
        own_sums,
        part_sums,
        update,
        resid,
        total,
    )
    return (forces.transpose(1, 0, 2).reshape(3, -1), potential, ion_next)


def solution(mesh):
    in_specs = (
        P(None, ("grp", "brick")),
        P(("grp", "brick")),
        P(("grp", "brick")),
        P(("grp", "brick")),
        P(("grp", "brick"), None),
        P(("grp", "brick"), None),
        P(("grp", "brick")),
        P(("grp", "brick")),
        P(("grp", "brick")),
        P("grp", "brick", None),
        P("grp", "brick", None),
        P("grp", "brick", None),
    )
    out_specs = (P(None, ("grp", "brick")), P("grp", "brick", None), P("grp", "brick", None))
    body = functools.partial(shards, mesh.shape["grp"], mesh.shape["brick"])
    return jax.shard_map(body, mesh=mesh, in_specs=in_specs, out_specs=out_specs, check_vma=False)
```

```python
import functools

import jax
import jax.numpy as jnp
from jax import lax
from jax.experimental import pallas as pl
from jax.experimental.pallas import tpu as pltpu
from jax.sharding import PartitionSpec as P

F32, BF16, I32 = jnp.float32, jnp.bfloat16, jnp.int32
SWEEPS = 4
EARLY = 3
coulomb_scale = 0.02
softening = 0.1
field_scale = 0.5
deposit_scale = 0.2
lowest_eig = 0.01
highest_eig = 1.99
mobility = 0.3
diffusion = 0.2
time_step = 0.2
OFFSETS = ((0, 0), (0, -1), (0, 1), (0, -2), (0, 2), (-1, 0), (1, 0))
MESH = pl.DeviceIdType.MESH
BATCH = 32
STEP = 32
ORDER = (4, 3, 2, 1)
TOP = 8


def split3(v):
    high = v.astype(BF16).astype(F32)
    rest = v - high
    mid = rest.astype(BF16).astype(F32)
    return high, mid, (rest - mid).astype(BF16).astype(F32)


def dot(a, b, dims=((1,), (0,))):
    return lax.dot_general(a, b, (dims, ((), ())), preferred_element_type=F32)


def select_rows(chooser, data, dims=((1,), (0,)), parts=3):
    pieces = split3(data)[:parts]
    total = dot(chooser, pieces[0].astype(BF16), dims)
    for piece in pieces[1:]:
        total = total + dot(chooser, piece.astype(BF16), dims)
    return total


def neighbour(step_g, step_b, groups, bricks):
    g = lax.axis_index("grp")
    b = lax.axis_index("brick")
    return (lax.rem(g + step_g + groups, groups), lax.rem(b + step_b + bricks, bricks))


def greet(groups, bricks):
    barrier = pltpu.get_barrier_semaphore()
    for step in OFFSETS[1:]:
        pl.semaphore_signal(
            barrier, inc=1, device_id=neighbour(*step, groups, bricks), device_id_type=MESH
        )
    return barrier


def slot_row(index_ref):
    return jnp.concatenate([index_ref[k : k + 1, :] for k in range(index_ref.shape[0])], axis=1)


def column(row):
    return jnp.transpose(jnp.broadcast_to(row, (128, 128)))


def columns(values):
    vals = values.astype(F32)
    return jnp.concatenate([column(vals[i : i + 1, :]) for i in range(vals.shape[0])], axis=0)


def neighbours_sum(pad, i):
    rows = pad.shape[1] - 16
    centre = pad[i + 1, TOP : TOP + rows, :]
    total = pad[i + 2, TOP : TOP + rows, :] + pad[i, TOP : TOP + rows, :]
    total = total + pad[i + 1, TOP + 1 : TOP + rows + 1, :] + pad[i + 1, TOP - 1 : TOP + rows - 1, :]
    above, below = z_shifts(centre)
    return centre, total + above + below


def z_shifts(v):
    depth = v.shape[1]
    lane = lax.broadcasted_iota(I32, v.shape, 1)
    above = jnp.where(lane == depth - 1, 0.0, pltpu.roll(v, depth - 1, 1))
    below = jnp.where(lane == 0, 0.0, pltpu.roll(v, 1, 1))
    return above, below


def face_flux(pot_low, pot_high, ion_low, ion_high):
    speed = -mobility * (pot_high - pot_low)
    return (
        jnp.maximum(speed, 0.0) * ion_low
        + jnp.minimum(speed, 0.0) * ion_high
        - diffusion * (ion_high - ion_low)
    )


def inside_flags(groups, bricks):
    g = lax.axis_index("grp")
    b = lax.axis_index("brick")
    return (
        jnp.where(g > 0, 1.0, 0.0),
        jnp.where(g < groups - 1, 1.0, 0.0),
        jnp.where(b > 0, 1.0, 0.0),
        jnp.where(b < bricks - 1, 1.0, 0.0),
    )


def start_halos(fields, turn, x_out, x_in, y_out, y_in, send, recv, groups, bricks):
    nx, ny = fields[0].shape[0] - 2, fields[0].shape[1] - 2 * TOP
    for f, field in enumerate(fields):
        y_out[turn, 0, f] = field[1 : nx + 1, TOP, :]
        y_out[turn, 1, f] = field[1 : nx + 1, TOP + ny - 1, :]
        x_out[turn, 0, f] = field[1, TOP : TOP + ny, :]
        x_out[turn, 1, f] = field[nx, TOP : TOP + ny, :]
    count = len(fields)
    copies = []
    for side in range(2):
        step = 2 * side - 1
        for axis, (out, into) in enumerate(((x_out, x_in), (y_out, y_in))):
            copy = pltpu.make_async_remote_copy(
                src_ref=out.at[turn, side, pl.ds(0, count)],
                dst_ref=into.at[turn, 1 - side, pl.ds(0, count)],
                send_sem=send.at[turn, 2 * axis + side],
                recv_sem=recv.at[turn, 2 * axis + 1 - side],
                device_id=neighbour(step * (1 - axis), step * axis, groups, bricks),
                device_id_type=MESH,
            )
            copy.start()
            copies.append(copy)
    return copies


def finish_halos(copies, fields, turn, x_in, y_in, inside):
    for copy in copies:
        copy.wait()
    nx, ny = fields[0].shape[0] - 2, fields[0].shape[1] - 2 * TOP
    for f, field in enumerate(fields):
        field[0, TOP : TOP + ny, :] = x_in[turn, 0, f] * inside[0]
        field[nx + 1, TOP : TOP + ny, :] = x_in[turn, 1, f] * inside[1]
        field[1 : nx + 1, TOP - 1, :] = y_in[turn, 0, f] * inside[2]
        field[1 : nx + 1, TOP + ny, :] = y_in[turn, 1, f] * inside[3]


def send_rows(source, target, towards, send, recv, groups, bricks):
    slots = source.shape[0] // len(OFFSETS)
    copies = []
    for k in range(1, len(OFFSETS)):
        step_g, step_b = OFFSETS[k]
        copy = pltpu.make_async_remote_copy(
            src_ref=source.at[pl.ds(k * slots, slots), :],
            dst_ref=target.at[pl.ds(k * slots, slots), :],
            send_sem=send.at[k - 1],
            recv_sem=recv.at[k - 1],
            device_id=neighbour(towards * step_g, towards * step_b, groups, bricks),
            device_id_type=MESH,
        )
        copy.start()
        copies.append(copy)
    return copies


def weights():
    middle = 0.5 * (highest_eig + lowest_eig)
    spread = 0.5 * (highest_eig - lowest_eig)
    ratio_ms = middle / spread
    now = 1.0 / ratio_ms
    table = [(0.0, 1.0 / middle)]
    for _ in range(SWEEPS - 1):
        after = 1.0 / (2.0 * ratio_ms - now)
        table.append((after * now, 2.0 * after / spread))
        now = after
    return table


def sweep(turn, held, other, resid, screen, total):
    keep, gain = weights()[turn]
    nx, ny, nz = resid.shape

    def plane(i, carry):
        centre, around = neighbours_sum(held, i)
        diag = 6.0 + screen[i]
        rest = resid[i] - (diag * centre - around)
        resid[i] = rest
        update = gain * (rest / diag)
        if turn:
            update = keep * centre + update
            total[i] = total[i] + update
        else:
            total[i] = centre + update
        other[i + 1, TOP : TOP + ny, :] = update
        return carry

    lax.fori_loop(0, nx, plane, 0, unroll=2)


def cell_tables(cell_ref, nx, ny, nz):
    cell = cell_ref[...]
    clusters = cell.shape[0] * cell.shape[1]
    row_of = cell // nz
    row_line = jnp.concatenate([row_of[i : i + 1, :] for i in range(cell.shape[0])], axis=1)
    into = jnp.where(
        lax.broadcasted_iota(I32, (nx * ny, clusters), 0) == row_line, 1.0, 0.0
    ).astype(BF16)
    k_col = columns(cell - row_of * nz)
    k_col = jnp.concatenate([k_col, k_col], axis=1)
    at_depth = jnp.where(
        lax.broadcasted_iota(I32, (clusters, nz), 1).astype(F32) == k_col, 1.0, 0.0
    )
    return into, at_depth


def send_kernel(
    groups,
    bricks,
    count_ref,
    pos_hbm,
    charge_hbm,
    fill_hbm,
    cell_hbm,
    index_hbm,
    ion_hbm,
    prev_hbm,
    screen_hbm,
    data_ref,
    arrived_ref,
    update_ref,
    resid_ref,
    total_ref,
    pos,
    charges,
    fill,
    cells,
    index,
    screen,
    out_rows,
    in_rows,
    x_out,
    x_in,
    y_out,
    y_in,
    pad,
    load,
    row_send,
    row_recv,
    halo_send,
    halo_recv,
):
    nx, ny, nz = ion_hbm.shape
    loads = [
        pltpu.make_async_copy(src, dst, load.at[i])
        for i, (src, dst) in enumerate(
            (
                (index_hbm, index),
                (fill_hbm, fill),
                (cell_hbm, cells),
                (prev_hbm, pad.at[0, pl.ds(1, nx), pl.ds(TOP, ny), :]),
                (pos_hbm, pos),
                (charge_hbm, charges),
                (ion_hbm, resid_ref),
                (screen_hbm, screen),
            )
        )
    ]
    for copy in loads:
        copy.start()
    barrier = greet(groups, bricks)
    inside = inside_flags(groups, bricks)
    for copy in loads[:4]:
        copy.wait()
    exchange = (x_out, x_in, y_out, y_in, halo_send, halo_recv, groups, bricks)
    clusters = charges.shape[0]
    slots = index.shape[1]
    wanted = slot_row(index)
    chooser = jnp.where(
        lax.broadcasted_iota(I32, (clusters, wanted.shape[1]), 0) == wanted, 1.0, 0.0
    ).astype(BF16)
    fill_col = columns(fill[...])
    lane = lax.broadcasted_iota(I32, (clusters, 128), 1).astype(F32)
    for copy in loads[4:]:
        copy.wait()
    charge = charges[...] * jnp.where(lane < fill_col, 1.0, 0.0)
    for d in range(3):
        data_ref[:, d * 128 : (d + 1) * 128] = pos[:, d, :]
    data_ref[:, 384:512] = charge
    pl.semaphore_wait(barrier, len(OFFSETS) - 1)
    halos = start_halos([pad.at[0]], 0, *exchange)
    out_rows[...] = select_rows(chooser, data_ref[...], ((0,), (0,)))
    slot_id = lax.broadcasted_iota(I32, (slots, 128), 0)
    for k in range(len(OFFSETS)):
        live = jnp.where(slot_id < count_ref[0, k], 1.0, 0.0)
        out_rows[k * slots : (k + 1) * slots, 384:512] = (
            out_rows[k * slots : (k + 1) * slots, 384:512] * live
        )
    sends = send_rows(out_rows, in_rows, -1, row_send, row_recv, groups, bricks)
    into, at_depth = cell_tables(cells, nx, ny, nz)
    deposit = select_rows(into, at_depth * jnp.sum(charge, axis=1, keepdims=True))
    resid_ref[...] = resid_ref[...] + deposit_scale * deposit.reshape(nx, ny, nz)
    for turn in range(EARLY):
        held, other = pad.at[turn % 2], pad.at[1 - turn % 2]
        if turn:
            halos = start_halos([held], turn, *exchange)
        finish_halos(halos, [held], turn, x_in, y_in, inside)
        sweep(turn, held, other, resid_ref, screen, total_ref)
    update_ref[...] = pad[EARLY % 2, 1 : nx + 1, TOP : TOP + ny, :]
    for copy in sends:
        copy.wait()
    arrived_ref[0:slots, :] = out_rows[0:slots, :]
    arrived_ref[slots:, :] = in_rows[slots:, :]


def return_kernel(
    groups,
    bricks,
    cell_hbm,
    index_hbm,
    ion_hbm,
    screen_hbm,
    data_ref,
    own_ref,
    part_ref,
    update_ref,
    resid_ref,
    total_ref,
    force_ref,
    pot_ref,
    next_ref,
    cells,
    index,
    screen,
    back,
    resid,
    x_out,
    x_in,
    y_out,
    y_in,
    pad,
    ion,
    efield,
    load,
    row_send,
    row_recv,
    halo_send,
    halo_recv,
):
    nx, ny, nz = ion_hbm.shape
    loads = [
        pltpu.make_async_copy(src, dst, load.at[i])
        for i, (src, dst) in enumerate(
            (
                (ion_hbm, ion.at[pl.ds(1, nx), pl.ds(TOP, ny), :]),
                (screen_hbm, screen),
                (index_hbm, index),
                (cell_hbm, cells),
            )
        )
    ]
    for copy in loads:
        copy.start()
    barrier = greet(groups, bricks)
    inside = inside_flags(groups, bricks)
    pad[EARLY % 2, 1 : nx + 1, TOP : TOP + ny, :] = update_ref[...]
    resid[...] = resid_ref[...]
    pot_ref[...] = total_ref[...]
    for copy in loads:
        copy.wait()
    exchange = (x_out, x_in, y_out, y_in, halo_send, halo_recv, groups, bricks)
    pl.semaphore_wait(barrier, len(OFFSETS) - 1)
    halos = start_halos([pad.at[EARLY % 2], ion], 0, *exchange)
    sends = send_rows(part_ref, back, 1, row_send, row_recv, groups, bricks)
    clusters = data_ref.shape[0]
    slots = index.shape[1]
    back[0:slots, :] = part_ref[0:slots, :]
    wanted = slot_row(index)
    chooser = jnp.where(
        lax.broadcasted_iota(I32, (clusters, wanted.shape[1]), 0) == wanted, 1.0, 0.0
    ).astype(BF16)
    into, at_depth = cell_tables(cells, nx, ny, nz)
    for turn in range(EARLY, SWEEPS):
        held, other = pad.at[turn % 2], pad.at[1 - turn % 2]
        fields = [held, ion] if turn == EARLY else [held]
        if turn > EARLY:
            halos = start_halos(fields, turn - EARLY, *exchange)
        finish_halos(halos, fields, turn - EARLY, x_in, y_in, inside)
        sweep(turn, held, other, resid, screen, pot_ref)
    pot = pad.at[SWEEPS % 2]
    pot[1 : nx + 1, TOP : TOP + ny, :] = pot_ref[...]
    halos = start_halos([pot], SWEEPS - EARLY, *exchange)
    finish_halos(halos, [pot], SWEEPS - EARLY, x_in, y_in, inside)

    def finish(i, carry):
        lo, hi = TOP, TOP + ny
        p, n = pot[i + 1, lo:hi, :], ion[i + 1, lo:hi, :]
        px = (pot[i, lo:hi, :], pot[i + 2, lo:hi, :])
        py = (pot[i + 1, lo - 1 : hi - 1, :], pot[i + 1, lo + 1 : hi + 1, :])
        ix = (ion[i, lo:hi, :], ion[i + 2, lo:hi, :])
        iy = (ion[i + 1, lo - 1 : hi - 1, :], ion[i + 1, lo + 1 : hi + 1, :])
        pz = z_shifts(p)[::-1]
        iz = z_shifts(n)[::-1]
        out = jnp.zeros_like(p)
        for d, (ps, ns) in enumerate(((px, ix), (py, iy), (pz, iz))):
            out = out + (face_flux(p, ps[1], n, ns[1]) - face_flux(ps[0], p, ns[0], n))
            efield[d, pl.ds(pl.multiple_of(i * ny, ny), ny), :] = -(ps[1] - ps[0]) * 0.5
        next_ref[i] = n - time_step * out
        return carry

    lax.fori_loop(0, nx, finish, 0)
    push = []
    for d in range(3):
        seen = select_rows(into, efield[d], ((0,), (0,)))
        push.append(field_scale * jnp.sum(seen * at_depth, axis=1, keepdims=True))
    for copy in sends:
        copy.wait()
    react = select_rows(chooser, back[...])
    charge = data_ref[:, 384:512]
    for d in range(3):
        near = slice(d * 128, (d + 1) * 128)
        pull = data_ref[:, near] * own_ref[:, 0:128] - own_ref[:, (d + 1) * 128 : (d + 2) * 128]
        force_ref[:, d, :] = charge * (coulomb_scale * pull + push[d]) + coulomb_scale * react[:, near]


def features(data, base, row_feat, lane_feat, vals):
    @pl.loop(0, data.shape[0] // 8, unroll=4)
    def _(g):
        at = pl.multiple_of(g * 8, 8)
        feature_rows(data[pl.ds(at, 8), :], base + at, row_feat, lane_feat, vals)


def feature_rows(data, base, row_feat, lane_feat, vals):
    spots = [data[:, d * 128 : (d + 1) * 128] for d in range(3)]
    charge = data[:, 384:512]
    here = pl.ds(base, 8)
    one = jnp.ones_like(charge)
    square = jnp.zeros_like(charge)
    left, right, weighed = [], [], []
    for d in range(3):
        high, mid, low = split3(spots[d])
        left += [-2.0 * part for part in (high, high, mid, mid, high, low)]
        right += [high, mid, high, mid, low, high]
        square = square + spots[d] * spots[d]
    left += list(split3(square + softening)) + [one] * 3
    right += [one] * 3 + list(split3(square))
    parts = [split3(v) for v in (charge, charge * spots[0], charge * spots[1], charge * spots[2])]
    for f in range(3):
        weighed += [part[f] for part in parts]
    weighed += [jnp.zeros_like(charge)] * 4
    for rows, table in ((left, row_feat), (right, lane_feat), (weighed, vals)):
        for k in range(0, len(rows), 8):
            table[here, k : k + 8, :] = jnp.transpose(jnp.stack(rows[k : k + 8]), (1, 0, 2))


def extent(data):
    charge = data[:, 384:512]
    lane = lax.broadcasted_iota(I32, charge.shape, 1).astype(F32) + 1.0
    return jnp.max(jnp.where(charge != 0.0, lane, 0.0), axis=1, keepdims=True)


def sort_pairs(local_ref, part_ids, own_extent, part_extent, order_vmem):
    rows = local_ref.shape[0]
    clusters, partners = own_extent.shape[0], part_extent.shape[0]
    own_lines, part_lines = [], []
    for r in range(rows):
        for lines, ids, ext in (
            (own_lines, local_ref[r : r + 1, :], own_extent),
            (part_lines, part_ids[r : r + 1, :], part_extent),
        ):
            spot = lax.broadcasted_iota(I32, (ext.shape[0], 128), 0)
            lines.append(jnp.sum(jnp.where(spot == ids, ext, 0.0), axis=0, keepdims=True))
    own_len = jnp.concatenate(own_lines, axis=0)
    part_len = jnp.concatenate(part_lines, axis=0)
    short = jnp.minimum(own_len, part_len)
    blank = clusters + partners
    own_code = blank - local_ref[...]
    part_code = partners - part_ids
    swap = part_len < own_len
    row_code = jnp.where(swap, part_code, own_code)
    lane_code = jnp.where(swap, own_code, part_code)
    fields = [
        v.astype(F32)
        for v in (row_code & 255, row_code >> 8, lane_code & 255, lane_code >> 8)
    ]
    upto = jnp.where(
        lax.broadcasted_iota(I32, (128, 128), 0) <= lax.broadcasted_iota(I32, (128, 128), 1), 1.0, 0.0
    ).astype(BF16)
    before = jnp.where(
        lax.broadcasted_iota(I32, (rows, rows), 1) < lax.broadcasted_iota(I32, (rows, rows), 0), 1.0, 0.0
    ).astype(BF16)
    place = jnp.full((rows, 128), -1.0, F32)
    base = jnp.int32(0)
    spans = []
    for blocks in ORDER:
        member = jnp.where((short > float(STEP) * (blocks - 1)) & (short <= float(STEP) * blocks), 1.0, 0.0)
        within = dot(member.astype(BF16), upto)
        total = jnp.sum(member, axis=1, keepdims=True)
        ahead = dot(before, jnp.broadcast_to(total, (rows, 128)).astype(BF16))
        place = jnp.where(member > 0.0, base.astype(F32) + ahead + within - 1.0, place)
        batches = (jnp.sum(member).astype(I32) + BATCH - 1) // BATCH
        spans.append((base, batches))
        base = base + batches * BATCH
    place = place.astype(I32)
    room = order_vmem.shape[1]
    found = jnp.zeros((4 * room, 128), F32)
    for r in range(rows):
        at = place[r : r + 1, :]
        here = jnp.where(lax.broadcasted_iota(I32, (128, 128), 0) == at & 127, 1.0, 0.0)
        ours = lax.broadcasted_iota(I32, (room, 128), 0) == at >> 7
        load = jnp.concatenate([jnp.where(ours, f[r : r + 1, :], 0.0) for f in fields], axis=0)
        found = found + dot(load.astype(BF16), here.astype(BF16), ((1,), (1,)))
    found = [found[i * room : (i + 1) * room, :] for i in range(4)]
    order_vmem[0] = blank - (found[0] + 256.0 * found[1]).astype(I32)
    order_vmem[1] = blank - (found[2] + 256.0 * found[3]).astype(I32)
    return spans


def distances(row_ids, lane_ids, rows, row_feat, lane_feat, dist):
    blank = jnp.zeros((24, 128), F32)
    for k in range(0, len(row_ids), 2):
        left = jnp.concatenate([row_feat[o] for o in row_ids[k : k + 2]], axis=0)
        left = left[:, :rows].astype(BF16)
        a, b = (lane_feat[r] for r in lane_ids[k : k + 2])
        right = jnp.concatenate(
            [
                jnp.concatenate([a, blank], axis=0).astype(BF16),
                jnp.concatenate([blank, b], axis=0).astype(BF16),
            ],
            axis=1,
        )
        dist[k // 2, 0:rows, :] = dot(left, right, ((0,), (0,)))


def tile_sums(row_ids, lane_ids, rows, dist, vals, acc):
    sums = []
    for j in range(len(row_ids)):
        root = lax.rsqrt(dist[j // 2, 0:rows, (j % 2) * 128 : (j % 2) * 128 + 128])
        u = root * root * root
        high = u.astype(BF16)
        low = (u - high.astype(F32)).astype(BF16)
        mine = vals[row_ids[j]][:, :rows].astype(BF16)
        theirs = vals[lane_ids[j]].astype(BF16)
        if rows == 128:
            on_lane = dot(jnp.concatenate([mine, mine], axis=1), jnp.concatenate([high, low], axis=0))
        else:
            on_lane = dot(mine, high) + dot(mine, low)
        on_row = dot(
            jnp.concatenate([theirs, theirs], axis=1),
            jnp.concatenate([high, low], axis=1),
            ((1,), (1,)),
        )
        sums.append((on_row, on_lane))
    for j, (on_row, on_lane) in enumerate(sums):
        acc[row_ids[j], :, 0:rows] += on_row
        acc[lane_ids[j]] += on_lane


def pair_kernel(
    local_ref,
    dir_ref,
    slot_ref,
    data_ref,
    arrived_ref,
    own_ref,
    part_ref,
    row_feat,
    lane_feat,
    vals,
    acc,
    dist,
    order_vmem,
    order,
    sem,
):
    clusters, partners = data_ref.shape[0], arrived_ref.shape[0]
    slots = partners // len(OFFSETS)
    part_ids = dir_ref[...] * slots + slot_ref[...]
    spans = sort_pairs(
        local_ref, part_ids, extent(data_ref[...]), extent(arrived_ref[...]), order_vmem
    )
    copy = pltpu.make_async_copy(order_vmem, order, sem)
    copy.start()
    features(data_ref, 0, row_feat, lane_feat, vals)
    features(arrived_ref, clusters, row_feat, lane_feat, vals)
    feature_rows(jnp.zeros((8, 512), F32), clusters + partners, row_feat, lane_feat, vals)
    acc[...] = jnp.zeros_like(acc)
    copy.wait()
    for blocks, (base, batches) in zip(ORDER, spans):
        rows = STEP * blocks

        def ids(turn, base=base):
            at = base + turn * BATCH
            line, first = at >> 7, at & 127
            return [[order[s, line, first + j] for j in range(BATCH)] for s in range(2)]

        @pl.when(batches > 0)
        def _(batches=batches, ids=ids, rows=rows):
            distances(*ids(0), rows, row_feat, lane_feat, dist)

            @pl.loop(0, batches)
            def _(turn):
                now = ids(turn)
                ahead = ids(jnp.minimum(turn + 1, batches - 1))
                tile_sums(*now, rows, dist, vals, acc)
                distances(*ahead, rows, row_feat, lane_feat, dist)

    def total(base, count, c):
        here = pl.ds(base, count)
        return acc[here, c, :] + (acc[here, 4 + c, :] + acc[here, 8 + c, :])

    for c in range(4):
        own_ref[:, c * 128 : (c + 1) * 128] = total(0, clusters, c)
    charge = arrived_ref[:, 384:512]
    whole = total(clusters, partners, 0)
    for d in range(3):
        near = slice(d * 128, (d + 1) * 128)
        part_ref[:, near] = charge * (arrived_ref[:, near] * whole - total(clusters, partners, d + 1))


def shards(
    groups,
    bricks,
    positions,
    charges,
    cluster_fill,
    cluster_cell,
    send_index,
    send_count,
    pair_local,
    pair_dir,
    pair_slot,
    ion_density,
    potential_prev,
    screening,
):
    clusters = cluster_fill.shape[0]
    psize = charges.shape[0] // clusters
    dirs, slots = send_index.shape
    nx, ny, nz = ion_density.shape
    placed = positions.reshape(3, clusters, psize).transpose(1, 0, 2)
    vmem = pl.BlockSpec(memory_space=pltpu.VMEM)
    smem = pl.BlockSpec(memory_space=pltpu.SMEM)
    hbm = pl.BlockSpec(memory_space=pltpu.HBM)
    shape = lambda *dims: jax.ShapeDtypeStruct(dims, F32)
    halo = lambda turns, fields, length: pltpu.VMEM((turns, 2, fields, length, nz), F32)
    block = shape(nx, ny, nz)
    rows = shape(dirs * slots, 4 * psize)
    padded = (nx + 2, ny + 2 * TOP, nz)
    cells = cluster_cell.reshape(clusters // 128, 128)
    late = SWEEPS + 1 - EARLY
    data, arrived, update, resid, total = pl.pallas_call(
        functools.partial(send_kernel, groups, bricks),
        out_shape=(shape(clusters, 4 * psize), rows, block, block, block),
        in_specs=[smem] + [hbm] * 8,
        out_specs=[vmem] * 5,
        scratch_shapes=[
            pltpu.VMEM((clusters, 3, psize), F32),
            pltpu.VMEM((clusters, psize), F32),
            pltpu.VMEM((clusters // 128, 128), I32),
            pltpu.VMEM((clusters // 128, 128), I32),
            pltpu.VMEM((dirs, slots), I32),
            pltpu.VMEM((nx, ny, nz), F32),
            pltpu.VMEM((dirs * slots, 4 * psize), F32),
            pltpu.VMEM((dirs * slots, 4 * psize), F32),
            halo(EARLY, 1, ny),
            halo(EARLY, 1, ny),
            halo(EARLY, 1, nx),
            halo(EARLY, 1, nx),
            pltpu.VMEM((2, *padded), F32),
            pltpu.SemaphoreType.DMA((8,)),
            pltpu.SemaphoreType.DMA((dirs - 1,)),
            pltpu.SemaphoreType.DMA((dirs - 1,)),
            pltpu.SemaphoreType.DMA((EARLY, 4)),
            pltpu.SemaphoreType.DMA((EARLY, 4)),
        ],
        compiler_params=pltpu.CompilerParams(
            collective_id=0, has_side_effects=True, vmem_limit_bytes=40 << 20
        ),
        name="send",
    )(
        send_count,
        placed,
        charges.reshape(clusters, psize),
        cluster_fill.reshape(clusters // 128, 128),
        cells,
        send_index,
        ion_density,
        potential_prev,
        screening,
    )
    pairs = pair_local.shape[0]
    table = (clusters + dirs * slots + 8,)
    room = -(-(pairs + len(ORDER) * BATCH) // 1024) * 8
    lines = lambda v: v.reshape(pairs // 128, 128)
    own_sums, part_sums = pl.pallas_call(
        pair_kernel,
        out_shape=(shape(clusters, 4 * psize), shape(dirs * slots, 3 * psize)),
        in_specs=[vmem] * 5,
        out_specs=[vmem] * 2,
        scratch_shapes=[
            pltpu.VMEM((*table, 24, psize), F32),
            pltpu.VMEM((*table, 24, psize), F32),
            pltpu.VMEM((*table, 16, psize), F32),
            pltpu.VMEM((*table, 16, psize), F32),
            pltpu.VMEM((BATCH // 2, psize, 2 * psize), F32),
            pltpu.VMEM((2, room, 128), I32),
            pltpu.SMEM((2, room, 128), I32),
            pltpu.SemaphoreType.DMA(()),
        ],
        compiler_params=pltpu.CompilerParams(vmem_limit_bytes=48 << 20),
        name="pairs",
    )(lines(pair_local), lines(pair_dir), lines(pair_slot), data, arrived)
    forces, potential, ion_next = pl.pallas_call(
        functools.partial(return_kernel, groups, bricks),
        out_shape=(shape(clusters, 3, psize), block, block),
        in_specs=[hbm] * 4 + [vmem] * 6,
        out_specs=[vmem] * 3,
        scratch_shapes=[
            pltpu.VMEM((clusters // 128, 128), I32),
            pltpu.VMEM((dirs, slots), I32),
            pltpu.VMEM((nx, ny, nz), F32),
            pltpu.VMEM((dirs * slots, 3 * psize), F32),
            pltpu.VMEM((nx, ny, nz), F32),
            halo(late, 2, ny),
            halo(late, 2, ny),
            halo(late, 2, nx),
            halo(late, 2, nx),
            pltpu.VMEM((2, *padded), F32),
            pltpu.VMEM(padded, F32),
            pltpu.VMEM((3, nx * ny, nz), F32),
            pltpu.SemaphoreType.DMA((4,)),
            pltpu.SemaphoreType.DMA((dirs - 1,)),
            pltpu.SemaphoreType.DMA((dirs - 1,)),
            pltpu.SemaphoreType.DMA((late, 4)),
            pltpu.SemaphoreType.DMA((late, 4)),
        ],
        compiler_params=pltpu.CompilerParams(
            collective_id=1, has_side_effects=True, vmem_limit_bytes=40 << 20
        ),
        name="back",
    )(
        cells,
        send_index,
        ion_density,
        screening,
        data,
        own_sums,
        part_sums,
        update,
        resid,
        total,
    )
    return (forces.transpose(1, 0, 2).reshape(3, -1), potential, ion_next)


def solution(mesh):
    in_specs = (
        P(None, ("grp", "brick")),
        P(("grp", "brick")),
        P(("grp", "brick")),
        P(("grp", "brick")),
        P(("grp", "brick"), None),
        P(("grp", "brick"), None),
        P(("grp", "brick")),
        P(("grp", "brick")),
        P(("grp", "brick")),
        P("grp", "brick", None),
        P("grp", "brick", None),
        P("grp", "brick", None),
    )
    out_specs = (P(None, ("grp", "brick")), P("grp", "brick", None), P("grp", "brick", None))
    body = functools.partial(shards, mesh.shape["grp"], mesh.shape["brick"])
    return jax.shard_map(body, mesh=mesh, in_specs=in_specs, out_specs=out_specs, check_vma=False)
```

```python
import functools

import jax
import jax.numpy as jnp
from jax import lax
from jax.experimental import pallas as pl
from jax.experimental.pallas import tpu as pltpu
from jax.sharding import PartitionSpec as P

F32, BF16, I32 = jnp.float32, jnp.bfloat16, jnp.int32
SWEEPS = 4
EARLY = 3
coulomb_scale = 0.02
softening = 0.1
field_scale = 0.5
deposit_scale = 0.2
lowest_eig = 0.01
highest_eig = 1.99
mobility = 0.3
diffusion = 0.2
time_step = 0.2
OFFSETS = ((0, 0), (0, -1), (0, 1), (0, -2), (0, 2), (-1, 0), (1, 0))
MESH = pl.DeviceIdType.MESH
BATCH = 32
STEP = 32
ORDER = (4, 3, 2, 1)
TOP = 8


def split3(v):
    high = v.astype(BF16).astype(F32)
    rest = v - high
    mid = rest.astype(BF16).astype(F32)
    return high, mid, (rest - mid).astype(BF16).astype(F32)


def dot(a, b, dims=((1,), (0,))):
    return lax.dot_general(a, b, (dims, ((), ())), preferred_element_type=F32)


def select_rows(chooser, data, dims=((1,), (0,)), parts=3):
    pieces = split3(data)[:parts]
    total = dot(chooser, pieces[0].astype(BF16), dims)
    for piece in pieces[1:]:
        total = total + dot(chooser, piece.astype(BF16), dims)
    return total


def neighbour(step_g, step_b, groups, bricks):
    g = lax.axis_index("grp")
    b = lax.axis_index("brick")
    return (lax.rem(g + step_g + groups, groups), lax.rem(b + step_b + bricks, bricks))


def greet(groups, bricks):
    barrier = pltpu.get_barrier_semaphore()
    for step in OFFSETS[1:]:
        pl.semaphore_signal(
            barrier, inc=1, device_id=neighbour(*step, groups, bricks), device_id_type=MESH
        )
    return barrier


def slot_row(index_ref):
    return jnp.concatenate([index_ref[k : k + 1, :] for k in range(index_ref.shape[0])], axis=1)


def column(row):
    return jnp.transpose(jnp.broadcast_to(row, (128, 128)))


def columns(values):
    vals = values.astype(F32)
    return jnp.concatenate([column(vals[i : i + 1, :]) for i in range(vals.shape[0])], axis=0)


def neighbours_sum(pad, i):
    rows = pad.shape[1] - 16
    centre = pad[i + 1, TOP : TOP + rows, :]
    total = pad[i + 2, TOP : TOP + rows, :] + pad[i, TOP : TOP + rows, :]
    total = total + pad[i + 1, TOP + 1 : TOP + rows + 1, :] + pad[i + 1, TOP - 1 : TOP + rows - 1, :]
    above, below = z_shifts(centre)
    return centre, total + above + below


def z_shifts(v):
    depth = v.shape[1]
    lane = lax.broadcasted_iota(I32, v.shape, 1)
    above = jnp.where(lane == depth - 1, 0.0, pltpu.roll(v, depth - 1, 1))
    below = jnp.where(lane == 0, 0.0, pltpu.roll(v, 1, 1))
    return above, below


def face_flux(pot_low, pot_high, ion_low, ion_high):
    speed = -mobility * (pot_high - pot_low)
    return (
        jnp.maximum(speed, 0.0) * ion_low
        + jnp.minimum(speed, 0.0) * ion_high
        - diffusion * (ion_high - ion_low)
    )


def inside_flags(groups, bricks):
    g = lax.axis_index("grp")
    b = lax.axis_index("brick")
    return (
        jnp.where(g > 0, 1.0, 0.0),
        jnp.where(g < groups - 1, 1.0, 0.0),
        jnp.where(b > 0, 1.0, 0.0),
        jnp.where(b < bricks - 1, 1.0, 0.0),
    )


def start_halos(axis, fields, turn, x_out, x_in, y_out, y_in, send, recv, groups, bricks):
    nx, ny = fields[0].shape[0] - 2, fields[0].shape[1] - 2 * TOP
    out, into = (y_out, y_in) if axis else (x_out, x_in)
    for f, field in enumerate(fields):
        if axis:
            out[turn, 0, f] = field[1 : nx + 1, TOP, :]
            out[turn, 1, f] = field[1 : nx + 1, TOP + ny - 1, :]
        else:
            out[turn, 0, f] = field[1, TOP : TOP + ny, :]
            out[turn, 1, f] = field[nx, TOP : TOP + ny, :]
    copies = []
    for side in range(2):
        step = 2 * side - 1
        copy = pltpu.make_async_remote_copy(
            src_ref=out.at[turn, side, pl.ds(0, len(fields))],
            dst_ref=into.at[turn, 1 - side, pl.ds(0, len(fields))],
            send_sem=send.at[turn, 2 * axis + side],
            recv_sem=recv.at[turn, 2 * axis + 1 - side],
            device_id=neighbour(step * (1 - axis), step * axis, groups, bricks),
            device_id_type=MESH,
        )
        copy.start()
        copies.append(copy)
    return copies


def finish_halos(copies, fields, turn, x_in, y_in, inside):
    for copy in copies:
        copy.wait()
    nx, ny = fields[0].shape[0] - 2, fields[0].shape[1] - 2 * TOP
    for f, field in enumerate(fields):
        field[0, TOP : TOP + ny, :] = x_in[turn, 0, f] * inside[0]
        field[nx + 1, TOP : TOP + ny, :] = x_in[turn, 1, f] * inside[1]
        field[1 : nx + 1, TOP - 1, :] = y_in[turn, 0, f] * inside[2]
        field[1 : nx + 1, TOP + ny, :] = y_in[turn, 1, f] * inside[3]


def send_rows(source, target, towards, send, recv, groups, bricks):
    slots = source.shape[0] // len(OFFSETS)
    copies = []
    for k in range(1, len(OFFSETS)):
        step_g, step_b = OFFSETS[k]
        copy = pltpu.make_async_remote_copy(
            src_ref=source.at[pl.ds(k * slots, slots), :],
            dst_ref=target.at[pl.ds(k * slots, slots), :],
            send_sem=send.at[k - 1],
            recv_sem=recv.at[k - 1],
            device_id=neighbour(towards * step_g, towards * step_b, groups, bricks),
            device_id_type=MESH,
        )
        copy.start()
        copies.append(copy)
    return copies


def weights():
    middle = 0.5 * (highest_eig + lowest_eig)
    spread = 0.5 * (highest_eig - lowest_eig)
    ratio_ms = middle / spread
    now = 1.0 / ratio_ms
    table = [(0.0, 1.0 / middle)]
    for _ in range(SWEEPS - 1):
        after = 1.0 / (2.0 * ratio_ms - now)
        table.append((after * now, 2.0 * after / spread))
        now = after
    return table


def sweep(turn, held, other, resid, screen, total, between, whole=False):
    keep, gain = weights()[turn]
    nx, ny, nz = resid.shape

    def plane(i, carry):
        centre, around = neighbours_sum(held, i)
        diag = 6.0 + screen[i]
        rest = resid[i] - (diag * centre - around)
        resid[i] = rest
        update = gain * (rest / diag)
        if turn:
            update = keep * centre + update
            done = total[i] + update
        else:
            done = centre + update
        total[i] = done
        other[i + 1, TOP : TOP + ny, :] = done if whole else update
        return carry

    plane(0, 0)
    plane(nx - 1, 0)
    result = between()
    lax.fori_loop(1, nx - 1, plane, 0, unroll=2)
    return result


def cell_tables(cell_ref, nx, ny, nz):
    cell = cell_ref[...]
    clusters = cell.shape[0] * cell.shape[1]
    row_of = cell // nz
    row_line = jnp.concatenate([row_of[i : i + 1, :] for i in range(cell.shape[0])], axis=1)
    into = jnp.where(
        lax.broadcasted_iota(I32, (nx * ny, clusters), 0) == row_line, 1.0, 0.0
    ).astype(BF16)
    k_col = columns(cell - row_of * nz)
    k_col = jnp.concatenate([k_col, k_col], axis=1)
    at_depth = jnp.where(
        lax.broadcasted_iota(I32, (clusters, nz), 1).astype(F32) == k_col, 1.0, 0.0
    )
    return into, at_depth


def send_kernel(
    groups,
    bricks,
    count_ref,
    pos_hbm,
    charge_hbm,
    fill_hbm,
    cell_hbm,
    index_hbm,
    local_hbm,
    dir_hbm,
    slot_hbm,
    ion_hbm,
    prev_hbm,
    screen_hbm,
    data_ref,
    arrived_ref,
    update_ref,
    resid_ref,
    total_ref,
    into_ref,
    depth_ref,
    order_ref,
    pos,
    charges,
    fill,
    cells,
    index,
    pair_local,
    pair_dir,
    pair_slot,
    screen,
    out_rows,
    in_rows,
    x_out,
    x_in,
    y_out,
    y_in,
    pad,
    load,
    row_send,
    row_recv,
    halo_send,
    halo_recv,
):
    nx, ny, nz = ion_hbm.shape
    loads = [
        pltpu.make_async_copy(src, dst, load.at[i])
        for i, (src, dst) in enumerate(
            (
                (index_hbm, index),
                (fill_hbm, fill),
                (cell_hbm, cells),
                (prev_hbm, pad.at[0, pl.ds(1, nx), pl.ds(TOP, ny), :]),
                (pos_hbm, pos),
                (charge_hbm, charges),
                (ion_hbm, resid_ref),
                (screen_hbm, screen),
                (local_hbm, pair_local),
                (dir_hbm, pair_dir),
                (slot_hbm, pair_slot),
            )
        )
    ]
    for copy in loads:
        copy.start()
    barrier = greet(groups, bricks)
    inside = inside_flags(groups, bricks)
    for copy in loads[:4]:
        copy.wait()
    exchange = (x_out, x_in, y_out, y_in, halo_send, halo_recv, groups, bricks)
    clusters = charges.shape[0]
    slots = index.shape[1]
    wanted = slot_row(index)
    chooser = jnp.where(
        lax.broadcasted_iota(I32, (clusters, wanted.shape[1]), 0) == wanted, 1.0, 0.0
    ).astype(BF16)
    fill_col = columns(fill[...])
    lane = lax.broadcasted_iota(I32, (clusters, 128), 1).astype(F32)
    for copy in loads[4:]:
        copy.wait()
    charge = charges[...] * jnp.where(lane < fill_col, 1.0, 0.0)
    for d in range(3):
        data_ref[:, d * 128 : (d + 1) * 128] = pos[:, d, :]
    data_ref[:, 384:512] = charge
    pl.semaphore_wait(barrier, len(OFFSETS) - 1)
    halos = start_halos(0, [pad.at[0]], 0, *exchange) + start_halos(1, [pad.at[0]], 0, *exchange)
    out_rows[...] = select_rows(chooser, data_ref[...], ((0,), (0,)))
    slot_id = lax.broadcasted_iota(I32, (slots, 128), 0)
    for k in range(len(OFFSETS)):
        live = jnp.where(slot_id < count_ref[0, k], 1.0, 0.0)
        out_rows[k * slots : (k + 1) * slots, 384:512] = (
            out_rows[k * slots : (k + 1) * slots, 384:512] * live
        )
    sends = send_rows(out_rows, in_rows, -1, row_send, row_recv, groups, bricks)
    into, at_depth = cell_tables(cells, nx, ny, nz)
    into_ref[...] = into
    depth_ref[...] = at_depth
    deposit = select_rows(into, at_depth * jnp.sum(charge, axis=1, keepdims=True))
    resid_ref[...] = resid_ref[...] + deposit_scale * deposit.reshape(nx, ny, nz)
    for turn in range(EARLY):
        held, other = pad.at[turn % 2], pad.at[1 - turn % 2]
        if turn == EARLY - 1:
            for copy in sends:
                copy.wait()
            arrived_ref[0:slots, :] = out_rows[0:slots, :]
            arrived_ref[slots:, :] = in_rows[slots:, :]
            sort_pairs(
                pair_local,
                pair_dir[...] * slots + pair_slot[...],
                extent(data_ref),
                extent(arrived_ref),
                order_ref,
            )
        finish_halos(halos, [held], turn, x_in, y_in, inside)
        if turn + 1 < EARLY:
            halos = sweep(
                turn,
                held,
                other,
                resid_ref,
                screen,
                total_ref,
                lambda turn=turn, other=other: start_halos(0, [other], turn + 1, *exchange),
            )
            halos = halos + start_halos(1, [other], turn + 1, *exchange)
        else:
            sweep(turn, held, other, resid_ref, screen, total_ref, lambda: None)
    update_ref[...] = pad[EARLY % 2, 1 : nx + 1, TOP : TOP + ny, :]


def back_kernel(
    groups,
    bricks,
    ion_hbm,
    screen_hbm,
    part_ref,
    update_ref,
    resid_ref,
    total_ref,
    back_ref,
    pot_ref,
    ion_ref,
    screen,
    back,
    resid,
    total,
    x_out,
    x_in,
    y_out,
    y_in,
    pad,
    load,
    row_send,
    row_recv,
    halo_send,
    halo_recv,
):
    nx, ny, nz = ion_hbm.shape
    loads = [
        pltpu.make_async_copy(
            ion_hbm, ion_ref.at[pl.ds(1, nx), pl.ds(TOP, ny), :], load.at[0]
        ),
        pltpu.make_async_copy(screen_hbm, screen, load.at[1]),
    ]
    for copy in loads:
        copy.start()
    barrier = greet(groups, bricks)
    inside = inside_flags(groups, bricks)
    first = pad.at[EARLY % 2]
    first[1 : nx + 1, TOP : TOP + ny, :] = update_ref[...]
    for copy in loads:
        copy.wait()
    exchange = (x_out, x_in, y_out, y_in, halo_send, halo_recv, groups, bricks)
    pl.semaphore_wait(barrier, len(OFFSETS) - 1)
    halos = start_halos(0, [first, ion_ref], 0, *exchange)
    halos = halos + start_halos(1, [first, ion_ref], 0, *exchange)
    sends = send_rows(part_ref, back, 1, row_send, row_recv, groups, bricks)
    resid[...] = resid_ref[...]
    total[...] = total_ref[...]
    slots = part_ref.shape[0] // len(OFFSETS)
    back_ref[0:slots, :] = part_ref[0:slots, :]
    for turn in range(EARLY, SWEEPS):
        held, other = pad.at[turn % 2], pad.at[1 - turn % 2]
        fields = [held, ion_ref] if turn == EARLY else [held]
        last = turn == SWEEPS - 1
        other = pot_ref if last else other
        finish_halos(halos, fields, turn - EARLY, x_in, y_in, inside)
        halos = sweep(
            turn,
            held,
            other,
            resid,
            screen,
            total,
            lambda turn=turn, other=other: start_halos(0, [other], turn + 1 - EARLY, *exchange),
            last,
        )
        halos = halos + start_halos(1, [other], turn + 1 - EARLY, *exchange)
    for copy in sends:
        copy.wait()
    back_ref[slots:, :] = back[slots:, :]
    finish_halos(halos, [pot_ref], SWEEPS - EARLY, x_in, y_in, inside)


def final_kernel(
    index_hbm,
    data_ref,
    own_ref,
    back_ref,
    pot,
    ion,
    into_ref,
    depth_ref,
    force_hbm,
    pot_hbm,
    next_hbm,
    force,
    after,
    efield,
    index,
    store,
):
    nx, ny, nz = pot_hbm.shape
    out = [
        pltpu.make_async_copy(pot.at[pl.ds(1, nx), pl.ds(TOP, ny), :], pot_hbm, store.at[0]),
        pltpu.make_async_copy(after, next_hbm, store.at[1]),
        pltpu.make_async_copy(force, force_hbm, store.at[2]),
    ]
    fetch = pltpu.make_async_copy(index_hbm, index, store.at[3])
    fetch.start()
    out[0].start()

    def finish(i, carry):
        lo, hi = TOP, TOP + ny
        p, n = pot[i + 1, lo:hi, :], ion[i + 1, lo:hi, :]
        px = (pot[i, lo:hi, :], pot[i + 2, lo:hi, :])
        py = (pot[i + 1, lo - 1 : hi - 1, :], pot[i + 1, lo + 1 : hi + 1, :])
        ix = (ion[i, lo:hi, :], ion[i + 2, lo:hi, :])
        iy = (ion[i + 1, lo - 1 : hi - 1, :], ion[i + 1, lo + 1 : hi + 1, :])
        pz = z_shifts(p)[::-1]
        iz = z_shifts(n)[::-1]
        change = jnp.zeros_like(p)
        for d, (ps, ns) in enumerate(((px, ix), (py, iy), (pz, iz))):
            change = change + (face_flux(p, ps[1], n, ns[1]) - face_flux(ps[0], p, ns[0], n))
            efield[d, pl.ds(pl.multiple_of(i * ny, ny), ny), :] = -(ps[1] - ps[0]) * 0.5
        after[i] = n - time_step * change
        return carry

    lax.fori_loop(0, nx, finish, 0)
    out[1].start()
    fetch.wait()
    wanted = slot_row(index)
    clusters = data_ref.shape[0]
    chooser = jnp.where(
        lax.broadcasted_iota(I32, (clusters, wanted.shape[1]), 0) == wanted, 1.0, 0.0
    ).astype(BF16)
    react = select_rows(chooser, back_ref[...])
    charge = data_ref[:, 384:512]
    for d in range(3):
        seen = select_rows(into_ref[...], efield[d], ((0,), (0,)))
        push = field_scale * jnp.sum(seen * depth_ref[...], axis=1, keepdims=True)
        near = slice(d * 128, (d + 1) * 128)
        pull = data_ref[:, near] * own_ref[:, 0:128] - own_ref[:, (d + 1) * 128 : (d + 2) * 128]
        force[:, d, :] = charge * (coulomb_scale * pull + push) + coulomb_scale * react[:, near]
    out[2].start()
    for copy in out:
        copy.wait()


def features(data, base, row_feat, lane_feat, vals):
    @pl.loop(0, data.shape[0] // 8, unroll=4)
    def _(g):
        at = pl.multiple_of(g * 8, 8)
        feature_rows(data[pl.ds(at, 8), :], base + at, row_feat, lane_feat, vals)


def feature_rows(data, base, row_feat, lane_feat, vals):
    spots = [data[:, d * 128 : (d + 1) * 128] for d in range(3)]
    charge = data[:, 384:512]
    here = pl.ds(base, 8)
    one = jnp.ones_like(charge)
    square = jnp.zeros_like(charge)
    left, right, weighed = [], [], []
    for d in range(3):
        high, mid, low = split3(spots[d])
        left += [-2.0 * part for part in (high, high, mid, mid, high, low)]
        right += [high, mid, high, mid, low, high]
        square = square + spots[d] * spots[d]
    left += list(split3(square + softening)) + [one] * 3
    right += [one] * 3 + list(split3(square))
    parts = [split3(v) for v in (charge, charge * spots[0], charge * spots[1], charge * spots[2])]
    for f in range(3):
        weighed += [part[f] for part in parts]
    weighed += [jnp.zeros_like(charge)] * 4
    for rows, table in ((left, row_feat), (right, lane_feat), (weighed, vals)):
        for k in range(0, len(rows), 8):
            table[here, k : k + 8, :] = jnp.transpose(jnp.stack(rows[k : k + 8]), (1, 0, 2))


def extent(data):
    charge = data[:, 384:512]
    lane = lax.broadcasted_iota(I32, charge.shape, 1).astype(F32) + 1.0
    return jnp.max(jnp.where(charge != 0.0, lane, 0.0), axis=1, keepdims=True)


def sort_pairs(local_ref, part_ids, own_extent, part_extent, order_ref):
    rows = local_ref.shape[0]
    clusters, partners = own_extent.shape[0], part_extent.shape[0]
    own_lines, part_lines = [], []
    for r in range(rows):
        for lines, ids, ext in (
            (own_lines, local_ref[r : r + 1, :], own_extent),
            (part_lines, part_ids[r : r + 1, :], part_extent),
        ):
            spot = lax.broadcasted_iota(I32, (ext.shape[0], 128), 0)
            lines.append(jnp.sum(jnp.where(spot == ids, ext, 0.0), axis=0, keepdims=True))
    own_len = jnp.concatenate(own_lines, axis=0)
    part_len = jnp.concatenate(part_lines, axis=0)
    short = jnp.minimum(own_len, part_len)
    blank = clusters + partners
    own_code = blank - local_ref[...]
    part_code = partners - part_ids
    swap = part_len < own_len
    row_code = jnp.where(swap, part_code, own_code)
    lane_code = jnp.where(swap, own_code, part_code)
    fields = [
        v.astype(F32)
        for v in (row_code & 255, row_code >> 8, lane_code & 255, lane_code >> 8)
    ]
    upto = jnp.where(
        lax.broadcasted_iota(I32, (128, 128), 0) <= lax.broadcasted_iota(I32, (128, 128), 1), 1.0, 0.0
    ).astype(BF16)
    before = jnp.where(
        lax.broadcasted_iota(I32, (rows, rows), 1) < lax.broadcasted_iota(I32, (rows, rows), 0), 1.0, 0.0
    ).astype(BF16)
    place = jnp.full((rows, 128), -1.0, F32)
    base = jnp.zeros((1, 1), F32)
    lane = lax.broadcasted_iota(I32, (1, 128), 1)
    spans = jnp.zeros((1, 128), F32)
    for blocks in ORDER:
        member = jnp.where((short > float(STEP) * (blocks - 1)) & (short <= float(STEP) * blocks), 1.0, 0.0)
        within = dot(member.astype(BF16), upto)
        total = jnp.sum(member, axis=1, keepdims=True)
        ahead = dot(before, jnp.broadcast_to(total, (rows, 128)).astype(BF16))
        place = jnp.where(member > 0.0, base + ahead + within - 1.0, place)
        batches = jnp.floor((jnp.sum(total, axis=0, keepdims=True) + (BATCH - 1.0)) / BATCH)
        spans = jnp.where(lane == len(ORDER) - blocks, batches, spans)
        base = base + batches * BATCH
    place = place.astype(I32)
    room = order_ref.shape[1] - 1
    found = jnp.zeros((4 * room, 128), F32)
    for r in range(rows):
        at = place[r : r + 1, :]
        here = jnp.where(lax.broadcasted_iota(I32, (128, 128), 0) == at & 127, 1.0, 0.0)
        ours = lax.broadcasted_iota(I32, (room, 128), 0) == at >> 7
        load = jnp.concatenate([jnp.where(ours, f[r : r + 1, :], 0.0) for f in fields], axis=0)
        found = found + dot(load.astype(BF16), here.astype(BF16), ((1,), (1,)))
    found = [found[i * room : (i + 1) * room, :] for i in range(4)]
    order_ref[0, 0:room, :] = blank - (found[0] + 256.0 * found[1]).astype(I32)
    order_ref[1, 0:room, :] = blank - (found[2] + 256.0 * found[3]).astype(I32)
    order_ref[0, room : room + 1, :] = spans.astype(I32)
    order_ref[1, room : room + 1, :] = spans.astype(I32)


def distances(row_ids, lane_ids, rows, row_feat, lane_feat, dist):
    blank = jnp.zeros((24, 128), F32)
    for k in range(0, len(row_ids), 2):
        left = jnp.concatenate([row_feat[o] for o in row_ids[k : k + 2]], axis=0)
        left = left[:, :rows].astype(BF16)
        a, b = (lane_feat[r] for r in lane_ids[k : k + 2])
        right = jnp.concatenate(
            [
                jnp.concatenate([a, blank], axis=0).astype(BF16),
                jnp.concatenate([blank, b], axis=0).astype(BF16),
            ],
            axis=1,
        )
        dist[k // 2, 0:rows, :] = dot(left, right, ((0,), (0,)))


def tile_sums(row_ids, lane_ids, rows, dist, vals, acc):
    sums = []
    for j in range(len(row_ids)):
        root = lax.rsqrt(dist[j // 2, 0:rows, (j % 2) * 128 : (j % 2) * 128 + 128])
        u = root * root * root
        high = u.astype(BF16)
        low = (u - high.astype(F32)).astype(BF16)
        mine = vals[row_ids[j]][:, :rows].astype(BF16)
        theirs = vals[lane_ids[j]].astype(BF16)
        if rows == 128:
            on_lane = dot(jnp.concatenate([mine, mine], axis=1), jnp.concatenate([high, low], axis=0))
        else:
            on_lane = dot(mine, high) + dot(mine, low)
        on_row = dot(
            jnp.concatenate([theirs, theirs], axis=1),
            jnp.concatenate([high, low], axis=1),
            ((1,), (1,)),
        )
        sums.append((on_row, on_lane))
    for j, (on_row, on_lane) in enumerate(sums):
        acc[row_ids[j], :, 0:rows] += on_row
        acc[lane_ids[j]] += on_lane


def pair_kernel(
    order,
    data_ref,
    arrived_ref,
    own_ref,
    part_ref,
    row_feat,
    lane_feat,
    vals,
    acc,
    dist,
):
    clusters, partners = data_ref.shape[0], arrived_ref.shape[0]
    features(data_ref, 0, row_feat, lane_feat, vals)
    features(arrived_ref, clusters, row_feat, lane_feat, vals)
    feature_rows(jnp.zeros((8, 512), F32), clusters + partners, row_feat, lane_feat, vals)
    acc[...] = jnp.zeros_like(acc)
    room = order.shape[1] - 1
    spans = []
    base = 0
    for at in range(len(ORDER)):
        batches = order[0, room, at]
        spans.append((base, batches))
        base = base + batches * BATCH
    for blocks, (base, batches) in zip(ORDER, spans):
        rows = STEP * blocks

        def ids(turn, base=base):
            at = base + turn * BATCH
            line, first = at >> 7, at & 127
            return [[order[s, line, first + j] for j in range(BATCH)] for s in range(2)]

        @pl.when(batches > 0)
        def _(batches=batches, ids=ids, rows=rows):
            distances(*ids(0), rows, row_feat, lane_feat, dist)

            @pl.loop(0, batches)
            def _(turn):
                now = ids(turn)
                ahead = ids(jnp.minimum(turn + 1, batches - 1))
                tile_sums(*now, rows, dist, vals, acc)
                distances(*ahead, rows, row_feat, lane_feat, dist)

    def total(base, count, c):
        here = pl.ds(base, count)
        return acc[here, c, :] + (acc[here, 4 + c, :] + acc[here, 8 + c, :])

    for c in range(4):
        own_ref[:, c * 128 : (c + 1) * 128] = total(0, clusters, c)
    charge = arrived_ref[:, 384:512]
    whole = total(clusters, partners, 0)
    for d in range(3):
        near = slice(d * 128, (d + 1) * 128)
        part_ref[:, near] = charge * (arrived_ref[:, near] * whole - total(clusters, partners, d + 1))


def shards(
    groups,
    bricks,
    positions,
    charges,
    cluster_fill,
    cluster_cell,
    send_index,
    send_count,
    pair_local,
    pair_dir,
    pair_slot,
    ion_density,
    potential_prev,
    screening,
):
    clusters = cluster_fill.shape[0]
    psize = charges.shape[0] // clusters
    dirs, slots = send_index.shape
    nx, ny, nz = ion_density.shape
    placed = positions.reshape(3, clusters, psize).transpose(1, 0, 2)
    vmem = pl.BlockSpec(memory_space=pltpu.VMEM)
    smem = pl.BlockSpec(memory_space=pltpu.SMEM)
    hbm = pl.BlockSpec(memory_space=pltpu.HBM)
    shape = lambda *dims: jax.ShapeDtypeStruct(dims, F32)
    halo = lambda turns, fields, length: pltpu.VMEM((turns, 2, fields, length, nz), F32)
    block = shape(nx, ny, nz)
    rows = shape(dirs * slots, 4 * psize)
    padded = (nx + 2, ny + 2 * TOP, nz)
    cells = cluster_cell.reshape(clusters // 128, 128)
    late = SWEEPS + 1 - EARLY
    pairs = pair_local.shape[0]
    lines = lambda v: v.reshape(pairs // 128, 128)
    room = -(-(pairs + len(ORDER) * BATCH) // 1024) * 8
    still = lambda v: pltpu.with_memory_space_constraint(v, pltpu.HBM)
    ion_density, potential_prev, screening = map(still, (ion_density, potential_prev, screening))
    data, arrived, update, resid, total, into, at_depth, order = pl.pallas_call(
        functools.partial(send_kernel, groups, bricks),
        out_shape=(
            shape(clusters, 4 * psize),
            rows,
            block,
            block,
            block,
            jax.ShapeDtypeStruct((nx * ny, clusters), BF16),
            shape(clusters, nz),
            jax.ShapeDtypeStruct((2, room + 1, 128), I32),
        ),
        in_specs=[smem] + [hbm] * 11,
        out_specs=[vmem] * 8,
        scratch_shapes=[
            pltpu.VMEM((clusters, 3, psize), F32),
            pltpu.VMEM((clusters, psize), F32),
            pltpu.VMEM((clusters // 128, 128), I32),
            pltpu.VMEM((clusters // 128, 128), I32),
            pltpu.VMEM((dirs, slots), I32),
            pltpu.VMEM((pairs // 128, 128), I32),
            pltpu.VMEM((pairs // 128, 128), I32),
            pltpu.VMEM((pairs // 128, 128), I32),
            pltpu.VMEM((nx, ny, nz), F32),
            pltpu.VMEM((dirs * slots, 4 * psize), F32),
            pltpu.VMEM((dirs * slots, 4 * psize), F32),
            halo(EARLY, 1, ny),
            halo(EARLY, 1, ny),
            halo(EARLY, 1, nx),
            halo(EARLY, 1, nx),
            pltpu.VMEM((2, *padded), F32),
            pltpu.SemaphoreType.DMA((11,)),
            pltpu.SemaphoreType.DMA((dirs - 1,)),
            pltpu.SemaphoreType.DMA((dirs - 1,)),
            pltpu.SemaphoreType.DMA((EARLY, 4)),
            pltpu.SemaphoreType.DMA((EARLY, 4)),
        ],
        compiler_params=pltpu.CompilerParams(
            collective_id=0, has_side_effects=True, vmem_limit_bytes=40 << 20
        ),
        name="send",
    )(
        still(send_count),
        still(placed),
        still(charges.reshape(clusters, psize)),
        still(cluster_fill.reshape(clusters // 128, 128)),
        still(cells),
        still(send_index),
        still(lines(pair_local)),
        still(lines(pair_dir)),
        still(lines(pair_slot)),
        ion_density,
        potential_prev,
        screening,
    )
    table = (clusters + dirs * slots + 8,)
    own_sums, part_sums = pl.pallas_call(
        pair_kernel,
        out_shape=(shape(clusters, 4 * psize), shape(dirs * slots, 3 * psize)),
        in_specs=[smem] + [vmem] * 2,
        out_specs=[vmem] * 2,
        scratch_shapes=[
            pltpu.VMEM((*table, 24, psize), F32),
            pltpu.VMEM((*table, 24, psize), F32),
            pltpu.VMEM((*table, 16, psize), F32),
            pltpu.VMEM((*table, 16, psize), F32),
            pltpu.VMEM((BATCH // 2, psize, 2 * psize), F32),
        ],
        compiler_params=pltpu.CompilerParams(vmem_limit_bytes=40 << 20),
        name="pairs",
    )(order, data, arrived)
    padding = shape(*padded)
    back, pot, ion = pl.pallas_call(
        functools.partial(back_kernel, groups, bricks),
        out_shape=(shape(dirs * slots, 3 * psize), padding, padding),
        in_specs=[hbm] * 2 + [vmem] * 4,
        out_specs=[vmem] * 3,
        scratch_shapes=[
            pltpu.VMEM((nx, ny, nz), F32),
            pltpu.VMEM((dirs * slots, 3 * psize), F32),
            pltpu.VMEM((nx, ny, nz), F32),
            pltpu.VMEM((nx, ny, nz), F32),
            halo(late, 2, ny),
            halo(late, 2, ny),
            halo(late, 2, nx),
            halo(late, 2, nx),
            pltpu.VMEM((2, *padded), F32),
            pltpu.SemaphoreType.DMA((2,)),
            pltpu.SemaphoreType.DMA((dirs - 1,)),
            pltpu.SemaphoreType.DMA((dirs - 1,)),
            pltpu.SemaphoreType.DMA((late, 4)),
            pltpu.SemaphoreType.DMA((late, 4)),
        ],
        compiler_params=pltpu.CompilerParams(
            collective_id=1, has_side_effects=True, vmem_limit_bytes=40 << 20
        ),
        name="back",
    )(ion_density, screening, part_sums, update, resid, total)
    forces, potential, ion_next = pl.pallas_call(
        final_kernel,
        out_shape=(shape(clusters, 3, psize), block, block),
        in_specs=[hbm] + [vmem] * 7,
        out_specs=[hbm] * 3,
        scratch_shapes=[
            pltpu.VMEM((clusters, 3, psize), F32),
            pltpu.VMEM((nx, ny, nz), F32),
            pltpu.VMEM((3, nx * ny, nz), F32),
            pltpu.VMEM((dirs, slots), I32),
            pltpu.SemaphoreType.DMA((4,)),
        ],
        compiler_params=pltpu.CompilerParams(vmem_limit_bytes=40 << 20),
        name="final",
    )(still(send_index), data, own_sums, back, pot, ion, into, at_depth)
    return (forces.transpose(1, 0, 2).reshape(3, -1), potential, ion_next)


def solution(mesh):
    in_specs = (
        P(None, ("grp", "brick")),
        P(("grp", "brick")),
        P(("grp", "brick")),
        P(("grp", "brick")),
        P(("grp", "brick"), None),
        P(("grp", "brick"), None),
        P(("grp", "brick")),
        P(("grp", "brick")),
        P(("grp", "brick")),
        P("grp", "brick", None),
        P("grp", "brick", None),
        P("grp", "brick", None),
    )
    out_specs = (P(None, ("grp", "brick")), P("grp", "brick", None), P("grp", "brick", None))
    body = functools.partial(shards, mesh.shape["grp"], mesh.shape["brick"])
    return jax.shard_map(body, mesh=mesh, in_specs=in_specs, out_specs=out_specs, check_vma=False)
```

```python
import functools

import jax
import jax.numpy as jnp
from jax import lax
from jax.experimental import pallas as pl
from jax.experimental.pallas import tpu as pltpu
from jax.sharding import PartitionSpec as P

F32, BF16, I32 = jnp.float32, jnp.bfloat16, jnp.int32
SWEEPS = 4
EARLY = 3
coulomb_scale = 0.02
softening = 0.1
field_scale = 0.5
deposit_scale = 0.2
lowest_eig = 0.01
highest_eig = 1.99
mobility = 0.3
diffusion = 0.2
time_step = 0.2
OFFSETS = ((0, 0), (0, -1), (0, 1), (0, -2), (0, 2), (-1, 0), (1, 0))
MESH = pl.DeviceIdType.MESH
BATCH = 32
STEP = 32
ORDER = (4, 3, 2, 1)
TOP = 8


def split3(v):
    high = v.astype(BF16).astype(F32)
    rest = v - high
    mid = rest.astype(BF16).astype(F32)
    return high, mid, (rest - mid).astype(BF16).astype(F32)


def dot(a, b, dims=((1,), (0,))):
    return lax.dot_general(a, b, (dims, ((), ())), preferred_element_type=F32)


def select_rows(chooser, data, dims=((1,), (0,)), parts=3):
    pieces = split3(data)[:parts]
    total = dot(chooser, pieces[0].astype(BF16), dims)
    for piece in pieces[1:]:
        total = total + dot(chooser, piece.astype(BF16), dims)
    return total


def neighbour(step_g, step_b, groups, bricks):
    g = lax.axis_index("grp")
    b = lax.axis_index("brick")
    return (lax.rem(g + step_g + groups, groups), lax.rem(b + step_b + bricks, bricks))


def greet(groups, bricks):
    barrier = pltpu.get_barrier_semaphore()
    for step in OFFSETS[1:]:
        pl.semaphore_signal(
            barrier, inc=1, device_id=neighbour(*step, groups, bricks), device_id_type=MESH
        )
    return barrier


def slot_row(index_ref):
    return jnp.concatenate([index_ref[k : k + 1, :] for k in range(index_ref.shape[0])], axis=1)


def column(row):
    return jnp.transpose(jnp.broadcast_to(row, (128, 128)))


def columns(values):
    vals = values.astype(F32)
    return jnp.concatenate([column(vals[i : i + 1, :]) for i in range(vals.shape[0])], axis=0)


def neighbours_sum(pad, i):
    rows = pad.shape[1] - 16
    centre = pad[i + 1, TOP : TOP + rows, :]
    total = pad[i + 2, TOP : TOP + rows, :] + pad[i, TOP : TOP + rows, :]
    total = total + pad[i + 1, TOP + 1 : TOP + rows + 1, :] + pad[i + 1, TOP - 1 : TOP + rows - 1, :]
    above, below = z_shifts(centre)
    return centre, total + above + below


def z_shifts(v):
    depth = v.shape[1]
    lane = lax.broadcasted_iota(I32, v.shape, 1)
    above = jnp.where(lane == depth - 1, 0.0, pltpu.roll(v, depth - 1, 1))
    below = jnp.where(lane == 0, 0.0, pltpu.roll(v, 1, 1))
    return above, below


def face_flux(pot_low, pot_high, ion_low, ion_high):
    speed = -mobility * (pot_high - pot_low)
    return (
        jnp.maximum(speed, 0.0) * ion_low
        + jnp.minimum(speed, 0.0) * ion_high
        - diffusion * (ion_high - ion_low)
    )


def inside_flags(groups, bricks):
    g = lax.axis_index("grp")
    b = lax.axis_index("brick")
    return (
        jnp.where(g > 0, 1.0, 0.0),
        jnp.where(g < groups - 1, 1.0, 0.0),
        jnp.where(b > 0, 1.0, 0.0),
        jnp.where(b < bricks - 1, 1.0, 0.0),
    )


def start_halos(axis, fields, turn, x_out, x_in, y_out, y_in, send, recv, groups, bricks):
    nx, ny = fields[0].shape[0] - 2, fields[0].shape[1] - 2 * TOP
    out, into = (y_out, y_in) if axis else (x_out, x_in)
    for f, field in enumerate(fields):
        if axis:
            out[turn, 0, f] = field[1 : nx + 1, TOP, :]
            out[turn, 1, f] = field[1 : nx + 1, TOP + ny - 1, :]
        else:
            out[turn, 0, f] = field[1, TOP : TOP + ny, :]
            out[turn, 1, f] = field[nx, TOP : TOP + ny, :]
    copies = []
    for side in range(2):
        step = 2 * side - 1
        copy = pltpu.make_async_remote_copy(
            src_ref=out.at[turn, side, pl.ds(0, len(fields))],
            dst_ref=into.at[turn, 1 - side, pl.ds(0, len(fields))],
            send_sem=send.at[turn, 2 * axis + side],
            recv_sem=recv.at[turn, 2 * axis + 1 - side],
            device_id=neighbour(step * (1 - axis), step * axis, groups, bricks),
            device_id_type=MESH,
        )
        copy.start()
        copies.append(copy)
    return copies


def place_halos(field, at, x_in, y_in, inside):
    nx, ny = field.shape[0] - 2, field.shape[1] - 2 * TOP
    field[0, TOP : TOP + ny, :] = x_in[at[0], 0, at[1]] * inside[0]
    field[nx + 1, TOP : TOP + ny, :] = x_in[at[0], 1, at[1]] * inside[1]
    field[1 : nx + 1, TOP - 1, :] = y_in[at[0], 0, at[1]] * inside[2]
    field[1 : nx + 1, TOP + ny, :] = y_in[at[0], 1, at[1]] * inside[3]


def clear_halos(field):
    nx, ny = field.shape[0] - 2, field.shape[1] - 2 * TOP
    edge = jnp.zeros(field.shape[1:], F32)
    field[0] = edge
    field[nx + 1] = edge
    for i in range(1, nx + 1):
        field[i, 0:TOP, :] = edge[:TOP]
        field[i, TOP + ny :, :] = edge[:TOP]


def send_rows(source, target, towards, send, recv, groups, bricks):
    slots = source.shape[0] // len(OFFSETS)
    copies = []
    for k in range(1, len(OFFSETS)):
        step_g, step_b = OFFSETS[k]
        copy = pltpu.make_async_remote_copy(
            src_ref=source.at[pl.ds(k * slots, slots), :],
            dst_ref=target.at[pl.ds(k * slots, slots), :],
            send_sem=send.at[k - 1],
            recv_sem=recv.at[k - 1],
            device_id=neighbour(towards * step_g, towards * step_b, groups, bricks),
            device_id_type=MESH,
        )
        copy.start()
        copies.append(copy)
    return copies


def weights():
    middle = 0.5 * (highest_eig + lowest_eig)
    spread = 0.5 * (highest_eig - lowest_eig)
    ratio_ms = middle / spread
    now = 1.0 / ratio_ms
    table = [(0.0, 1.0 / middle)]
    for _ in range(SWEEPS - 1):
        after = 1.0 / (2.0 * ratio_ms - now)
        table.append((after * now, 2.0 * after / spread))
        now = after
    return table


def sweep(turn, held, other, resid, screen, total, whole=False):
    keep, gain = weights()[turn]
    nx, ny, nz = resid.shape

    def plane(i, carry):
        centre, around = neighbours_sum(held, i)
        diag = 6.0 + screen[i]
        rest = resid[i] - (diag * centre - around)
        resid[i] = rest
        update = gain * (rest / diag)
        if turn:
            update = keep * centre + update
            done = total[i] + update
        else:
            done = centre + update
        total[i] = done
        other[i + 1, TOP : TOP + ny, :] = done if whole else update
        return carry

    lax.fori_loop(0, nx, plane, 0, unroll=2)


def add_halos(turn, at, other, resid, screen, total, x_in, y_in, inside):
    gain = weights()[turn][1]
    nx, ny, nz = resid.shape
    for side in range(2):
        i = side * (nx - 1)
        halo = x_in[at, side, 0] * inside[side]
        step = gain * (halo / (6.0 + screen[i]))
        resid[i] = resid[i] + halo
        total[i] = total[i] + step
        other[i + 1, TOP : TOP + ny, :] = other[i + 1, TOP : TOP + ny, :] + step
    for side in range(2):
        j = side * (ny - 1)
        halo = y_in[at, side, 0] * inside[2 + side]
        step = gain * (halo / (6.0 + screen[:, j, :]))
        resid[:, j, :] = resid[:, j, :] + halo
        total[:, j, :] = total[:, j, :] + step
        other[1 : nx + 1, TOP + j, :] = other[1 : nx + 1, TOP + j, :] + step


def cell_tables(cell_ref, nx, ny, nz):
    cell = cell_ref[...]
    clusters = cell.shape[0] * cell.shape[1]
    row_of = cell // nz
    row_line = jnp.concatenate([row_of[i : i + 1, :] for i in range(cell.shape[0])], axis=1)
    into = jnp.where(
        lax.broadcasted_iota(I32, (nx * ny, clusters), 0) == row_line, 1.0, 0.0
    ).astype(BF16)
    k_col = columns(cell - row_of * nz)
    k_col = jnp.concatenate([k_col, k_col], axis=1)
    at_depth = jnp.where(
        lax.broadcasted_iota(I32, (clusters, nz), 1).astype(F32) == k_col, 1.0, 0.0
    )
    return into, at_depth


def send_kernel(
    groups,
    bricks,
    count_ref,
    pos_hbm,
    charge_hbm,
    fill_hbm,
    cell_hbm,
    index_hbm,
    local_hbm,
    dir_hbm,
    slot_hbm,
    ion_hbm,
    prev_hbm,
    screen_hbm,
    data_ref,
    arrived_ref,
    update_ref,
    resid_ref,
    total_ref,
    into_ref,
    depth_ref,
    order_ref,
    row_feat,
    lane_feat,
    vals,
    pos,
    charges,
    fill,
    cells,
    index,
    pair_local,
    pair_dir,
    pair_slot,
    screen,
    out_rows,
    in_rows,
    x_out,
    x_in,
    y_out,
    y_in,
    pad,
    load,
    row_send,
    row_recv,
    halo_send,
    halo_recv,
):
    nx, ny, nz = ion_hbm.shape
    loads = [
        pltpu.make_async_copy(src, dst, load.at[i])
        for i, (src, dst) in enumerate(
            (
                (index_hbm, index),
                (fill_hbm, fill),
                (cell_hbm, cells),
                (prev_hbm, pad.at[0, pl.ds(1, nx), pl.ds(TOP, ny), :]),
                (pos_hbm, pos),
                (charge_hbm, charges),
                (ion_hbm, resid_ref),
                (screen_hbm, screen),
                (local_hbm, pair_local),
                (dir_hbm, pair_dir),
                (slot_hbm, pair_slot),
            )
        )
    ]
    for copy in loads:
        copy.start()
    barrier = greet(groups, bricks)
    inside = inside_flags(groups, bricks)
    clear_halos(pad.at[0])
    clear_halos(pad.at[1])
    for copy in loads[:4]:
        copy.wait()
    exchange = (x_out, x_in, y_out, y_in, halo_send, halo_recv, groups, bricks)
    clusters = charges.shape[0]
    slots = index.shape[1]
    wanted = slot_row(index)
    chooser = jnp.where(
        lax.broadcasted_iota(I32, (clusters, wanted.shape[1]), 0) == wanted, 1.0, 0.0
    ).astype(BF16)
    fill_col = columns(fill[...])
    lane = lax.broadcasted_iota(I32, (clusters, 128), 1).astype(F32)
    for copy in loads[4:]:
        copy.wait()
    charge = charges[...] * jnp.where(lane < fill_col, 1.0, 0.0)
    for d in range(3):
        data_ref[:, d * 128 : (d + 1) * 128] = pos[:, d, :]
    data_ref[:, 384:512] = charge
    pl.semaphore_wait(barrier, len(OFFSETS) - 1)
    halos = start_halos(0, [pad.at[0]], 0, *exchange) + start_halos(1, [pad.at[0]], 0, *exchange)
    out_rows[...] = select_rows(chooser, data_ref[...], ((0,), (0,)))
    slot_id = lax.broadcasted_iota(I32, (slots, 128), 0)
    for k in range(len(OFFSETS)):
        live = jnp.where(slot_id < count_ref[0, k], 1.0, 0.0)
        out_rows[k * slots : (k + 1) * slots, 384:512] = (
            out_rows[k * slots : (k + 1) * slots, 384:512] * live
        )
    sends = send_rows(out_rows, in_rows, -1, row_send, row_recv, groups, bricks)
    into, at_depth = cell_tables(cells, nx, ny, nz)
    into_ref[...] = into
    depth_ref[...] = at_depth
    deposit = select_rows(into, at_depth * jnp.sum(charge, axis=1, keepdims=True))
    resid_ref[...] = resid_ref[...] + deposit_scale * deposit.reshape(nx, ny, nz)
    for turn in range(EARLY):
        held, other = pad.at[turn % 2], pad.at[1 - turn % 2]
        if turn == EARLY - 2:
            features(data_ref, 0, row_feat, lane_feat, vals)
        if turn == EARLY - 1:
            for copy in sends:
                copy.wait()
            arrived_ref[0:slots, :] = out_rows[0:slots, :]
            arrived_ref[slots:, :] = in_rows[slots:, :]
            sort_pairs(
                pair_local,
                pair_dir[...] * slots + pair_slot[...],
                extent(data_ref),
                extent(arrived_ref),
                order_ref,
            )
            partners = arrived_ref.shape[0]
            features(arrived_ref, clusters, row_feat, lane_feat, vals)
            feature_rows(jnp.zeros((8, 512), F32), clusters + partners, row_feat, lane_feat, vals)
        sweep(turn, held, other, resid_ref, screen, total_ref)
        for copy in halos:
            copy.wait()
        add_halos(turn, turn, other, resid_ref, screen, total_ref, x_in, y_in, inside)
        if turn + 1 < EARLY:
            halos = start_halos(0, [other], turn + 1, *exchange)
            halos = halos + start_halos(1, [other], turn + 1, *exchange)
    update_ref[...] = pad[EARLY % 2, 1 : nx + 1, TOP : TOP + ny, :]


def back_kernel(
    groups,
    bricks,
    index_hbm,
    ion_hbm,
    screen_hbm,
    data_ref,
    own_ref,
    part_ref,
    update_ref,
    resid_ref,
    total_ref,
    pull_ref,
    pot_ref,
    ion_ref,
    index,
    screen,
    back,
    resid,
    total,
    x_out,
    x_in,
    y_out,
    y_in,
    pad,
    load,
    row_send,
    row_recv,
    halo_send,
    halo_recv,
):
    nx, ny, nz = ion_hbm.shape
    loads = [
        pltpu.make_async_copy(
            ion_hbm, ion_ref.at[pl.ds(1, nx), pl.ds(TOP, ny), :], load.at[0]
        ),
        pltpu.make_async_copy(screen_hbm, screen, load.at[1]),
        pltpu.make_async_copy(index_hbm, index, load.at[2]),
    ]
    for copy in loads:
        copy.start()
    barrier = greet(groups, bricks)
    inside = inside_flags(groups, bricks)
    first = pad.at[EARLY % 2]
    clear_halos(pad.at[0])
    clear_halos(pad.at[1])
    first[1 : nx + 1, TOP : TOP + ny, :] = update_ref[...]
    for copy in loads:
        copy.wait()
    exchange = (x_out, x_in, y_out, y_in, halo_send, halo_recv, groups, bricks)
    pl.semaphore_wait(barrier, len(OFFSETS) - 1)
    halos = start_halos(0, [first, ion_ref], 0, *exchange)
    halos = halos + start_halos(1, [first, ion_ref], 0, *exchange)
    sends = send_rows(part_ref, back, 1, row_send, row_recv, groups, bricks)
    resid[...] = resid_ref[...]
    total[...] = total_ref[...]
    slots = part_ref.shape[0] // len(OFFSETS)
    back[0:slots, :] = part_ref[0:slots, :]
    wanted = slot_row(index)
    clusters = data_ref.shape[0]
    chooser = jnp.where(
        lax.broadcasted_iota(I32, (clusters, wanted.shape[1]), 0) == wanted, 1.0, 0.0
    ).astype(BF16)
    for d in range(3):
        near = slice(d * 128, (d + 1) * 128)
        pull = data_ref[:, near] * own_ref[:, 0:128] - own_ref[:, (d + 1) * 128 : (d + 2) * 128]
        pull_ref[:, near] = coulomb_scale * data_ref[:, 384:512] * pull
    for turn in range(EARLY, SWEEPS):
        held, other = pad.at[turn % 2], pad.at[1 - turn % 2]
        last = turn == SWEEPS - 1
        other = pot_ref if last else other
        sweep(turn, held, other, resid, screen, total, last)
        for copy in halos:
            copy.wait()
        add_halos(turn, turn - EARLY, other, resid, screen, total, x_in, y_in, inside)
        halos = start_halos(0, [other], turn + 1 - EARLY, *exchange)
        halos = halos + start_halos(1, [other], turn + 1 - EARLY, *exchange)
        if turn == EARLY:
            place_halos(ion_ref, (0, 1), x_in, y_in, inside)
    for copy in sends:
        copy.wait()
    pull_ref[...] = pull_ref[...] + coulomb_scale * select_rows(chooser, back[...])
    for copy in halos:
        copy.wait()
    place_halos(pot_ref, (SWEEPS - EARLY, 0), x_in, y_in, inside)


def final_kernel(
    data_ref,
    pull_ref,
    pot,
    ion,
    into_ref,
    depth_ref,
    force_hbm,
    pot_hbm,
    next_hbm,
    force,
    after,
    efield,
    store,
):
    nx, ny, nz = pot_hbm.shape
    out = [
        pltpu.make_async_copy(pot.at[pl.ds(1, nx), pl.ds(TOP, ny), :], pot_hbm, store.at[0]),
        pltpu.make_async_copy(after, next_hbm, store.at[1]),
        pltpu.make_async_copy(force, force_hbm, store.at[2]),
    ]
    out[0].start()

    def finish(i, carry):
        lo, hi = TOP, TOP + ny
        p, n = pot[i + 1, lo:hi, :], ion[i + 1, lo:hi, :]
        px = (pot[i, lo:hi, :], pot[i + 2, lo:hi, :])
        py = (pot[i + 1, lo - 1 : hi - 1, :], pot[i + 1, lo + 1 : hi + 1, :])
        ix = (ion[i, lo:hi, :], ion[i + 2, lo:hi, :])
        iy = (ion[i + 1, lo - 1 : hi - 1, :], ion[i + 1, lo + 1 : hi + 1, :])
        pz = z_shifts(p)[::-1]
        iz = z_shifts(n)[::-1]
        change = jnp.zeros_like(p)
        for d, (ps, ns) in enumerate(((px, ix), (py, iy), (pz, iz))):
            change = change + (face_flux(p, ps[1], n, ns[1]) - face_flux(ps[0], p, ns[0], n))
            efield[d, pl.ds(pl.multiple_of(i * ny, ny), ny), :] = -(ps[1] - ps[0]) * 0.5
        after[i] = n - time_step * change
        return carry

    lax.fori_loop(0, nx, finish, 0)
    out[1].start()
    charge = field_scale * data_ref[:, 384:512]
    for d in range(3):
        seen = select_rows(into_ref[...], efield[d], ((0,), (0,)), 2)
        push = jnp.sum(seen * depth_ref[...], axis=1, keepdims=True)
        force[:, d, :] = charge * push + pull_ref[:, d * 128 : (d + 1) * 128]
    out[2].start()
    for copy in out:
        copy.wait()


def features(data, base, row_feat, lane_feat, vals):
    @pl.loop(0, data.shape[0] // 8, unroll=4)
    def _(g):
        at = pl.multiple_of(g * 8, 8)
        feature_rows(data[pl.ds(at, 8), :], base + at, row_feat, lane_feat, vals)


def feature_rows(data, base, row_feat, lane_feat, vals):
    spots = [data[:, d * 128 : (d + 1) * 128] for d in range(3)]
    charge = data[:, 384:512]
    here = pl.ds(base, 8)
    one = jnp.ones_like(charge)
    square = jnp.zeros_like(charge)
    left, right, weighed = [], [], []
    for d in range(3):
        high, mid, low = split3(spots[d])
        left += [-2.0 * part for part in (high, high, mid, mid, high, low)]
        right += [high, mid, high, mid, low, high]
        square = square + spots[d] * spots[d]
    left += list(split3(square + softening)) + [one] * 3
    right += [one] * 3 + list(split3(square))
    parts = [split3(v) for v in (charge, charge * spots[0], charge * spots[1], charge * spots[2])]
    for f in range(3):
        weighed += [part[f] for part in parts]
    weighed += [jnp.zeros_like(charge)] * 4
    for rows, table in ((left, row_feat), (right, lane_feat), (weighed, vals)):
        for k in range(0, len(rows), 8):
            table[here, k : k + 8, :] = jnp.transpose(jnp.stack(rows[k : k + 8]), (1, 0, 2))


def extent(data):
    charge = data[:, 384:512]
    lane = lax.broadcasted_iota(I32, charge.shape, 1).astype(F32) + 1.0
    return jnp.max(jnp.where(charge != 0.0, lane, 0.0), axis=1, keepdims=True)


def sort_pairs(local_ref, part_ids, own_extent, part_extent, order_ref):
    rows = local_ref.shape[0]
    clusters, partners = own_extent.shape[0], part_extent.shape[0]
    own_lines, part_lines = [], []
    for r in range(rows):
        for lines, ids, ext in (
            (own_lines, local_ref[r : r + 1, :], own_extent),
            (part_lines, part_ids[r : r + 1, :], part_extent),
        ):
            spot = lax.broadcasted_iota(I32, (ext.shape[0], 128), 0)
            lines.append(jnp.sum(jnp.where(spot == ids, ext, 0.0), axis=0, keepdims=True))
    own_len = jnp.concatenate(own_lines, axis=0)
    part_len = jnp.concatenate(part_lines, axis=0)
    short = jnp.minimum(own_len, part_len)
    blank = clusters + partners
    own_code = blank - local_ref[...]
    part_code = partners - part_ids
    swap = part_len < own_len
    row_code = jnp.where(swap, part_code, own_code)
    lane_code = jnp.where(swap, own_code, part_code)
    fields = [
        v.astype(F32)
        for v in (row_code & 255, row_code >> 8, lane_code & 255, lane_code >> 8)
    ]
    upto = jnp.where(
        lax.broadcasted_iota(I32, (128, 128), 0) <= lax.broadcasted_iota(I32, (128, 128), 1), 1.0, 0.0
    ).astype(BF16)
    before = jnp.where(
        lax.broadcasted_iota(I32, (rows, rows), 1) < lax.broadcasted_iota(I32, (rows, rows), 0), 1.0, 0.0
    ).astype(BF16)
    place = jnp.full((rows, 128), -1.0, F32)
    base = jnp.zeros((1, 1), F32)
    lane = lax.broadcasted_iota(I32, (1, 128), 1)
    spans = jnp.zeros((1, 128), F32)
    for blocks in ORDER:
        member = jnp.where((short > float(STEP) * (blocks - 1)) & (short <= float(STEP) * blocks), 1.0, 0.0)
        within = dot(member.astype(BF16), upto)
        total = jnp.sum(member, axis=1, keepdims=True)
        ahead = dot(before, jnp.broadcast_to(total, (rows, 128)).astype(BF16))
        place = jnp.where(member > 0.0, base + ahead + within - 1.0, place)
        batches = jnp.floor((jnp.sum(total, axis=0, keepdims=True) + (BATCH - 1.0)) / BATCH)
        spans = jnp.where(lane == len(ORDER) - blocks, batches, spans)
        base = base + batches * BATCH
    place = place.astype(I32)
    room = order_ref.shape[1] - 1
    found = jnp.zeros((4 * room, 128), F32)
    for r in range(rows):
        at = place[r : r + 1, :]
        here = jnp.where(lax.broadcasted_iota(I32, (128, 128), 0) == at & 127, 1.0, 0.0)
        ours = lax.broadcasted_iota(I32, (room, 128), 0) == at >> 7
        load = jnp.concatenate([jnp.where(ours, f[r : r + 1, :], 0.0) for f in fields], axis=0)
        found = found + dot(load.astype(BF16), here.astype(BF16), ((1,), (1,)))
    found = [found[i * room : (i + 1) * room, :] for i in range(4)]
    order_ref[0, 0:room, :] = blank - (found[0] + 256.0 * found[1]).astype(I32)
    order_ref[1, 0:room, :] = blank - (found[2] + 256.0 * found[3]).astype(I32)
    order_ref[0, room : room + 1, :] = spans.astype(I32)
    order_ref[1, room : room + 1, :] = spans.astype(I32)


def distances(row_ids, lane_ids, rows, row_feat, lane_feat, dist):
    blank = jnp.zeros((24, 128), F32)
    for k in range(0, len(row_ids), 2):
        left = jnp.concatenate([row_feat[o] for o in row_ids[k : k + 2]], axis=0)
        left = left[:, :rows].astype(BF16)
        a, b = (lane_feat[r] for r in lane_ids[k : k + 2])
        right = jnp.concatenate(
            [
                jnp.concatenate([a, blank], axis=0).astype(BF16),
                jnp.concatenate([blank, b], axis=0).astype(BF16),
            ],
            axis=1,
        )
        dist[k // 2, 0:rows, :] = dot(left, right, ((0,), (0,)))


def tile_sums(row_ids, lane_ids, rows, dist, vals, acc):
    sums = []
    for j in range(len(row_ids)):
        root = lax.rsqrt(dist[j // 2, 0:rows, (j % 2) * 128 : (j % 2) * 128 + 128])
        u = root * root * root
        high = u.astype(BF16)
        low = (u - high.astype(F32)).astype(BF16)
        mine = vals[row_ids[j]][:, :rows].astype(BF16)
        theirs = vals[lane_ids[j]].astype(BF16)
        if rows == 128:
            on_lane = dot(jnp.concatenate([mine, mine], axis=1), jnp.concatenate([high, low], axis=0))
        else:
            on_lane = dot(mine, high) + dot(mine, low)
        on_row = dot(
            jnp.concatenate([theirs, theirs], axis=1),
            jnp.concatenate([high, low], axis=1),
            ((1,), (1,)),
        )
        sums.append((on_row, on_lane))
    for j, (on_row, on_lane) in enumerate(sums):
        acc[row_ids[j], :, 0:rows] += on_row
        acc[lane_ids[j]] += on_lane


def pair_kernel(
    order,
    arrived_ref,
    row_feat,
    lane_feat,
    vals,
    own_ref,
    part_ref,
    acc,
    dist,
):
    clusters, partners = own_ref.shape[0], arrived_ref.shape[0]
    acc[...] = jnp.zeros_like(acc)
    room = order.shape[1] - 1
    spans = []
    base = 0
    for at in range(len(ORDER)):
        batches = order[0, room, at]
        spans.append((base, batches))
        base = base + batches * BATCH
    for blocks, (base, batches) in zip(ORDER, spans):
        rows = STEP * blocks

        def ids(turn, base=base):
            at = base + turn * BATCH
            line, first = at >> 7, at & 127
            return [[order[s, line, first + j] for j in range(BATCH)] for s in range(2)]

        @pl.when(batches > 0)
        def _(batches=batches, ids=ids, rows=rows):
            distances(*ids(0), rows, row_feat, lane_feat, dist)

            @pl.loop(0, batches)
            def _(turn):
                now = ids(turn)
                ahead = ids(jnp.minimum(turn + 1, batches - 1))
                tile_sums(*now, rows, dist, vals, acc)
                distances(*ahead, rows, row_feat, lane_feat, dist)

    def total(base, count, c):
        here = pl.ds(base, count)
        return acc[here, c, :] + (acc[here, 4 + c, :] + acc[here, 8 + c, :])

    for c in range(4):
        own_ref[:, c * 128 : (c + 1) * 128] = total(0, clusters, c)
    charge = arrived_ref[:, 384:512]
    whole = total(clusters, partners, 0)
    for d in range(3):
        near = slice(d * 128, (d + 1) * 128)
        part_ref[:, near] = charge * (arrived_ref[:, near] * whole - total(clusters, partners, d + 1))


def shards(
    groups,
    bricks,
    positions,
    charges,
    cluster_fill,
    cluster_cell,
    send_index,
    send_count,
    pair_local,
    pair_dir,
    pair_slot,
    ion_density,
    potential_prev,
    screening,
):
    clusters = cluster_fill.shape[0]
    psize = charges.shape[0] // clusters
    dirs, slots = send_index.shape
    nx, ny, nz = ion_density.shape
    placed = positions.reshape(3, clusters, psize).transpose(1, 0, 2)
    vmem = pl.BlockSpec(memory_space=pltpu.VMEM)
    smem = pl.BlockSpec(memory_space=pltpu.SMEM)
    hbm = pl.BlockSpec(memory_space=pltpu.HBM)
    shape = lambda *dims: jax.ShapeDtypeStruct(dims, F32)
    halo = lambda turns, fields, length: pltpu.VMEM((turns, 2, fields, length, nz), F32)
    block = shape(nx, ny, nz)
    rows = shape(dirs * slots, 4 * psize)
    padded = (nx + 2, ny + 2 * TOP, nz)
    cells = cluster_cell.reshape(clusters // 128, 128)
    late = SWEEPS + 1 - EARLY
    table = (clusters + dirs * slots + 8,)
    pairs = pair_local.shape[0]
    lines = lambda v: v.reshape(pairs // 128, 128)
    room = -(-(pairs + len(ORDER) * BATCH) // 1024) * 8
    still = lambda v: pltpu.with_memory_space_constraint(v, pltpu.HBM)
    ion_density, potential_prev, screening = map(still, (ion_density, potential_prev, screening))
    data, arrived, update, resid, total, into, at_depth, order, *tables = pl.pallas_call(
        functools.partial(send_kernel, groups, bricks),
        out_shape=(
            shape(clusters, 4 * psize),
            rows,
            block,
            block,
            block,
            jax.ShapeDtypeStruct((nx * ny, clusters), BF16),
            shape(clusters, nz),
            jax.ShapeDtypeStruct((2, room + 1, 128), I32),
            shape(*table, 24, psize),
            shape(*table, 24, psize),
            shape(*table, 16, psize),
        ),
        in_specs=[smem] + [hbm] * 11,
        out_specs=[vmem] * 11,
        scratch_shapes=[
            pltpu.VMEM((clusters, 3, psize), F32),
            pltpu.VMEM((clusters, psize), F32),
            pltpu.VMEM((clusters // 128, 128), I32),
            pltpu.VMEM((clusters // 128, 128), I32),
            pltpu.VMEM((dirs, slots), I32),
            pltpu.VMEM((pairs // 128, 128), I32),
            pltpu.VMEM((pairs // 128, 128), I32),
            pltpu.VMEM((pairs // 128, 128), I32),
            pltpu.VMEM((nx, ny, nz), F32),
            pltpu.VMEM((dirs * slots, 4 * psize), F32),
            pltpu.VMEM((dirs * slots, 4 * psize), F32),
            halo(EARLY, 1, ny),
            halo(EARLY, 1, ny),
            halo(EARLY, 1, nx),
            halo(EARLY, 1, nx),
            pltpu.VMEM((2, *padded), F32),
            pltpu.SemaphoreType.DMA((11,)),
            pltpu.SemaphoreType.DMA((dirs - 1,)),
            pltpu.SemaphoreType.DMA((dirs - 1,)),
            pltpu.SemaphoreType.DMA((EARLY, 4)),
            pltpu.SemaphoreType.DMA((EARLY, 4)),
        ],
        compiler_params=pltpu.CompilerParams(
            collective_id=0, has_side_effects=True, vmem_limit_bytes=32 << 20
        ),
        name="send",
    )(
        still(send_count),
        still(placed),
        still(charges.reshape(clusters, psize)),
        still(cluster_fill.reshape(clusters // 128, 128)),
        still(cells),
        still(send_index),
        still(lines(pair_local)),
        still(lines(pair_dir)),
        still(lines(pair_slot)),
        ion_density,
        potential_prev,
        screening,
    )
    own_sums, part_sums = pl.pallas_call(
        pair_kernel,
        out_shape=(shape(clusters, 4 * psize), shape(dirs * slots, 3 * psize)),
        in_specs=[smem] + [vmem] * 4,
        out_specs=[vmem] * 2,
        scratch_shapes=[
            pltpu.VMEM((*table, 16, psize), F32),
            pltpu.VMEM((BATCH // 2, psize, 2 * psize), F32),
        ],
        compiler_params=pltpu.CompilerParams(vmem_limit_bytes=28 << 20),
        name="pairs",
    )(order, arrived, *tables)
    padding = shape(*padded)
    pull, pot, ion = pl.pallas_call(
        functools.partial(back_kernel, groups, bricks),
        out_shape=(shape(clusters, 3 * psize), padding, padding),
        in_specs=[hbm] * 3 + [vmem] * 6,
        out_specs=[vmem] * 3,
        scratch_shapes=[
            pltpu.VMEM((dirs, slots), I32),
            pltpu.VMEM((nx, ny, nz), F32),
            pltpu.VMEM((dirs * slots, 3 * psize), F32),
            pltpu.VMEM((nx, ny, nz), F32),
            pltpu.VMEM((nx, ny, nz), F32),
            halo(late, 2, ny),
            halo(late, 2, ny),
            halo(late, 2, nx),
            halo(late, 2, nx),
            pltpu.VMEM((2, *padded), F32),
            pltpu.SemaphoreType.DMA((3,)),
            pltpu.SemaphoreType.DMA((dirs - 1,)),
            pltpu.SemaphoreType.DMA((dirs - 1,)),
            pltpu.SemaphoreType.DMA((late, 4)),
            pltpu.SemaphoreType.DMA((late, 4)),
        ],
        compiler_params=pltpu.CompilerParams(
            collective_id=1, has_side_effects=True, vmem_limit_bytes=28 << 20
        ),
        name="back",
    )(still(send_index), ion_density, screening, data, own_sums, part_sums, update, resid, total)
    forces, potential, ion_next = pl.pallas_call(
        final_kernel,
        out_shape=(shape(clusters, 3, psize), block, block),
        in_specs=[vmem] * 6,
        out_specs=[hbm] * 3,
        scratch_shapes=[
            pltpu.VMEM((clusters, 3, psize), F32),
            pltpu.VMEM((nx, ny, nz), F32),
            pltpu.VMEM((3, nx * ny, nz), F32),
            pltpu.SemaphoreType.DMA((3,)),
        ],
        compiler_params=pltpu.CompilerParams(vmem_limit_bytes=28 << 20),
        name="final",
    )(data, pull, pot, ion, into, at_depth)
    return (forces.transpose(1, 0, 2).reshape(3, -1), potential, ion_next)


def solution(mesh):
    in_specs = (
        P(None, ("grp", "brick")),
        P(("grp", "brick")),
        P(("grp", "brick")),
        P(("grp", "brick")),
        P(("grp", "brick"), None),
        P(("grp", "brick"), None),
        P(("grp", "brick")),
        P(("grp", "brick")),
        P(("grp", "brick")),
        P("grp", "brick", None),
        P("grp", "brick", None),
        P("grp", "brick", None),
    )
    out_specs = (P(None, ("grp", "brick")), P("grp", "brick", None), P("grp", "brick", None))
    body = functools.partial(shards, mesh.shape["grp"], mesh.shape["brick"])
    return jax.shard_map(body, mesh=mesh, in_specs=in_specs, out_specs=out_specs, check_vma=False)
```

```python
import functools

import jax
import jax.numpy as jnp
from jax import lax
from jax.experimental import pallas as pl
from jax.experimental.pallas import tpu as pltpu
from jax.sharding import PartitionSpec as P

F32, BF16, I32 = jnp.float32, jnp.bfloat16, jnp.int32
SWEEPS = 4
EARLY = 3
coulomb_scale = 0.02
softening = 0.1
field_scale = 0.5
deposit_scale = 0.2
lowest_eig = 0.01
highest_eig = 1.99
mobility = 0.3
diffusion = 0.2
time_step = 0.2
OFFSETS = ((0, 0), (0, -1), (0, 1), (0, -2), (0, 2), (-1, 0), (1, 0))
MESH = pl.DeviceIdType.MESH
BATCH = 32
STEP = 32
ORDER = (4, 3, 2, 1)
TOP = 8


def split3(v):
    high = v.astype(BF16).astype(F32)
    rest = v - high
    mid = rest.astype(BF16).astype(F32)
    return high, mid, (rest - mid).astype(BF16).astype(F32)


def dot(a, b, dims=((1,), (0,))):
    return lax.dot_general(a, b, (dims, ((), ())), preferred_element_type=F32)


def select_rows(chooser, data, dims=((1,), (0,)), parts=3):
    pieces = split3(data)[:parts]
    total = dot(chooser, pieces[0].astype(BF16), dims)
    for piece in pieces[1:]:
        total = total + dot(chooser, piece.astype(BF16), dims)
    return total


def neighbour(step_g, step_b, groups, bricks):
    g = lax.axis_index("grp")
    b = lax.axis_index("brick")
    return (lax.rem(g + step_g + groups, groups), lax.rem(b + step_b + bricks, bricks))


def greet(groups, bricks):
    barrier = pltpu.get_barrier_semaphore()
    for step in OFFSETS[1:]:
        pl.semaphore_signal(
            barrier, inc=1, device_id=neighbour(*step, groups, bricks), device_id_type=MESH
        )
    return barrier


def slot_row(index_ref):
    return jnp.concatenate([index_ref[k : k + 1, :] for k in range(index_ref.shape[0])], axis=1)


def column(row):
    return jnp.transpose(jnp.broadcast_to(row, (128, 128)))


def columns(values):
    vals = values.astype(F32)
    return jnp.concatenate([column(vals[i : i + 1, :]) for i in range(vals.shape[0])], axis=0)


def neighbours_sum(pad, i):
    rows = pad.shape[1] - 16
    centre = pad[i + 1, TOP : TOP + rows, :]
    total = pad[i + 2, TOP : TOP + rows, :] + pad[i, TOP : TOP + rows, :]
    total = total + pad[i + 1, TOP + 1 : TOP + rows + 1, :] + pad[i + 1, TOP - 1 : TOP + rows - 1, :]
    above, below = z_shifts(centre)
    return centre, total + above + below


def z_shifts(v):
    depth = v.shape[1]
    lane = lax.broadcasted_iota(I32, v.shape, 1)
    above = jnp.where(lane == depth - 1, 0.0, pltpu.roll(v, depth - 1, 1))
    below = jnp.where(lane == 0, 0.0, pltpu.roll(v, 1, 1))
    return above, below


def face_flux(pot_low, pot_high, ion_low, ion_high):
    speed = -mobility * (pot_high - pot_low)
    return (
        jnp.maximum(speed, 0.0) * ion_low
        + jnp.minimum(speed, 0.0) * ion_high
        - diffusion * (ion_high - ion_low)
    )


def inside_flags(groups, bricks):
    g = lax.axis_index("grp")
    b = lax.axis_index("brick")
    return (
        jnp.where(g > 0, 1.0, 0.0),
        jnp.where(g < groups - 1, 1.0, 0.0),
        jnp.where(b > 0, 1.0, 0.0),
        jnp.where(b < bricks - 1, 1.0, 0.0),
    )


def start_halos(axis, fields, turn, x_out, x_in, y_out, y_in, send, recv, groups, bricks):
    nx, ny = fields[0].shape[0] - 2, fields[0].shape[1] - 2 * TOP
    out, into = (y_out, y_in) if axis else (x_out, x_in)
    for f, field in enumerate(fields):
        if axis:
            out[turn, 0, f] = field[1 : nx + 1, TOP, :]
            out[turn, 1, f] = field[1 : nx + 1, TOP + ny - 1, :]
        else:
            out[turn, 0, f] = field[1, TOP : TOP + ny, :]
            out[turn, 1, f] = field[nx, TOP : TOP + ny, :]
    copies = []
    for side in range(2):
        step = 2 * side - 1
        copy = pltpu.make_async_remote_copy(
            src_ref=out.at[turn, side, pl.ds(0, len(fields))],
            dst_ref=into.at[turn, 1 - side, pl.ds(0, len(fields))],
            send_sem=send.at[turn, 2 * axis + side],
            recv_sem=recv.at[turn, 2 * axis + 1 - side],
            device_id=neighbour(step * (1 - axis), step * axis, groups, bricks),
            device_id_type=MESH,
        )
        copy.start()
        copies.append(copy)
    return copies


def place_halos(field, at, x_in, y_in, inside):
    nx, ny = field.shape[0] - 2, field.shape[1] - 2 * TOP
    field[0, TOP : TOP + ny, :] = x_in[at[0], 0, at[1]] * inside[0]
    field[nx + 1, TOP : TOP + ny, :] = x_in[at[0], 1, at[1]] * inside[1]
    field[1 : nx + 1, TOP - 1, :] = y_in[at[0], 0, at[1]] * inside[2]
    field[1 : nx + 1, TOP + ny, :] = y_in[at[0], 1, at[1]] * inside[3]


def clear_halos(field):
    nx, ny = field.shape[0] - 2, field.shape[1] - 2 * TOP
    edge = jnp.zeros(field.shape[1:], F32)
    field[0] = edge
    field[nx + 1] = edge
    for i in range(1, nx + 1):
        field[i, 0:TOP, :] = edge[:TOP]
        field[i, TOP + ny :, :] = edge[:TOP]


def send_rows(source, target, towards, send, recv, groups, bricks):
    slots = source.shape[0] // len(OFFSETS)
    copies = []
    for k in range(1, len(OFFSETS)):
        step_g, step_b = OFFSETS[k]
        copy = pltpu.make_async_remote_copy(
            src_ref=source.at[pl.ds(k * slots, slots), :],
            dst_ref=target.at[pl.ds(k * slots, slots), :],
            send_sem=send.at[k - 1],
            recv_sem=recv.at[k - 1],
            device_id=neighbour(towards * step_g, towards * step_b, groups, bricks),
            device_id_type=MESH,
        )
        copy.start()
        copies.append(copy)
    return copies


def weights():
    middle = 0.5 * (highest_eig + lowest_eig)
    spread = 0.5 * (highest_eig - lowest_eig)
    ratio_ms = middle / spread
    now = 1.0 / ratio_ms
    table = [(0.0, 1.0 / middle)]
    for _ in range(SWEEPS - 1):
        after = 1.0 / (2.0 * ratio_ms - now)
        table.append((after * now, 2.0 * after / spread))
        now = after
    return table


def sweep(turn, held, other, resid, screen, total, whole=False):
    keep, gain = weights()[turn]
    nx, ny, nz = resid.shape

    def plane(i, carry):
        centre, around = neighbours_sum(held, i)
        diag = 6.0 + screen[i]
        rest = resid[i] - (diag * centre - around)
        resid[i] = rest
        update = gain * (rest / diag)
        if turn:
            update = keep * centre + update
            done = total[i] + update
        else:
            done = centre + update
        total[i] = done
        other[i + 1, TOP : TOP + ny, :] = done if whole else update
        return carry

    lax.fori_loop(0, nx, plane, 0, unroll=2)


def add_halos(turn, at, other, resid, screen, total, x_in, y_in, inside):
    gain = weights()[turn][1]
    nx, ny, nz = resid.shape
    for side in range(2):
        i = side * (nx - 1)
        halo = x_in[at, side, 0] * inside[side]
        step = gain * (halo / (6.0 + screen[i]))
        resid[i] = resid[i] + halo
        total[i] = total[i] + step
        other[i + 1, TOP : TOP + ny, :] = other[i + 1, TOP : TOP + ny, :] + step
    for side in range(2):
        j = side * (ny - 1)
        halo = y_in[at, side, 0] * inside[2 + side]
        step = gain * (halo / (6.0 + screen[:, j, :]))
        resid[:, j, :] = resid[:, j, :] + halo
        total[:, j, :] = total[:, j, :] + step
        other[1 : nx + 1, TOP + j, :] = other[1 : nx + 1, TOP + j, :] + step


def cell_tables(cell_ref, nx, ny, nz):
    cell = cell_ref[...]
    clusters = cell.shape[0] * cell.shape[1]
    row_of = cell // nz
    row_line = jnp.concatenate([row_of[i : i + 1, :] for i in range(cell.shape[0])], axis=1)
    into = jnp.where(
        lax.broadcasted_iota(I32, (nx * ny, clusters), 0) == row_line, 1.0, 0.0
    ).astype(BF16)
    k_col = columns(cell - row_of * nz)
    k_col = jnp.concatenate([k_col, k_col], axis=1)
    at_depth = jnp.where(
        lax.broadcasted_iota(I32, (clusters, nz), 1).astype(F32) == k_col, 1.0, 0.0
    )
    i_line = row_line // ny
    j_line = row_line - i_line * ny
    edge_line = jnp.where(j_line == 0, i_line, jnp.where(j_line == ny - 1, nx + i_line, -1))
    edge = jnp.where(
        lax.broadcasted_iota(I32, (2 * nx, clusters), 0) == edge_line, 1.0, 0.0
    ).astype(BF16)
    return into, at_depth, edge


def send_kernel(
    groups,
    bricks,
    count_ref,
    pos_hbm,
    charge_hbm,
    fill_hbm,
    cell_hbm,
    index_hbm,
    local_hbm,
    dir_hbm,
    slot_hbm,
    ion_hbm,
    prev_hbm,
    screen_hbm,
    data_ref,
    arrived_ref,
    update_ref,
    resid_ref,
    total_ref,
    into_ref,
    depth_ref,
    edge_ref,
    order_ref,
    row_feat,
    lane_feat,
    vals,
    pos,
    charges,
    fill,
    cells,
    index,
    pair_local,
    pair_dir,
    pair_slot,
    screen,
    out_rows,
    in_rows,
    x_out,
    x_in,
    y_out,
    y_in,
    pad,
    load,
    row_send,
    row_recv,
    halo_send,
    halo_recv,
):
    nx, ny, nz = ion_hbm.shape
    loads = [
        pltpu.make_async_copy(src, dst, load.at[i])
        for i, (src, dst) in enumerate(
            (
                (index_hbm, index),
                (fill_hbm, fill),
                (cell_hbm, cells),
                (prev_hbm, pad.at[0, pl.ds(1, nx), pl.ds(TOP, ny), :]),
                (pos_hbm, pos),
                (charge_hbm, charges),
                (ion_hbm, resid_ref),
                (screen_hbm, screen),
                (local_hbm, pair_local),
                (dir_hbm, pair_dir),
                (slot_hbm, pair_slot),
            )
        )
    ]
    for copy in loads:
        copy.start()
    barrier = greet(groups, bricks)
    inside = inside_flags(groups, bricks)
    clear_halos(pad.at[0])
    clear_halos(pad.at[1])
    for copy in loads[:4]:
        copy.wait()
    exchange = (x_out, x_in, y_out, y_in, halo_send, halo_recv, groups, bricks)
    clusters = charges.shape[0]
    slots = index.shape[1]
    wanted = slot_row(index)
    chooser = jnp.where(
        lax.broadcasted_iota(I32, (clusters, wanted.shape[1]), 0) == wanted, 1.0, 0.0
    ).astype(BF16)
    fill_col = columns(fill[...])
    lane = lax.broadcasted_iota(I32, (clusters, 128), 1).astype(F32)
    for copy in loads[4:]:
        copy.wait()
    charge = charges[...] * jnp.where(lane < fill_col, 1.0, 0.0)
    for d in range(3):
        data_ref[:, d * 128 : (d + 1) * 128] = pos[:, d, :]
    data_ref[:, 384:512] = charge
    pl.semaphore_wait(barrier, len(OFFSETS) - 1)
    halos = start_halos(0, [pad.at[0]], 0, *exchange) + start_halos(1, [pad.at[0]], 0, *exchange)
    out_rows[...] = select_rows(chooser, data_ref[...], ((0,), (0,)))
    slot_id = lax.broadcasted_iota(I32, (slots, 128), 0)
    for k in range(len(OFFSETS)):
        live = jnp.where(slot_id < count_ref[0, k], 1.0, 0.0)
        out_rows[k * slots : (k + 1) * slots, 384:512] = (
            out_rows[k * slots : (k + 1) * slots, 384:512] * live
        )
    sends = send_rows(out_rows, in_rows, -1, row_send, row_recv, groups, bricks)
    into, at_depth, edge = cell_tables(cells, nx, ny, nz)
    into_ref[...] = into
    edge_ref[...] = edge
    depth_ref[...] = at_depth
    deposit = select_rows(into, at_depth * jnp.sum(charge, axis=1, keepdims=True))
    resid_ref[...] = resid_ref[...] + deposit_scale * deposit.reshape(nx, ny, nz)
    for turn in range(EARLY):
        held, other = pad.at[turn % 2], pad.at[1 - turn % 2]
        if turn == EARLY - 2:
            features(data_ref, 0, row_feat, lane_feat, vals)
        if turn == EARLY - 1:
            for copy in sends:
                copy.wait()
            arrived_ref[0:slots, :] = out_rows[0:slots, :]
            arrived_ref[slots:, :] = in_rows[slots:, :]
            sort_pairs(
                pair_local,
                pair_dir[...] * slots + pair_slot[...],
                extent(data_ref),
                extent(arrived_ref),
                order_ref,
            )
            partners = arrived_ref.shape[0]
            features(arrived_ref, clusters, row_feat, lane_feat, vals)
            feature_rows(jnp.zeros((8, 512), F32), clusters + partners, row_feat, lane_feat, vals)
        sweep(turn, held, other, resid_ref, screen, total_ref)
        for copy in halos:
            copy.wait()
        add_halos(turn, turn, other, resid_ref, screen, total_ref, x_in, y_in, inside)
        if turn + 1 < EARLY:
            halos = start_halos(0, [other], turn + 1, *exchange)
            halos = halos + start_halos(1, [other], turn + 1, *exchange)
    update_ref[...] = pad[EARLY % 2, 1 : nx + 1, TOP : TOP + ny, :]


def back_kernel(
    groups,
    bricks,
    index_hbm,
    ion_hbm,
    screen_hbm,
    data_ref,
    into_ref,
    depth_ref,
    own_ref,
    part_ref,
    update_ref,
    resid_ref,
    total_ref,
    pull_ref,
    pot_ref,
    ion_ref,
    index,
    screen,
    back,
    resid,
    total,
    efield,
    x_out,
    x_in,
    y_out,
    y_in,
    pad,
    load,
    row_send,
    row_recv,
    halo_send,
    halo_recv,
):
    nx, ny, nz = ion_hbm.shape
    loads = [
        pltpu.make_async_copy(
            ion_hbm, ion_ref.at[pl.ds(1, nx), pl.ds(TOP, ny), :], load.at[0]
        ),
        pltpu.make_async_copy(screen_hbm, screen, load.at[1]),
        pltpu.make_async_copy(index_hbm, index, load.at[2]),
    ]
    for copy in loads:
        copy.start()
    barrier = greet(groups, bricks)
    inside = inside_flags(groups, bricks)
    first = pad.at[EARLY % 2]
    clear_halos(pad.at[0])
    clear_halos(pad.at[1])
    clear_halos(pot_ref)
    first[1 : nx + 1, TOP : TOP + ny, :] = update_ref[...]
    for copy in loads:
        copy.wait()
    exchange = (x_out, x_in, y_out, y_in, halo_send, halo_recv, groups, bricks)
    pl.semaphore_wait(barrier, len(OFFSETS) - 1)
    halos = start_halos(0, [first, ion_ref], 0, *exchange)
    halos = halos + start_halos(1, [first, ion_ref], 0, *exchange)
    sends = send_rows(part_ref, back, 1, row_send, row_recv, groups, bricks)
    resid[...] = resid_ref[...]
    total[...] = total_ref[...]
    slots = part_ref.shape[0] // len(OFFSETS)
    back[0:slots, :] = part_ref[0:slots, :]
    wanted = slot_row(index)
    clusters = data_ref.shape[0]
    chooser = jnp.where(
        lax.broadcasted_iota(I32, (clusters, wanted.shape[1]), 0) == wanted, 1.0, 0.0
    ).astype(BF16)
    for d in range(3):
        near = slice(d * 128, (d + 1) * 128)
        pull = data_ref[:, near] * own_ref[:, 0:128] - own_ref[:, (d + 1) * 128 : (d + 2) * 128]
        pull_ref[:, near] = coulomb_scale * data_ref[:, 384:512] * pull
    for turn in range(EARLY, SWEEPS):
        held, other = pad.at[turn % 2], pad.at[1 - turn % 2]
        last = turn == SWEEPS - 1
        other = pot_ref if last else other
        sweep(turn, held, other, resid, screen, total, last)
        for copy in halos:
            copy.wait()
        add_halos(turn, turn - EARLY, other, resid, screen, total, x_in, y_in, inside)
        halos = start_halos(0, [other], turn + 1 - EARLY, *exchange)
        halos = halos + start_halos(1, [other], turn + 1 - EARLY, *exchange)
        if turn == EARLY:
            place_halos(ion_ref, (0, 1), x_in, y_in, inside)

    def field(i, carry):
        lo, hi = TOP, TOP + ny
        above, below = z_shifts(pot_ref[i + 1, lo:hi, :])
        spot = pl.ds(pl.multiple_of(i * ny, ny), ny)
        efield[0, spot, :] = -(pot_ref[i + 2, lo:hi, :] - pot_ref[i, lo:hi, :]) * 0.5
        efield[1, spot, :] = -(pot_ref[i + 1, lo + 1 : hi + 1, :] - pot_ref[i + 1, lo - 1 : hi - 1, :]) * 0.5
        efield[2, spot, :] = -(above - below) * 0.5
        return carry

    lax.fori_loop(0, nx, field, 0, unroll=2)
    for d in range(3):
        seen = select_rows(into_ref[...], efield[d], ((0,), (0,)), 2)
        push = field_scale * jnp.sum(seen * depth_ref[...], axis=1, keepdims=True)
        near = slice(d * 128, (d + 1) * 128)
        pull_ref[:, near] = pull_ref[:, near] + data_ref[:, 384:512] * push
    for copy in sends:
        copy.wait()
    pull_ref[...] = pull_ref[...] + coulomb_scale * select_rows(chooser, back[...])
    for copy in halos:
        copy.wait()
    place_halos(pot_ref, (SWEEPS - EARLY, 0), x_in, y_in, inside)


def final_kernel(
    data_ref,
    pull_ref,
    pot,
    ion,
    into_ref,
    edge_ref,
    depth_ref,
    force_hbm,
    pot_hbm,
    next_hbm,
    force,
    after,
    store,
):
    nx, ny, nz = pot_hbm.shape
    out = [
        pltpu.make_async_copy(pot.at[pl.ds(1, nx), pl.ds(TOP, ny), :], pot_hbm, store.at[0]),
        pltpu.make_async_copy(force, force_hbm, store.at[2]),
    ]
    half = nx // 2
    for k in range(2):
        span = pl.ds(k * half, half)
        out.append(pltpu.make_async_copy(after.at[span], next_hbm.at[span], store.at[2 * k + 1]))
    out[0].start()

    charge = field_scale * data_ref[:, 384:512]
    beside = 0.5 * jnp.concatenate([pot[0, TOP : TOP + ny, :], -pot[nx + 1, TOP : TOP + ny, :]], axis=0)
    across = 0.5 * jnp.concatenate(
        [pot[1 : nx + 1, TOP - 1, :], -pot[1 : nx + 1, TOP + ny, :]], axis=0
    )
    ends = jnp.concatenate([into_ref[0:ny, :], into_ref[(nx - 1) * ny :, :]], axis=0)
    for d, (chooser, halo) in enumerate(((ends, beside), (edge_ref[...], across))):
        seen = select_rows(chooser, halo, ((0,), (0,)), 2)
        push = jnp.sum(seen * depth_ref[...], axis=1, keepdims=True)
        force[:, d, :] = charge * push + pull_ref[:, d * 128 : (d + 1) * 128]
    force[:, 2, :] = pull_ref[:, 256:384]
    out[1].start()

    def finish(i, carry):
        lo, hi = TOP, TOP + ny
        p, n = pot[i + 1, lo:hi, :], ion[i + 1, lo:hi, :]
        px = (pot[i, lo:hi, :], pot[i + 2, lo:hi, :])
        py = (pot[i + 1, lo - 1 : hi - 1, :], pot[i + 1, lo + 1 : hi + 1, :])
        ix = (ion[i, lo:hi, :], ion[i + 2, lo:hi, :])
        iy = (ion[i + 1, lo - 1 : hi - 1, :], ion[i + 1, lo + 1 : hi + 1, :])
        pz = z_shifts(p)[::-1]
        iz = z_shifts(n)[::-1]
        change = jnp.zeros_like(p)
        for ps, ns in ((px, ix), (py, iy), (pz, iz)):
            change = change + (face_flux(p, ps[1], n, ns[1]) - face_flux(ps[0], p, ns[0], n))
        after[i] = n - time_step * change
        return carry

    for k in range(2):
        lax.fori_loop(k * half, (k + 1) * half, finish, 0, unroll=2)
        out[2 + k].start()
    for copy in out:
        copy.wait()


def features(data, base, row_feat, lane_feat, vals):
    @pl.loop(0, data.shape[0] // 8, unroll=4)
    def _(g):
        at = pl.multiple_of(g * 8, 8)
        feature_rows(data[pl.ds(at, 8), :], base + at, row_feat, lane_feat, vals)


def feature_rows(data, base, row_feat, lane_feat, vals):
    spots = [data[:, d * 128 : (d + 1) * 128] for d in range(3)]
    charge = data[:, 384:512]
    here = pl.ds(base, 8)
    one = jnp.ones_like(charge)
    square = jnp.zeros_like(charge)
    left, right, weighed = [], [], []
    for d in range(3):
        high, mid, low = split3(spots[d])
        left += [-2.0 * part for part in (high, high, mid, mid, high, low)]
        right += [high, mid, high, mid, low, high]
        square = square + spots[d] * spots[d]
    left += list(split3(square + softening)) + [one] * 3
    right += [one] * 3 + list(split3(square))
    parts = [split3(v) for v in (charge, charge * spots[0], charge * spots[1], charge * spots[2])]
    for f in range(3):
        weighed += [part[f] for part in parts]
    weighed += [jnp.zeros_like(charge)] * 4
    for rows, table in ((left, row_feat), (right, lane_feat)):
        for k in range(0, len(rows), 8):
            table[here, k : k + 8, :] = jnp.transpose(jnp.stack(rows[k : k + 8]), (1, 0, 2))
    halves = [jnp.transpose(jnp.stack(weighed[k : k + 8]), (1, 0, 2)) for k in (0, 8)]
    vals[here] = jnp.concatenate(halves, axis=1).astype(BF16)


def extent(data):
    charge = data[:, 384:512]
    lane = lax.broadcasted_iota(I32, charge.shape, 1).astype(F32) + 1.0
    return jnp.max(jnp.where(charge != 0.0, lane, 0.0), axis=1, keepdims=True)


def sort_pairs(local_ref, part_ids, own_extent, part_extent, order_ref):
    rows = local_ref.shape[0]
    clusters, partners = own_extent.shape[0], part_extent.shape[0]
    own_lines, part_lines = [], []
    for r in range(rows):
        for lines, ids, ext in (
            (own_lines, local_ref[r : r + 1, :], own_extent),
            (part_lines, part_ids[r : r + 1, :], part_extent),
        ):
            spot = lax.broadcasted_iota(I32, (ext.shape[0], 128), 0)
            lines.append(jnp.sum(jnp.where(spot == ids, ext, 0.0), axis=0, keepdims=True))
    own_len = jnp.concatenate(own_lines, axis=0)
    part_len = jnp.concatenate(part_lines, axis=0)
    short = jnp.minimum(own_len, part_len)
    blank = clusters + partners
    own_code = blank - local_ref[...]
    part_code = partners - part_ids
    swap = part_len < own_len
    row_code = jnp.where(swap, part_code, own_code)
    lane_code = jnp.where(swap, own_code, part_code)
    fields = [
        v.astype(F32)
        for v in (row_code & 255, row_code >> 8, lane_code & 255, lane_code >> 8)
    ]
    upto = jnp.where(
        lax.broadcasted_iota(I32, (128, 128), 0) <= lax.broadcasted_iota(I32, (128, 128), 1), 1.0, 0.0
    ).astype(BF16)
    before = jnp.where(
        lax.broadcasted_iota(I32, (rows, rows), 1) < lax.broadcasted_iota(I32, (rows, rows), 0), 1.0, 0.0
    ).astype(BF16)
    place = jnp.full((rows, 128), -1.0, F32)
    base = jnp.zeros((1, 1), F32)
    lane = lax.broadcasted_iota(I32, (1, 128), 1)
    spans = jnp.zeros((1, 128), F32)
    for blocks in ORDER:
        member = jnp.where((short > float(STEP) * (blocks - 1)) & (short <= float(STEP) * blocks), 1.0, 0.0)
        within = dot(member.astype(BF16), upto)
        total = jnp.sum(member, axis=1, keepdims=True)
        ahead = dot(before, jnp.broadcast_to(total, (rows, 128)).astype(BF16))
        place = jnp.where(member > 0.0, base + ahead + within - 1.0, place)
        batches = jnp.floor((jnp.sum(total, axis=0, keepdims=True) + (BATCH - 1.0)) / BATCH)
        spans = jnp.where(lane == len(ORDER) - blocks, batches, spans)
        base = base + batches * BATCH
    place = place.astype(I32)
    room = order_ref.shape[1] - 1
    found = jnp.zeros((4 * room, 128), F32)
    for r in range(rows):
        at = place[r : r + 1, :]
        here = jnp.where(lax.broadcasted_iota(I32, (128, 128), 0) == at & 127, 1.0, 0.0)
        ours = lax.broadcasted_iota(I32, (room, 128), 0) == at >> 7
        load = jnp.concatenate([jnp.where(ours, f[r : r + 1, :], 0.0) for f in fields], axis=0)
        found = found + dot(load.astype(BF16), here.astype(BF16), ((1,), (1,)))
    found = [found[i * room : (i + 1) * room, :] for i in range(4)]
    order_ref[0, 0:room, :] = blank - (found[0] + 256.0 * found[1]).astype(I32)
    order_ref[1, 0:room, :] = blank - (found[2] + 256.0 * found[3]).astype(I32)
    order_ref[0, room : room + 1, :] = spans.astype(I32)
    order_ref[1, room : room + 1, :] = spans.astype(I32)


def distances(row_ids, lane_ids, rows, row_feat, lane_feat, dist):
    blank = jnp.zeros((24, 128), F32)
    for k in range(0, len(row_ids), 2):
        left = jnp.concatenate([row_feat[o] for o in row_ids[k : k + 2]], axis=0)
        left = left[:, :rows].astype(BF16)
        a, b = (lane_feat[r] for r in lane_ids[k : k + 2])
        right = jnp.concatenate(
            [
                jnp.concatenate([a, blank], axis=0).astype(BF16),
                jnp.concatenate([blank, b], axis=0).astype(BF16),
            ],
            axis=1,
        )
        dist[k // 2, 0:rows, :] = dot(left, right, ((0,), (0,)))


def tile_sums(row_ids, lane_ids, rows, dist, vals, acc):
    sums = []
    for j in range(len(row_ids)):
        root = lax.rsqrt(dist[j // 2, 0:rows, (j % 2) * 128 : (j % 2) * 128 + 128])
        u = root * root * root
        high = u.astype(BF16)
        low = (u - high.astype(F32)).astype(BF16)
        mine = vals[row_ids[j]][:, :rows]
        theirs = vals[lane_ids[j]]
        if rows == 128:
            on_lane = dot(jnp.concatenate([mine, mine], axis=1), jnp.concatenate([high, low], axis=0))
        else:
            on_lane = dot(mine, high) + dot(mine, low)
        on_row = dot(
            jnp.concatenate([theirs, theirs], axis=1),
            jnp.concatenate([high, low], axis=1),
            ((1,), (1,)),
        )
        sums.append((on_row, on_lane))
    for j, (on_row, on_lane) in enumerate(sums):
        acc[row_ids[j], :, 0:rows] += on_row
        acc[lane_ids[j]] += on_lane


def pair_kernel(
    order,
    arrived_ref,
    row_feat,
    lane_feat,
    vals,
    own_ref,
    part_ref,
    acc,
    dist,
):
    clusters, partners = own_ref.shape[0], arrived_ref.shape[0]
    acc[...] = jnp.zeros_like(acc)
    room = order.shape[1] - 1
    spans = []
    base = 0
    for at in range(len(ORDER)):
        batches = order[0, room, at]
        spans.append((base, batches))
        base = base + batches * BATCH
    for blocks, (base, batches) in zip(ORDER, spans):
        rows = STEP * blocks

        def ids(turn, base=base):
            at = base + turn * BATCH
            line, first = at >> 7, at & 127
            return [[order[s, line, first + j] for j in range(BATCH)] for s in range(2)]

        @pl.when(batches > 0)
        def _(batches=batches, ids=ids, rows=rows):
            distances(*ids(0), rows, row_feat, lane_feat, dist)

            @pl.loop(0, batches)
            def _(turn):
                now = ids(turn)
                ahead = ids(jnp.minimum(turn + 1, batches - 1))
                tile_sums(*now, rows, dist, vals, acc)
                distances(*ahead, rows, row_feat, lane_feat, dist)

    def totals(first):
        parts = [
            jnp.transpose(acc[pl.ds(first, 8), f : f + 8, :], (1, 0, 2)) for f in (0, 8)
        ]
        return [parts[0][c] + (parts[0][4 + c] + parts[1][c]) for c in range(4)]

    @pl.loop(0, clusters // 8, unroll=4)
    def _(g):
        at = pl.multiple_of(g * 8, 8)
        for c, total in enumerate(totals(at)):
            own_ref[pl.ds(at, 8), c * 128 : (c + 1) * 128] = total

    @pl.loop(0, partners // 8, unroll=4)
    def _(g):
        at = pl.multiple_of(g * 8, 8)
        sums = totals(clusters + at)
        here = arrived_ref[pl.ds(at, 8), :]
        for d in range(3):
            near = slice(d * 128, (d + 1) * 128)
            part_ref[pl.ds(at, 8), near] = here[:, 384:512] * (here[:, near] * sums[0] - sums[d + 1])


def shards(
    groups,
    bricks,
    positions,
    charges,
    cluster_fill,
    cluster_cell,
    send_index,
    send_count,
    pair_local,
    pair_dir,
    pair_slot,
    ion_density,
    potential_prev,
    screening,
):
    clusters = cluster_fill.shape[0]
    psize = charges.shape[0] // clusters
    dirs, slots = send_index.shape
    nx, ny, nz = ion_density.shape
    placed = positions.reshape(3, clusters, psize).transpose(1, 0, 2)
    vmem = pl.BlockSpec(memory_space=pltpu.VMEM)
    smem = pl.BlockSpec(memory_space=pltpu.SMEM)
    hbm = pl.BlockSpec(memory_space=pltpu.HBM)
    shape = lambda *dims: jax.ShapeDtypeStruct(dims, F32)
    halo = lambda turns, fields, length: pltpu.VMEM((turns, 2, fields, length, nz), F32)
    block = shape(nx, ny, nz)
    rows = shape(dirs * slots, 4 * psize)
    padded = (nx + 2, ny + 2 * TOP, nz)
    cells = cluster_cell.reshape(clusters // 128, 128)
    late = SWEEPS + 1 - EARLY
    table = (clusters + dirs * slots + 8,)
    pairs = pair_local.shape[0]
    lines = lambda v: v.reshape(pairs // 128, 128)
    room = -(-(pairs + len(ORDER) * BATCH) // 1024) * 8
    still = lambda v: pltpu.with_memory_space_constraint(v, pltpu.HBM)
    ion_density, potential_prev, screening = map(still, (ion_density, potential_prev, screening))
    data, arrived, update, resid, total, into, at_depth, edge, order, *tables = pl.pallas_call(
        functools.partial(send_kernel, groups, bricks),
        out_shape=(
            shape(clusters, 4 * psize),
            rows,
            block,
            block,
            block,
            jax.ShapeDtypeStruct((nx * ny, clusters), BF16),
            shape(clusters, nz),
            jax.ShapeDtypeStruct((2 * nx, clusters), BF16),
            jax.ShapeDtypeStruct((2, room + 1, 128), I32),
            shape(*table, 24, psize),
            shape(*table, 24, psize),
            jax.ShapeDtypeStruct((*table, 16, psize), BF16),
        ),
        in_specs=[smem] + [hbm] * 11,
        out_specs=[vmem] * 12,
        scratch_shapes=[
            pltpu.VMEM((clusters, 3, psize), F32),
            pltpu.VMEM((clusters, psize), F32),
            pltpu.VMEM((clusters // 128, 128), I32),
            pltpu.VMEM((clusters // 128, 128), I32),
            pltpu.VMEM((dirs, slots), I32),
            pltpu.VMEM((pairs // 128, 128), I32),
            pltpu.VMEM((pairs // 128, 128), I32),
            pltpu.VMEM((pairs // 128, 128), I32),
            pltpu.VMEM((nx, ny, nz), F32),
            pltpu.VMEM((dirs * slots, 4 * psize), F32),
            pltpu.VMEM((dirs * slots, 4 * psize), F32),
            halo(EARLY, 1, ny),
            halo(EARLY, 1, ny),
            halo(EARLY, 1, nx),
            halo(EARLY, 1, nx),
            pltpu.VMEM((2, *padded), F32),
            pltpu.SemaphoreType.DMA((11,)),
            pltpu.SemaphoreType.DMA((dirs - 1,)),
            pltpu.SemaphoreType.DMA((dirs - 1,)),
            pltpu.SemaphoreType.DMA((EARLY, 4)),
            pltpu.SemaphoreType.DMA((EARLY, 4)),
        ],
        compiler_params=pltpu.CompilerParams(
            collective_id=0, has_side_effects=True, vmem_limit_bytes=32 << 20
        ),
        name="send",
    )(
        still(send_count),
        still(placed),
        still(charges.reshape(clusters, psize)),
        still(cluster_fill.reshape(clusters // 128, 128)),
        still(cells),
        still(send_index),
        still(lines(pair_local)),
        still(lines(pair_dir)),
        still(lines(pair_slot)),
        ion_density,
        potential_prev,
        screening,
    )
    own_sums, part_sums = pl.pallas_call(
        pair_kernel,
        out_shape=(shape(clusters, 4 * psize), shape(dirs * slots, 3 * psize)),
        in_specs=[smem] + [vmem] * 4,
        out_specs=[vmem] * 2,
        scratch_shapes=[
            pltpu.VMEM((*table, 16, psize), F32),
            pltpu.VMEM((BATCH // 2, psize, 2 * psize), F32),
        ],
        compiler_params=pltpu.CompilerParams(vmem_limit_bytes=28 << 20),
        name="pairs",
    )(order, arrived, *tables)
    padding = shape(*padded)
    pull, pot, ion = pl.pallas_call(
        functools.partial(back_kernel, groups, bricks),
        out_shape=(shape(clusters, 3 * psize), padding, padding),
        in_specs=[hbm] * 3 + [vmem] * 8,
        out_specs=[vmem] * 3,
        scratch_shapes=[
            pltpu.VMEM((dirs, slots), I32),
            pltpu.VMEM((nx, ny, nz), F32),
            pltpu.VMEM((dirs * slots, 3 * psize), F32),
            pltpu.VMEM((nx, ny, nz), F32),
            pltpu.VMEM((nx, ny, nz), F32),
            pltpu.VMEM((3, nx * ny, nz), F32),
            halo(late, 2, ny),
            halo(late, 2, ny),
            halo(late, 2, nx),
            halo(late, 2, nx),
            pltpu.VMEM((2, *padded), F32),
            pltpu.SemaphoreType.DMA((3,)),
            pltpu.SemaphoreType.DMA((dirs - 1,)),
            pltpu.SemaphoreType.DMA((dirs - 1,)),
            pltpu.SemaphoreType.DMA((late, 4)),
            pltpu.SemaphoreType.DMA((late, 4)),
        ],
        compiler_params=pltpu.CompilerParams(
            collective_id=1, has_side_effects=True, vmem_limit_bytes=28 << 20
        ),
        name="back",
    )(still(send_index), ion_density, screening, data, into, at_depth, own_sums, part_sums, update, resid, total)
    forces, potential, ion_next = pl.pallas_call(
        final_kernel,
        out_shape=(shape(clusters, 3, psize), block, block),
        in_specs=[vmem] * 7,
        out_specs=[hbm] * 3,
        scratch_shapes=[
            pltpu.VMEM((clusters, 3, psize), F32),
            pltpu.VMEM((nx, ny, nz), F32),
            pltpu.SemaphoreType.DMA((4,)),
        ],
        compiler_params=pltpu.CompilerParams(vmem_limit_bytes=28 << 20),
        name="final",
    )(data, pull, pot, ion, into, edge, at_depth)
    return (forces.transpose(1, 0, 2).reshape(3, -1), potential, ion_next)


def solution(mesh):
    in_specs = (
        P(None, ("grp", "brick")),
        P(("grp", "brick")),
        P(("grp", "brick")),
        P(("grp", "brick")),
        P(("grp", "brick"), None),
        P(("grp", "brick"), None),
        P(("grp", "brick")),
        P(("grp", "brick")),
        P(("grp", "brick")),
        P("grp", "brick", None),
        P("grp", "brick", None),
        P("grp", "brick", None),
    )
    out_specs = (P(None, ("grp", "brick")), P("grp", "brick", None), P("grp", "brick", None))
    body = functools.partial(shards, mesh.shape["grp"], mesh.shape["brick"])
    return jax.shard_map(body, mesh=mesh, in_specs=in_specs, out_specs=out_specs, check_vma=False)
```

```python
import functools

import jax
import jax.numpy as jnp
from jax import lax
from jax.experimental import pallas as pl
from jax.experimental.pallas import tpu as pltpu
from jax.sharding import PartitionSpec as P

F32, BF16, I32 = jnp.float32, jnp.bfloat16, jnp.int32
SWEEPS = 4
EARLY = 3
coulomb_scale = 0.02
softening = 0.1
field_scale = 0.5
deposit_scale = 0.2
lowest_eig = 0.01
highest_eig = 1.99
mobility = 0.3
diffusion = 0.2
time_step = 0.2
OFFSETS = ((0, 0), (0, -1), (0, 1), (0, -2), (0, 2), (-1, 0), (1, 0))
MESH = pl.DeviceIdType.MESH
BATCH = 32
STEP = 32
ORDER = (4, 3, 2, 1)
TOP = 8


def split3(v):
    high = v.astype(BF16).astype(F32)
    rest = v - high
    mid = rest.astype(BF16).astype(F32)
    return high, mid, (rest - mid).astype(BF16).astype(F32)


def dot(a, b, dims=((1,), (0,))):
    return lax.dot_general(a, b, (dims, ((), ())), preferred_element_type=F32)


def select_rows(chooser, data, dims=((1,), (0,)), parts=3):
    pieces = split3(data)[:parts]
    total = dot(chooser, pieces[0].astype(BF16), dims)
    for piece in pieces[1:]:
        total = total + dot(chooser, piece.astype(BF16), dims)
    return total


def neighbour(step_g, step_b, groups, bricks):
    g = lax.axis_index("grp")
    b = lax.axis_index("brick")
    return (lax.rem(g + step_g + groups, groups), lax.rem(b + step_b + bricks, bricks))


def greet(groups, bricks):
    barrier = pltpu.get_barrier_semaphore()
    for step in OFFSETS[1:]:
        pl.semaphore_signal(
            barrier, inc=1, device_id=neighbour(*step, groups, bricks), device_id_type=MESH
        )
    return barrier


def slot_row(index_ref):
    return jnp.concatenate([index_ref[k : k + 1, :] for k in range(index_ref.shape[0])], axis=1)


def column(row):
    return jnp.transpose(jnp.broadcast_to(row, (128, 128)))


def columns(values):
    vals = values.astype(F32)
    return jnp.concatenate([column(vals[i : i + 1, :]) for i in range(vals.shape[0])], axis=0)


def neighbours_sum(pad, i):
    rows = pad.shape[1] - 16
    centre = pad[i + 1, TOP : TOP + rows, :]
    total = pad[i + 2, TOP : TOP + rows, :] + pad[i, TOP : TOP + rows, :]
    total = total + pad[i + 1, TOP + 1 : TOP + rows + 1, :] + pad[i + 1, TOP - 1 : TOP + rows - 1, :]
    above, below = z_shifts(centre)
    return centre, total + above + below


def z_shifts(v):
    depth = v.shape[1]
    lane = lax.broadcasted_iota(I32, v.shape, 1)
    above = jnp.where(lane == depth - 1, 0.0, pltpu.roll(v, depth - 1, 1))
    below = jnp.where(lane == 0, 0.0, pltpu.roll(v, 1, 1))
    return above, below


def face_flux(pot_low, pot_high, ion_low, ion_high):
    speed = -mobility * (pot_high - pot_low)
    return (
        jnp.maximum(speed, 0.0) * ion_low
        + jnp.minimum(speed, 0.0) * ion_high
        - diffusion * (ion_high - ion_low)
    )


def inside_flags(groups, bricks):
    g = lax.axis_index("grp")
    b = lax.axis_index("brick")
    return (
        jnp.where(g > 0, 1.0, 0.0),
        jnp.where(g < groups - 1, 1.0, 0.0),
        jnp.where(b > 0, 1.0, 0.0),
        jnp.where(b < bricks - 1, 1.0, 0.0),
    )


def start_halos(axis, fields, turn, x_out, x_in, y_out, y_in, send, recv, groups, bricks):
    nx, ny = fields[0].shape[0] - 2, fields[0].shape[1] - 2 * TOP
    out, into = (y_out, y_in) if axis else (x_out, x_in)
    for f, field in enumerate(fields):
        if axis:
            out[turn, 0, f] = field[1 : nx + 1, TOP, :]
            out[turn, 1, f] = field[1 : nx + 1, TOP + ny - 1, :]
        else:
            out[turn, 0, f] = field[1, TOP : TOP + ny, :]
            out[turn, 1, f] = field[nx, TOP : TOP + ny, :]
    copies = []
    for side in range(2):
        step = 2 * side - 1
        copy = pltpu.make_async_remote_copy(
            src_ref=out.at[turn, side, pl.ds(0, len(fields))],
            dst_ref=into.at[turn, 1 - side, pl.ds(0, len(fields))],
            send_sem=send.at[turn, 2 * axis + side],
            recv_sem=recv.at[turn, 2 * axis + 1 - side],
            device_id=neighbour(step * (1 - axis), step * axis, groups, bricks),
            device_id_type=MESH,
        )
        copy.start()
        copies.append(copy)
    return copies


def place_halos(field, at, x_in, y_in, inside):
    nx, ny = field.shape[0] - 2, field.shape[1] - 2 * TOP
    field[0, TOP : TOP + ny, :] = x_in[at[0], 0, at[1]] * inside[0]
    field[nx + 1, TOP : TOP + ny, :] = x_in[at[0], 1, at[1]] * inside[1]
    field[1 : nx + 1, TOP - 1, :] = y_in[at[0], 0, at[1]] * inside[2]
    field[1 : nx + 1, TOP + ny, :] = y_in[at[0], 1, at[1]] * inside[3]


def clear_halos(field):
    nx, ny = field.shape[0] - 2, field.shape[1] - 2 * TOP
    edge = jnp.zeros(field.shape[1:], F32)
    field[0] = edge
    field[nx + 1] = edge
    for i in range(1, nx + 1):
        field[i, 0:TOP, :] = edge[:TOP]
        field[i, TOP + ny :, :] = edge[:TOP]


def send_rows(source, target, towards, send, recv, groups, bricks):
    slots = source.shape[0] // len(OFFSETS)
    copies = []
    for k in range(1, len(OFFSETS)):
        step_g, step_b = OFFSETS[k]
        copy = pltpu.make_async_remote_copy(
            src_ref=source.at[pl.ds(k * slots, slots), :],
            dst_ref=target.at[pl.ds(k * slots, slots), :],
            send_sem=send.at[k - 1],
            recv_sem=recv.at[k - 1],
            device_id=neighbour(towards * step_g, towards * step_b, groups, bricks),
            device_id_type=MESH,
        )
        copy.start()
        copies.append(copy)
    return copies


def weights():
    middle = 0.5 * (highest_eig + lowest_eig)
    spread = 0.5 * (highest_eig - lowest_eig)
    ratio_ms = middle / spread
    now = 1.0 / ratio_ms
    table = [(0.0, 1.0 / middle)]
    for _ in range(SWEEPS - 1):
        after = 1.0 / (2.0 * ratio_ms - now)
        table.append((after * now, 2.0 * after / spread))
        now = after
    return table


def sweep(turn, held, other, resid, screen, total, whole=False):
    keep, gain = weights()[turn]
    nx, ny, nz = resid.shape

    def plane(i, carry):
        centre, around = neighbours_sum(held, i)
        diag = 6.0 + screen[i]
        rest = resid[i] - (diag * centre - around)
        resid[i] = rest
        update = gain * (rest / diag)
        if turn:
            update = keep * centre + update
            done = total[i] + update
        else:
            done = centre + update
        total[i] = done
        other[i + 1, TOP : TOP + ny, :] = done if whole else update
        return carry

    lax.fori_loop(0, nx, plane, 0, unroll=2)


def add_halos(turn, at, other, resid, screen, total, x_in, y_in, inside):
    gain = weights()[turn][1]
    nx, ny, nz = resid.shape
    for side in range(2):
        i = side * (nx - 1)
        halo = x_in[at, side, 0] * inside[side]
        step = gain * (halo / (6.0 + screen[i]))
        resid[i] = resid[i] + halo
        total[i] = total[i] + step
        other[i + 1, TOP : TOP + ny, :] = other[i + 1, TOP : TOP + ny, :] + step
    for side in range(2):
        j = side * (ny - 1)
        halo = y_in[at, side, 0] * inside[2 + side]
        step = gain * (halo / (6.0 + screen[:, j, :]))
        resid[:, j, :] = resid[:, j, :] + halo
        total[:, j, :] = total[:, j, :] + step
        other[1 : nx + 1, TOP + j, :] = other[1 : nx + 1, TOP + j, :] + step


def cell_tables(cell_ref, nx, ny, nz):
    cell = cell_ref[...]
    clusters = cell.shape[0] * cell.shape[1]
    row_of = cell // nz
    row_line = jnp.concatenate([row_of[i : i + 1, :] for i in range(cell.shape[0])], axis=1)
    into = jnp.where(
        lax.broadcasted_iota(I32, (nx * ny, clusters), 0) == row_line, 1.0, 0.0
    ).astype(BF16)
    k_col = columns(cell - row_of * nz)
    k_col = jnp.concatenate([k_col, k_col], axis=1)
    at_depth = jnp.where(
        lax.broadcasted_iota(I32, (clusters, nz), 1).astype(F32) == k_col, 1.0, 0.0
    )
    i_line = row_line // ny
    j_line = row_line - i_line * ny
    edge_line = jnp.where(j_line == 0, i_line, jnp.where(j_line == ny - 1, nx + i_line, -1))
    edge = jnp.where(
        lax.broadcasted_iota(I32, (2 * nx, clusters), 0) == edge_line, 1.0, 0.0
    ).astype(BF16)
    return into, at_depth, edge


def send_kernel(
    groups,
    bricks,
    count_ref,
    pos_hbm,
    charge_hbm,
    fill_hbm,
    cell_hbm,
    index_hbm,
    local_hbm,
    dir_hbm,
    slot_hbm,
    ion_hbm,
    prev_hbm,
    screen_hbm,
    data_ref,
    arrived_ref,
    update_ref,
    resid_ref,
    total_ref,
    ion_ref,
    into_ref,
    depth_ref,
    edge_ref,
    order_ref,
    row_feat,
    lane_feat,
    vals,
    pos,
    charges,
    fill,
    cells,
    index,
    pair_local,
    pair_dir,
    pair_slot,
    screen,
    out_rows,
    in_rows,
    x_out,
    x_in,
    y_out,
    y_in,
    pad,
    load,
    row_send,
    row_recv,
    halo_send,
    halo_recv,
):
    nx, ny, nz = ion_hbm.shape
    loads = [
        pltpu.make_async_copy(src, dst, load.at[i])
        for i, (src, dst) in enumerate(
            (
                (prev_hbm, pad.at[0, pl.ds(1, nx), pl.ds(TOP, ny), :]),
                (ion_hbm, ion_ref.at[pl.ds(1, nx), pl.ds(TOP, ny), :]),
                (index_hbm, index),
                (fill_hbm, fill),
                (cell_hbm, cells),
                (pos_hbm, pos),
                (charge_hbm, charges),
                (screen_hbm, screen),
                (local_hbm, pair_local),
                (dir_hbm, pair_dir),
                (slot_hbm, pair_slot),
            )
        )
    ]
    for copy in loads:
        copy.start()
    barrier = greet(groups, bricks)
    inside = inside_flags(groups, bricks)
    clear_halos(pad.at[0])
    clear_halos(pad.at[1])
    for copy in loads[:2]:
        copy.wait()
    exchange = (x_out, x_in, y_out, y_in, halo_send, halo_recv, groups, bricks)
    pl.semaphore_wait(barrier, len(OFFSETS) - 1)
    fields = [pad.at[0], ion_ref]
    halos = start_halos(0, fields, 0, *exchange) + start_halos(1, fields, 0, *exchange)
    for copy in loads[2:]:
        copy.wait()
    clusters = charges.shape[0]
    slots = index.shape[1]
    wanted = slot_row(index)
    chooser = jnp.where(
        lax.broadcasted_iota(I32, (clusters, wanted.shape[1]), 0) == wanted, 1.0, 0.0
    ).astype(BF16)
    fill_col = columns(fill[...])
    lane = lax.broadcasted_iota(I32, (clusters, 128), 1).astype(F32)
    charge = charges[...] * jnp.where(lane < fill_col, 1.0, 0.0)
    for d in range(3):
        data_ref[:, d * 128 : (d + 1) * 128] = pos[:, d, :]
    data_ref[:, 384:512] = charge
    out_rows[...] = select_rows(chooser, data_ref[...], ((0,), (0,)))
    slot_id = lax.broadcasted_iota(I32, (slots, 128), 0)
    for k in range(len(OFFSETS)):
        live = jnp.where(slot_id < count_ref[0, k], 1.0, 0.0)
        out_rows[k * slots : (k + 1) * slots, 384:512] = (
            out_rows[k * slots : (k + 1) * slots, 384:512] * live
        )
    sends = send_rows(out_rows, in_rows, -1, row_send, row_recv, groups, bricks)
    into, at_depth, edge = cell_tables(cells, nx, ny, nz)
    into_ref[...] = into
    edge_ref[...] = edge
    depth_ref[...] = at_depth
    deposit = select_rows(into, at_depth * jnp.sum(charge, axis=1, keepdims=True))
    density = ion_ref[1 : nx + 1, TOP : TOP + ny, :]
    resid_ref[...] = density + deposit_scale * deposit.reshape(nx, ny, nz)
    for turn in range(EARLY):
        held, other = pad.at[turn % 2], pad.at[1 - turn % 2]
        if turn == EARLY - 2:
            features(data_ref, 0, row_feat, lane_feat, vals)
        if turn == EARLY - 1:
            for copy in sends:
                copy.wait()
            arrived_ref[0:slots, :] = out_rows[0:slots, :]
            arrived_ref[slots:, :] = in_rows[slots:, :]
            sort_pairs(
                pair_local,
                pair_dir[...] * slots + pair_slot[...],
                extent(data_ref),
                extent(arrived_ref),
                order_ref,
            )
            partners = arrived_ref.shape[0]
            features(arrived_ref, clusters, row_feat, lane_feat, vals)
            feature_rows(jnp.zeros((8, 512), F32), clusters + partners, row_feat, lane_feat, vals)
        sweep(turn, held, other, resid_ref, screen, total_ref)
        for copy in halos:
            copy.wait()
        add_halos(turn, turn, other, resid_ref, screen, total_ref, x_in, y_in, inside)
        if turn + 1 < EARLY:
            halos = start_halos(0, [other], turn + 1, *exchange)
            halos = halos + start_halos(1, [other], turn + 1, *exchange)
        if turn == 0:
            place_halos(ion_ref, (0, 1), x_in, y_in, inside)
    update_ref[...] = pad[EARLY % 2, 1 : nx + 1, TOP : TOP + ny, :]


def back_kernel(
    groups,
    bricks,
    index_hbm,
    screen_hbm,
    data_ref,
    into_ref,
    depth_ref,
    own_ref,
    part_ref,
    update_ref,
    resid_ref,
    total_ref,
    pull_ref,
    pot_ref,
    index,
    screen,
    back,
    resid,
    total,
    efield,
    x_out,
    x_in,
    y_out,
    y_in,
    pad,
    load,
    row_send,
    row_recv,
    halo_send,
    halo_recv,
):
    nx, ny, nz = screen_hbm.shape
    loads = [
        pltpu.make_async_copy(screen_hbm, screen, load.at[0]),
        pltpu.make_async_copy(index_hbm, index, load.at[1]),
    ]
    for copy in loads:
        copy.start()
    barrier = greet(groups, bricks)
    inside = inside_flags(groups, bricks)
    first = pad.at[EARLY % 2]
    clear_halos(pad.at[0])
    clear_halos(pad.at[1])
    clear_halos(pot_ref)
    first[1 : nx + 1, TOP : TOP + ny, :] = update_ref[...]
    exchange = (x_out, x_in, y_out, y_in, halo_send, halo_recv, groups, bricks)
    pl.semaphore_wait(barrier, len(OFFSETS) - 1)
    halos = start_halos(0, [first], 0, *exchange) + start_halos(1, [first], 0, *exchange)
    sends = send_rows(part_ref, back, 1, row_send, row_recv, groups, bricks)
    for copy in loads:
        copy.wait()
    resid[...] = resid_ref[...]
    total[...] = total_ref[...]
    slots = part_ref.shape[0] // len(OFFSETS)
    back[0:slots, :] = part_ref[0:slots, :]
    wanted = slot_row(index)
    clusters = data_ref.shape[0]
    chooser = jnp.where(
        lax.broadcasted_iota(I32, (clusters, wanted.shape[1]), 0) == wanted, 1.0, 0.0
    ).astype(BF16)
    for d in range(3):
        near = slice(d * 128, (d + 1) * 128)
        pull = data_ref[:, near] * own_ref[:, 0:128] - own_ref[:, (d + 1) * 128 : (d + 2) * 128]
        pull_ref[:, near] = coulomb_scale * data_ref[:, 384:512] * pull
    for turn in range(EARLY, SWEEPS):
        held, other = pad.at[turn % 2], pad.at[1 - turn % 2]
        last = turn == SWEEPS - 1
        other = pot_ref if last else other
        sweep(turn, held, other, resid, screen, total, last)
        for copy in halos:
            copy.wait()
        add_halos(turn, turn - EARLY, other, resid, screen, total, x_in, y_in, inside)
        halos = start_halos(0, [other], turn + 1 - EARLY, *exchange)
        halos = halos + start_halos(1, [other], turn + 1 - EARLY, *exchange)

    def field(i, carry):
        lo, hi = TOP, TOP + ny
        above, below = z_shifts(pot_ref[i + 1, lo:hi, :])
        spot = pl.ds(pl.multiple_of(i * ny, ny), ny)
        efield[0, spot, :] = -(pot_ref[i + 2, lo:hi, :] - pot_ref[i, lo:hi, :]) * 0.5
        efield[1, spot, :] = -(pot_ref[i + 1, lo + 1 : hi + 1, :] - pot_ref[i + 1, lo - 1 : hi - 1, :]) * 0.5
        efield[2, spot, :] = -(above - below) * 0.5
        return carry

    lax.fori_loop(0, nx, field, 0, unroll=2)
    for d in range(3):
        seen = select_rows(into_ref[...], efield[d], ((0,), (0,)), 2)
        push = field_scale * jnp.sum(seen * depth_ref[...], axis=1, keepdims=True)
        near = slice(d * 128, (d + 1) * 128)
        pull_ref[:, near] = pull_ref[:, near] + data_ref[:, 384:512] * push
    for copy in sends:
        copy.wait()
    pull_ref[...] = pull_ref[...] + coulomb_scale * select_rows(chooser, back[...])
    for copy in halos:
        copy.wait()
    place_halos(pot_ref, (SWEEPS - EARLY, 0), x_in, y_in, inside)


def final_kernel(
    data_ref,
    pull_ref,
    pot,
    ion,
    into_ref,
    edge_ref,
    depth_ref,
    force_hbm,
    pot_hbm,
    next_hbm,
    force,
    after,
    store,
):
    nx, ny, nz = pot_hbm.shape
    out = [
        pltpu.make_async_copy(pot.at[pl.ds(1, nx), pl.ds(TOP, ny), :], pot_hbm, store.at[0]),
        pltpu.make_async_copy(force, force_hbm, store.at[2]),
    ]
    half = nx // 2
    for k in range(2):
        span = pl.ds(k * half, half)
        out.append(pltpu.make_async_copy(after.at[span], next_hbm.at[span], store.at[2 * k + 1]))
    out[0].start()

    charge = field_scale * data_ref[:, 384:512]
    beside = 0.5 * jnp.concatenate([pot[0, TOP : TOP + ny, :], -pot[nx + 1, TOP : TOP + ny, :]], axis=0)
    across = 0.5 * jnp.concatenate(
        [pot[1 : nx + 1, TOP - 1, :], -pot[1 : nx + 1, TOP + ny, :]], axis=0
    )
    ends = jnp.concatenate([into_ref[0:ny, :], into_ref[(nx - 1) * ny :, :]], axis=0)
    for d, (chooser, halo) in enumerate(((ends, beside), (edge_ref[...], across))):
        seen = select_rows(chooser, halo, ((0,), (0,)), 2)
        push = jnp.sum(seen * depth_ref[...], axis=1, keepdims=True)
        force[:, d, :] = charge * push + pull_ref[:, d * 128 : (d + 1) * 128]
    force[:, 2, :] = pull_ref[:, 256:384]
    out[1].start()

    def finish(i, carry):
        lo, hi = TOP, TOP + ny
        p, n = pot[i + 1, lo:hi, :], ion[i + 1, lo:hi, :]
        px = (pot[i, lo:hi, :], pot[i + 2, lo:hi, :])
        py = (pot[i + 1, lo - 1 : hi - 1, :], pot[i + 1, lo + 1 : hi + 1, :])
        ix = (ion[i, lo:hi, :], ion[i + 2, lo:hi, :])
        iy = (ion[i + 1, lo - 1 : hi - 1, :], ion[i + 1, lo + 1 : hi + 1, :])
        pz = z_shifts(p)[::-1]
        iz = z_shifts(n)[::-1]
        change = jnp.zeros_like(p)
        for ps, ns in ((px, ix), (py, iy), (pz, iz)):
            change = change + (face_flux(p, ps[1], n, ns[1]) - face_flux(ps[0], p, ns[0], n))
        after[i] = n - time_step * change
        return carry

    for k in range(2):
        lax.fori_loop(k * half, (k + 1) * half, finish, 0, unroll=2)
        out[2 + k].start()
    for copy in out:
        copy.wait()


def features(data, base, row_feat, lane_feat, vals):
    @pl.loop(0, data.shape[0] // 8, unroll=4)
    def _(g):
        at = pl.multiple_of(g * 8, 8)
        feature_rows(data[pl.ds(at, 8), :], base + at, row_feat, lane_feat, vals)


def feature_rows(data, base, row_feat, lane_feat, vals):
    spots = [data[:, d * 128 : (d + 1) * 128] for d in range(3)]
    charge = data[:, 384:512]
    here = pl.ds(base, 8)
    one = jnp.ones_like(charge)
    square = jnp.zeros_like(charge)
    left, right, weighed = [], [], []
    for d in range(3):
        high, mid, low = split3(spots[d])
        left += [-2.0 * part for part in (high, high, mid, mid, high, low)]
        right += [high, mid, high, mid, low, high]
        square = square + spots[d] * spots[d]
    left += list(split3(square + softening)) + [one] * 3
    right += [one] * 3 + list(split3(square))
    parts = [split3(v) for v in (charge, charge * spots[0], charge * spots[1], charge * spots[2])]
    for f in range(3):
        weighed += [part[f] for part in parts]
    weighed += [jnp.zeros_like(charge)] * 4
    for rows, table in ((left, row_feat), (right, lane_feat)):
        for k in range(0, len(rows), 8):
            table[here, k : k + 8, :] = jnp.transpose(jnp.stack(rows[k : k + 8]), (1, 0, 2))
    halves = [jnp.transpose(jnp.stack(weighed[k : k + 8]), (1, 0, 2)) for k in (0, 8)]
    vals[here] = jnp.concatenate(halves, axis=1).astype(BF16)


def extent(data):
    charge = data[:, 384:512]
    lane = lax.broadcasted_iota(I32, charge.shape, 1).astype(F32) + 1.0
    return jnp.max(jnp.where(charge != 0.0, lane, 0.0), axis=1, keepdims=True)


def sort_pairs(local_ref, part_ids, own_extent, part_extent, order_ref):
    rows = local_ref.shape[0]
    clusters, partners = own_extent.shape[0], part_extent.shape[0]
    own_lines, part_lines = [], []
    for r in range(rows):
        for lines, ids, ext in (
            (own_lines, local_ref[r : r + 1, :], own_extent),
            (part_lines, part_ids[r : r + 1, :], part_extent),
        ):
            spot = lax.broadcasted_iota(I32, (ext.shape[0], 128), 0)
            lines.append(jnp.sum(jnp.where(spot == ids, ext, 0.0), axis=0, keepdims=True))
    own_len = jnp.concatenate(own_lines, axis=0)
    part_len = jnp.concatenate(part_lines, axis=0)
    short = jnp.minimum(own_len, part_len)
    blank = clusters + partners
    own_code = blank - local_ref[...]
    part_code = partners - part_ids
    swap = part_len < own_len
    row_code = jnp.where(swap, part_code, own_code)
    lane_code = jnp.where(swap, own_code, part_code)
    fields = [
        v.astype(F32)
        for v in (row_code & 255, row_code >> 8, lane_code & 255, lane_code >> 8)
    ]
    upto = jnp.where(
        lax.broadcasted_iota(I32, (128, 128), 0) <= lax.broadcasted_iota(I32, (128, 128), 1), 1.0, 0.0
    ).astype(BF16)
    before = jnp.where(
        lax.broadcasted_iota(I32, (rows, rows), 1) < lax.broadcasted_iota(I32, (rows, rows), 0), 1.0, 0.0
    ).astype(BF16)
    place = jnp.full((rows, 128), -1.0, F32)
    base = jnp.zeros((1, 1), F32)
    lane = lax.broadcasted_iota(I32, (1, 128), 1)
    spans = jnp.zeros((1, 128), F32)
    for blocks in ORDER:
        member = jnp.where((short > float(STEP) * (blocks - 1)) & (short <= float(STEP) * blocks), 1.0, 0.0)
        within = dot(member.astype(BF16), upto)
        total = jnp.sum(member, axis=1, keepdims=True)
        ahead = dot(before, jnp.broadcast_to(total, (rows, 128)).astype(BF16))
        place = jnp.where(member > 0.0, base + ahead + within - 1.0, place)
        batches = jnp.floor((jnp.sum(total, axis=0, keepdims=True) + (BATCH - 1.0)) / BATCH)
        spans = jnp.where(lane == len(ORDER) - blocks, batches, spans)
        base = base + batches * BATCH
    place = place.astype(I32)
    room = order_ref.shape[1] - 1
    found = jnp.zeros((4 * room, 128), F32)
    for r in range(rows):
        at = place[r : r + 1, :]
        here = jnp.where(lax.broadcasted_iota(I32, (128, 128), 0) == at & 127, 1.0, 0.0)
        ours = lax.broadcasted_iota(I32, (room, 128), 0) == at >> 7
        load = jnp.concatenate([jnp.where(ours, f[r : r + 1, :], 0.0) for f in fields], axis=0)
        found = found + dot(load.astype(BF16), here.astype(BF16), ((1,), (1,)))
    found = [found[i * room : (i + 1) * room, :] for i in range(4)]
    order_ref[0, 0:room, :] = blank - (found[0] + 256.0 * found[1]).astype(I32)
    order_ref[1, 0:room, :] = blank - (found[2] + 256.0 * found[3]).astype(I32)
    order_ref[0, room : room + 1, :] = spans.astype(I32)
    order_ref[1, room : room + 1, :] = spans.astype(I32)


def distances(row_ids, lane_ids, rows, row_feat, lane_feat, dist):
    blank = jnp.zeros((24, 128), F32)
    for k in range(0, len(row_ids), 2):
        left = jnp.concatenate([row_feat[o] for o in row_ids[k : k + 2]], axis=0)
        left = left[:, :rows].astype(BF16)
        a, b = (lane_feat[r] for r in lane_ids[k : k + 2])
        right = jnp.concatenate(
            [
                jnp.concatenate([a, blank], axis=0).astype(BF16),
                jnp.concatenate([blank, b], axis=0).astype(BF16),
            ],
            axis=1,
        )
        dist[k // 2, 0:rows, :] = dot(left, right, ((0,), (0,)))


def tile_sums(row_ids, lane_ids, rows, dist, vals, acc):
    sums = []
    for j in range(len(row_ids)):
        root = lax.rsqrt(dist[j // 2, 0:rows, (j % 2) * 128 : (j % 2) * 128 + 128])
        u = root * root * root
        high = u.astype(BF16)
        low = (u - high.astype(F32)).astype(BF16)
        mine = vals[row_ids[j]][:, :rows]
        theirs = vals[lane_ids[j]]
        if rows == 128:
            on_lane = dot(jnp.concatenate([mine, mine], axis=1), jnp.concatenate([high, low], axis=0))
        else:
            on_lane = dot(mine, high) + dot(mine, low)
        on_row = dot(
            jnp.concatenate([theirs, theirs], axis=1),
            jnp.concatenate([high, low], axis=1),
            ((1,), (1,)),
        )
        sums.append((on_row, on_lane))
    for j, (on_row, on_lane) in enumerate(sums):
        acc[row_ids[j], :, 0:rows] += on_row
        acc[lane_ids[j]] += on_lane


def pair_kernel(
    order,
    arrived_ref,
    row_feat,
    lane_feat,
    vals,
    own_ref,
    part_ref,
    acc,
    dist,
):
    clusters, partners = own_ref.shape[0], arrived_ref.shape[0]
    acc[...] = jnp.zeros_like(acc)
    room = order.shape[1] - 1
    spans = []
    base = 0
    for at in range(len(ORDER)):
        batches = order[0, room, at]
        spans.append((base, batches))
        base = base + batches * BATCH
    for blocks, (base, batches) in zip(ORDER, spans):
        rows = STEP * blocks

        def ids(turn, base=base):
            at = base + turn * BATCH
            line, first = at >> 7, at & 127
            return [[order[s, line, first + j] for j in range(BATCH)] for s in range(2)]

        @pl.when(batches > 0)
        def _(batches=batches, ids=ids, rows=rows):
            distances(*ids(0), rows, row_feat, lane_feat, dist)

            @pl.loop(0, batches)
            def _(turn):
                now = ids(turn)
                ahead = ids(jnp.minimum(turn + 1, batches - 1))
                tile_sums(*now, rows, dist, vals, acc)
                distances(*ahead, rows, row_feat, lane_feat, dist)

    def totals(first):
        parts = [
            jnp.transpose(acc[pl.ds(first, 8), f : f + 8, :], (1, 0, 2)) for f in (0, 8)
        ]
        return [parts[0][c] + (parts[0][4 + c] + parts[1][c]) for c in range(4)]

    @pl.loop(0, clusters // 8, unroll=4)
    def _(g):
        at = pl.multiple_of(g * 8, 8)
        for c, total in enumerate(totals(at)):
            own_ref[pl.ds(at, 8), c * 128 : (c + 1) * 128] = total

    @pl.loop(0, partners // 8, unroll=4)
    def _(g):
        at = pl.multiple_of(g * 8, 8)
        sums = totals(clusters + at)
        here = arrived_ref[pl.ds(at, 8), :]
        for d in range(3):
            near = slice(d * 128, (d + 1) * 128)
            part_ref[pl.ds(at, 8), near] = here[:, 384:512] * (here[:, near] * sums[0] - sums[d + 1])


def shards(
    groups,
    bricks,
    positions,
    charges,
    cluster_fill,
    cluster_cell,
    send_index,
    send_count,
    pair_local,
    pair_dir,
    pair_slot,
    ion_density,
    potential_prev,
    screening,
):
    clusters = cluster_fill.shape[0]
    psize = charges.shape[0] // clusters
    dirs, slots = send_index.shape
    nx, ny, nz = ion_density.shape
    placed = positions.reshape(3, clusters, psize).transpose(1, 0, 2)
    vmem = pl.BlockSpec(memory_space=pltpu.VMEM)
    smem = pl.BlockSpec(memory_space=pltpu.SMEM)
    hbm = pl.BlockSpec(memory_space=pltpu.HBM)
    shape = lambda *dims: jax.ShapeDtypeStruct(dims, F32)
    halo = lambda turns, fields, length: pltpu.VMEM((turns, 2, fields, length, nz), F32)
    block = shape(nx, ny, nz)
    rows = shape(dirs * slots, 4 * psize)
    padded = (nx + 2, ny + 2 * TOP, nz)
    cells = cluster_cell.reshape(clusters // 128, 128)
    late = SWEEPS + 1 - EARLY
    table = (clusters + dirs * slots + 8,)
    pairs = pair_local.shape[0]
    lines = lambda v: v.reshape(pairs // 128, 128)
    room = -(-(pairs + len(ORDER) * BATCH) // 1024) * 8
    still = lambda v: pltpu.with_memory_space_constraint(v, pltpu.HBM)
    ion_density, potential_prev, screening = map(still, (ion_density, potential_prev, screening))
    data, arrived, update, resid, total, ion, into, at_depth, edge, order, *tables = pl.pallas_call(
        functools.partial(send_kernel, groups, bricks),
        out_shape=(
            shape(clusters, 4 * psize),
            rows,
            block,
            block,
            block,
            shape(*padded),
            jax.ShapeDtypeStruct((nx * ny, clusters), BF16),
            shape(clusters, nz),
            jax.ShapeDtypeStruct((2 * nx, clusters), BF16),
            jax.ShapeDtypeStruct((2, room + 1, 128), I32),
            shape(*table, 24, psize),
            shape(*table, 24, psize),
            jax.ShapeDtypeStruct((*table, 16, psize), BF16),
        ),
        in_specs=[smem] + [hbm] * 11,
        out_specs=[vmem] * 13,
        scratch_shapes=[
            pltpu.VMEM((clusters, 3, psize), F32),
            pltpu.VMEM((clusters, psize), F32),
            pltpu.VMEM((clusters // 128, 128), I32),
            pltpu.VMEM((clusters // 128, 128), I32),
            pltpu.VMEM((dirs, slots), I32),
            pltpu.VMEM((pairs // 128, 128), I32),
            pltpu.VMEM((pairs // 128, 128), I32),
            pltpu.VMEM((pairs // 128, 128), I32),
            pltpu.VMEM((nx, ny, nz), F32),
            pltpu.VMEM((dirs * slots, 4 * psize), F32),
            pltpu.VMEM((dirs * slots, 4 * psize), F32),
            halo(EARLY, 2, ny),
            halo(EARLY, 2, ny),
            halo(EARLY, 2, nx),
            halo(EARLY, 2, nx),
            pltpu.VMEM((2, *padded), F32),
            pltpu.SemaphoreType.DMA((11,)),
            pltpu.SemaphoreType.DMA((dirs - 1,)),
            pltpu.SemaphoreType.DMA((dirs - 1,)),
            pltpu.SemaphoreType.DMA((EARLY, 4)),
            pltpu.SemaphoreType.DMA((EARLY, 4)),
        ],
        compiler_params=pltpu.CompilerParams(
            collective_id=0, has_side_effects=True, vmem_limit_bytes=32 << 20
        ),
        name="send",
    )(
        still(send_count),
        still(placed),
        still(charges.reshape(clusters, psize)),
        still(cluster_fill.reshape(clusters // 128, 128)),
        still(cells),
        still(send_index),
        still(lines(pair_local)),
        still(lines(pair_dir)),
        still(lines(pair_slot)),
        ion_density,
        potential_prev,
        screening,
    )
    own_sums, part_sums = pl.pallas_call(
        pair_kernel,
        out_shape=(shape(clusters, 4 * psize), shape(dirs * slots, 3 * psize)),
        in_specs=[smem] + [vmem] * 4,
        out_specs=[vmem] * 2,
        scratch_shapes=[
            pltpu.VMEM((*table, 16, psize), F32),
            pltpu.VMEM((BATCH // 2, psize, 2 * psize), F32),
        ],
        compiler_params=pltpu.CompilerParams(vmem_limit_bytes=28 << 20),
        name="pairs",
    )(order, arrived, *tables)
    padding = shape(*padded)
    pull, pot = pl.pallas_call(
        functools.partial(back_kernel, groups, bricks),
        out_shape=(shape(clusters, 3 * psize), padding),
        in_specs=[hbm] * 2 + [vmem] * 8,
        out_specs=[vmem] * 2,
        scratch_shapes=[
            pltpu.VMEM((dirs, slots), I32),
            pltpu.VMEM((nx, ny, nz), F32),
            pltpu.VMEM((dirs * slots, 3 * psize), F32),
            pltpu.VMEM((nx, ny, nz), F32),
            pltpu.VMEM((nx, ny, nz), F32),
            pltpu.VMEM((3, nx * ny, nz), F32),
            halo(late, 1, ny),
            halo(late, 1, ny),
            halo(late, 1, nx),
            halo(late, 1, nx),
            pltpu.VMEM((2, *padded), F32),
            pltpu.SemaphoreType.DMA((2,)),
            pltpu.SemaphoreType.DMA((dirs - 1,)),
            pltpu.SemaphoreType.DMA((dirs - 1,)),
            pltpu.SemaphoreType.DMA((late, 4)),
            pltpu.SemaphoreType.DMA((late, 4)),
        ],
        compiler_params=pltpu.CompilerParams(
            collective_id=1, has_side_effects=True, vmem_limit_bytes=28 << 20
        ),
        name="back",
    )(still(send_index), screening, data, into, at_depth, own_sums, part_sums, update, resid, total)
    forces, potential, ion_next = pl.pallas_call(
        final_kernel,
        out_shape=(shape(clusters, 3, psize), block, block),
        in_specs=[vmem] * 7,
        out_specs=[hbm] * 3,
        scratch_shapes=[
            pltpu.VMEM((clusters, 3, psize), F32),
            pltpu.VMEM((nx, ny, nz), F32),
            pltpu.SemaphoreType.DMA((4,)),
        ],
        compiler_params=pltpu.CompilerParams(vmem_limit_bytes=28 << 20),
        name="final",
    )(data, pull, pot, ion, into, edge, at_depth)
    return (forces.transpose(1, 0, 2).reshape(3, -1), potential, ion_next)


def solution(mesh):
    in_specs = (
        P(None, ("grp", "brick")),
        P(("grp", "brick")),
        P(("grp", "brick")),
        P(("grp", "brick")),
        P(("grp", "brick"), None),
        P(("grp", "brick"), None),
        P(("grp", "brick")),
        P(("grp", "brick")),
        P(("grp", "brick")),
        P("grp", "brick", None),
        P("grp", "brick", None),
        P("grp", "brick", None),
    )
    out_specs = (P(None, ("grp", "brick")), P("grp", "brick", None), P("grp", "brick", None))
    body = functools.partial(shards, mesh.shape["grp"], mesh.shape["brick"])
    return jax.shard_map(body, mesh=mesh, in_specs=in_specs, out_specs=out_specs, check_vma=False)
```

```python
import functools

import jax
import jax.numpy as jnp
from jax import lax
from jax.experimental import pallas as pl
from jax.experimental.pallas import tpu as pltpu
from jax.sharding import PartitionSpec as P

F32, BF16, I32 = jnp.float32, jnp.bfloat16, jnp.int32
SWEEPS = 4
EARLY = 3
coulomb_scale = 0.02
softening = 0.1
field_scale = 0.5
deposit_scale = 0.2
lowest_eig = 0.01
highest_eig = 1.99
mobility = 0.3
diffusion = 0.2
time_step = 0.2
OFFSETS = ((0, 0), (0, -1), (0, 1), (0, -2), (0, 2), (-1, 0), (1, 0))
MESH = pl.DeviceIdType.MESH
BATCH = 32
STEP = 32
ORDER = (4, 3, 2, 1)
TOP = 8


def split3(v):
    high = v.astype(BF16).astype(F32)
    rest = v - high
    mid = rest.astype(BF16).astype(F32)
    return high, mid, (rest - mid).astype(BF16).astype(F32)


def dot(a, b, dims=((1,), (0,))):
    return lax.dot_general(a, b, (dims, ((), ())), preferred_element_type=F32)


def select_rows(chooser, data, dims=((1,), (0,)), parts=3):
    pieces = split3(data)[:parts]
    total = dot(chooser, pieces[0].astype(BF16), dims)
    for piece in pieces[1:]:
        total = total + dot(chooser, piece.astype(BF16), dims)
    return total


def neighbour(step_g, step_b, groups, bricks):
    g = lax.axis_index("grp")
    b = lax.axis_index("brick")
    return (lax.rem(g + step_g + groups, groups), lax.rem(b + step_b + bricks, bricks))


def greet(groups, bricks):
    barrier = pltpu.get_barrier_semaphore()
    for step in OFFSETS[1:]:
        pl.semaphore_signal(
            barrier, inc=1, device_id=neighbour(*step, groups, bricks), device_id_type=MESH
        )
    return barrier


def slot_row(index_ref):
    return jnp.concatenate([index_ref[k : k + 1, :] for k in range(index_ref.shape[0])], axis=1)


def column(row):
    return jnp.transpose(jnp.broadcast_to(row, (128, 128)))


def columns(values):
    vals = values.astype(F32)
    return jnp.concatenate([column(vals[i : i + 1, :]) for i in range(vals.shape[0])], axis=0)


def neighbours_sum(pad, i):
    rows = pad.shape[1] - 16
    centre = pad[i + 1, TOP : TOP + rows, :]
    total = pad[i + 2, TOP : TOP + rows, :] + pad[i, TOP : TOP + rows, :]
    total = total + pad[i + 1, TOP + 1 : TOP + rows + 1, :] + pad[i + 1, TOP - 1 : TOP + rows - 1, :]
    above, below = z_shifts(centre)
    return centre, total + above + below


def z_shifts(v):
    depth = v.shape[1]
    lane = lax.broadcasted_iota(I32, v.shape, 1)
    above = jnp.where(lane == depth - 1, 0.0, pltpu.roll(v, depth - 1, 1))
    below = jnp.where(lane == 0, 0.0, pltpu.roll(v, 1, 1))
    return above, below


def face_flux(pot_low, pot_high, ion_low, ion_high):
    speed = -mobility * (pot_high - pot_low)
    return (
        jnp.maximum(speed, 0.0) * ion_low
        + jnp.minimum(speed, 0.0) * ion_high
        - diffusion * (ion_high - ion_low)
    )


def inside_flags(groups, bricks):
    g = lax.axis_index("grp")
    b = lax.axis_index("brick")
    return (
        jnp.where(g > 0, 1.0, 0.0),
        jnp.where(g < groups - 1, 1.0, 0.0),
        jnp.where(b > 0, 1.0, 0.0),
        jnp.where(b < bricks - 1, 1.0, 0.0),
    )


def start_halos(axis, fields, turn, x_out, x_in, y_out, y_in, send, recv, groups, bricks):
    nx, ny = fields[0].shape[0] - 2, fields[0].shape[1] - 2 * TOP
    out, into = (y_out, y_in) if axis else (x_out, x_in)
    for f, field in enumerate(fields):
        if axis:
            out[turn, 0, f] = field[1 : nx + 1, TOP, :]
            out[turn, 1, f] = field[1 : nx + 1, TOP + ny - 1, :]
        else:
            out[turn, 0, f] = field[1, TOP : TOP + ny, :]
            out[turn, 1, f] = field[nx, TOP : TOP + ny, :]
    copies = []
    for side in range(2):
        step = 2 * side - 1
        copy = pltpu.make_async_remote_copy(
            src_ref=out.at[turn, side, pl.ds(0, len(fields))],
            dst_ref=into.at[turn, 1 - side, pl.ds(0, len(fields))],
            send_sem=send.at[turn, 2 * axis + side],
            recv_sem=recv.at[turn, 2 * axis + 1 - side],
            device_id=neighbour(step * (1 - axis), step * axis, groups, bricks),
            device_id_type=MESH,
        )
        copy.start()
        copies.append(copy)
    return copies


def place_halos(field, at, x_in, y_in, inside):
    nx, ny = field.shape[0] - 2, field.shape[1] - 2 * TOP
    field[0, TOP : TOP + ny, :] = x_in[at[0], 0, at[1]] * inside[0]
    field[nx + 1, TOP : TOP + ny, :] = x_in[at[0], 1, at[1]] * inside[1]
    field[1 : nx + 1, TOP - 1, :] = y_in[at[0], 0, at[1]] * inside[2]
    field[1 : nx + 1, TOP + ny, :] = y_in[at[0], 1, at[1]] * inside[3]


def clear_halos(field):
    nx, ny = field.shape[0] - 2, field.shape[1] - 2 * TOP
    edge = jnp.zeros(field.shape[1:], F32)
    field[0] = edge
    field[nx + 1] = edge
    for i in range(1, nx + 1):
        field[i, 0:TOP, :] = edge[:TOP]
        field[i, TOP + ny :, :] = edge[:TOP]


def send_rows(source, target, towards, send, recv, groups, bricks):
    slots = source.shape[0] // len(OFFSETS)
    copies = []
    for k in range(1, len(OFFSETS)):
        step_g, step_b = OFFSETS[k]
        copy = pltpu.make_async_remote_copy(
            src_ref=source.at[pl.ds(k * slots, slots), :],
            dst_ref=target.at[pl.ds(k * slots, slots), :],
            send_sem=send.at[k - 1],
            recv_sem=recv.at[k - 1],
            device_id=neighbour(towards * step_g, towards * step_b, groups, bricks),
            device_id_type=MESH,
        )
        copy.start()
        copies.append(copy)
    return copies


def weights():
    middle = 0.5 * (highest_eig + lowest_eig)
    spread = 0.5 * (highest_eig - lowest_eig)
    ratio_ms = middle / spread
    now = 1.0 / ratio_ms
    table = [(0.0, 1.0 / middle)]
    for _ in range(SWEEPS - 1):
        after = 1.0 / (2.0 * ratio_ms - now)
        table.append((after * now, 2.0 * after / spread))
        now = after
    return table


def sweep(turn, held, other, resid, screen, total, whole=False):
    keep, gain = weights()[turn]
    nx, ny, nz = resid.shape

    def plane(i, carry):
        centre, around = neighbours_sum(held, i)
        diag = 6.0 + screen[i]
        rest = resid[i] - (diag * centre - around)
        resid[i] = rest
        update = gain * (rest / diag)
        if turn:
            update = keep * centre + update
            done = total[i] + update
        else:
            done = centre + update
        total[i] = done
        other[i + 1, TOP : TOP + ny, :] = done if whole else update
        return carry

    lax.fori_loop(0, nx, plane, 0, unroll=2)


def add_halos(turn, at, other, resid, screen, total, x_in, y_in, inside):
    gain = weights()[turn][1]
    nx, ny, nz = resid.shape
    for side in range(2):
        i = side * (nx - 1)
        halo = x_in[at, side, 0] * inside[side]
        step = gain * (halo / (6.0 + screen[i]))
        resid[i] = resid[i] + halo
        total[i] = total[i] + step
        other[i + 1, TOP : TOP + ny, :] = other[i + 1, TOP : TOP + ny, :] + step
    for side in range(2):
        j = side * (ny - 1)
        halo = y_in[at, side, 0] * inside[2 + side]
        step = gain * (halo / (6.0 + screen[:, j, :]))
        resid[:, j, :] = resid[:, j, :] + halo
        total[:, j, :] = total[:, j, :] + step
        other[1 : nx + 1, TOP + j, :] = other[1 : nx + 1, TOP + j, :] + step


def cell_tables(cell_ref, nx, ny, nz):
    cell = cell_ref[...]
    clusters = cell.shape[0] * cell.shape[1]
    row_of = cell // nz
    row_line = jnp.concatenate([row_of[i : i + 1, :] for i in range(cell.shape[0])], axis=1)
    into = jnp.where(
        lax.broadcasted_iota(I32, (nx * ny, clusters), 0) == row_line, 1.0, 0.0
    ).astype(BF16)
    k_col = columns(cell - row_of * nz)
    k_col = jnp.concatenate([k_col, k_col], axis=1)
    at_depth = jnp.where(
        lax.broadcasted_iota(I32, (clusters, nz), 1).astype(F32) == k_col, 1.0, 0.0
    )
    i_line = row_line // ny
    j_line = row_line - i_line * ny
    edge_line = jnp.where(j_line == 0, i_line, jnp.where(j_line == ny - 1, nx + i_line, -1))
    edge = jnp.where(
        lax.broadcasted_iota(I32, (2 * nx, clusters), 0) == edge_line, 1.0, 0.0
    ).astype(BF16)
    return into, at_depth, edge


def send_kernel(
    groups,
    bricks,
    count_ref,
    pos_hbm,
    charge_hbm,
    fill_hbm,
    cell_hbm,
    index_hbm,
    local_hbm,
    dir_hbm,
    slot_hbm,
    ion_hbm,
    prev_hbm,
    screen_hbm,
    data_ref,
    arrived_ref,
    update_ref,
    resid_ref,
    total_ref,
    ion_ref,
    into_ref,
    depth_ref,
    edge_ref,
    order_ref,
    row_feat,
    lane_feat,
    vals,
    pos,
    charges,
    fill,
    cells,
    index,
    pair_local,
    pair_dir,
    pair_slot,
    screen,
    out_rows,
    in_rows,
    x_out,
    x_in,
    y_out,
    y_in,
    pad,
    load,
    row_send,
    row_recv,
    halo_send,
    halo_recv,
):
    nx, ny, nz = ion_hbm.shape
    loads = [
        pltpu.make_async_copy(src, dst, load.at[i])
        for i, (src, dst) in enumerate(
            (
                (prev_hbm, pad.at[0, pl.ds(1, nx), pl.ds(TOP, ny), :]),
                (ion_hbm, ion_ref.at[pl.ds(1, nx), pl.ds(TOP, ny), :]),
                (index_hbm, index),
                (fill_hbm, fill),
                (cell_hbm, cells),
                (pos_hbm, pos),
                (charge_hbm, charges),
                (screen_hbm, screen),
                (local_hbm, pair_local),
                (dir_hbm, pair_dir),
                (slot_hbm, pair_slot),
            )
        )
    ]
    for copy in loads:
        copy.start()
    barrier = greet(groups, bricks)
    inside = inside_flags(groups, bricks)
    clear_halos(pad.at[0])
    clear_halos(pad.at[1])
    loads[0].wait()
    exchange = (x_out, x_in, y_out, y_in, halo_send, halo_recv, groups, bricks)
    pl.semaphore_wait(barrier, len(OFFSETS) - 1)
    halos = start_halos(0, [pad.at[0]], 0, *exchange) + start_halos(1, [pad.at[0]], 0, *exchange)
    for copy in loads[1:]:
        copy.wait()
    clusters = charges.shape[0]
    slots = index.shape[1]
    wanted = slot_row(index)
    chooser = jnp.where(
        lax.broadcasted_iota(I32, (clusters, wanted.shape[1]), 0) == wanted, 1.0, 0.0
    ).astype(BF16)
    fill_col = columns(fill[...])
    lane = lax.broadcasted_iota(I32, (clusters, 128), 1).astype(F32)
    charge = charges[...] * jnp.where(lane < fill_col, 1.0, 0.0)
    for d in range(3):
        data_ref[:, d * 128 : (d + 1) * 128] = pos[:, d, :]
    data_ref[:, 384:512] = charge
    out_rows[...] = select_rows(chooser, data_ref[...], ((0,), (0,)))
    slot_id = lax.broadcasted_iota(I32, (slots, 128), 0)
    for k in range(len(OFFSETS)):
        live = jnp.where(slot_id < count_ref[0, k], 1.0, 0.0)
        out_rows[k * slots : (k + 1) * slots, 384:512] = (
            out_rows[k * slots : (k + 1) * slots, 384:512] * live
        )
    sends = send_rows(out_rows, in_rows, -1, row_send, row_recv, groups, bricks)
    ion_halos = start_halos(0, [ion_ref], EARLY, *exchange)
    ion_halos = ion_halos + start_halos(1, [ion_ref], EARLY, *exchange)
    into, at_depth, edge = cell_tables(cells, nx, ny, nz)
    into_ref[...] = into
    edge_ref[...] = edge
    depth_ref[...] = at_depth
    deposit = select_rows(into, at_depth * jnp.sum(charge, axis=1, keepdims=True))
    density = ion_ref[1 : nx + 1, TOP : TOP + ny, :]
    resid_ref[...] = density + deposit_scale * deposit.reshape(nx, ny, nz)
    for turn in range(EARLY):
        held, other = pad.at[turn % 2], pad.at[1 - turn % 2]
        if turn == EARLY - 2:
            features(data_ref, 0, row_feat, lane_feat, vals)
        if turn == EARLY - 1:
            for copy in sends:
                copy.wait()
            arrived_ref[0:slots, :] = out_rows[0:slots, :]
            arrived_ref[slots:, :] = in_rows[slots:, :]
            sort_pairs(
                pair_local,
                pair_dir[...] * slots + pair_slot[...],
                extent(data_ref),
                extent(arrived_ref),
                order_ref,
            )
            partners = arrived_ref.shape[0]
            features(arrived_ref, clusters, row_feat, lane_feat, vals)
            feature_rows(jnp.zeros((8, 512), F32), clusters + partners, row_feat, lane_feat, vals)
        sweep(turn, held, other, resid_ref, screen, total_ref)
        for copy in halos:
            copy.wait()
        add_halos(turn, turn, other, resid_ref, screen, total_ref, x_in, y_in, inside)
        if turn + 1 < EARLY:
            halos = start_halos(0, [other], turn + 1, *exchange)
            halos = halos + start_halos(1, [other], turn + 1, *exchange)
    for copy in ion_halos:
        copy.wait()
    place_halos(ion_ref, (EARLY, 0), x_in, y_in, inside)
    update_ref[...] = pad[EARLY % 2, 1 : nx + 1, TOP : TOP + ny, :]


def back_kernel(
    groups,
    bricks,
    index_hbm,
    screen_hbm,
    data_ref,
    into_ref,
    depth_ref,
    own_ref,
    part_ref,
    update_ref,
    resid_ref,
    total_ref,
    pull_ref,
    pot_ref,
    index,
    screen,
    back,
    resid,
    total,
    efield,
    x_out,
    x_in,
    y_out,
    y_in,
    pad,
    load,
    row_send,
    row_recv,
    halo_send,
    halo_recv,
):
    nx, ny, nz = screen_hbm.shape
    loads = [
        pltpu.make_async_copy(screen_hbm, screen, load.at[0]),
        pltpu.make_async_copy(index_hbm, index, load.at[1]),
    ]
    for copy in loads:
        copy.start()
    barrier = greet(groups, bricks)
    inside = inside_flags(groups, bricks)
    first = pad.at[EARLY % 2]
    clear_halos(pad.at[0])
    clear_halos(pad.at[1])
    clear_halos(pot_ref)
    first[1 : nx + 1, TOP : TOP + ny, :] = update_ref[...]
    exchange = (x_out, x_in, y_out, y_in, halo_send, halo_recv, groups, bricks)
    pl.semaphore_wait(barrier, len(OFFSETS) - 1)
    halos = start_halos(0, [first], 0, *exchange) + start_halos(1, [first], 0, *exchange)
    sends = send_rows(part_ref, back, 1, row_send, row_recv, groups, bricks)
    for copy in loads:
        copy.wait()
    resid[...] = resid_ref[...]
    total[...] = total_ref[...]
    slots = part_ref.shape[0] // len(OFFSETS)
    back[0:slots, :] = part_ref[0:slots, :]
    wanted = slot_row(index)
    clusters = data_ref.shape[0]
    chooser = jnp.where(
        lax.broadcasted_iota(I32, (clusters, wanted.shape[1]), 0) == wanted, 1.0, 0.0
    ).astype(BF16)
    for d in range(3):
        near = slice(d * 128, (d + 1) * 128)
        pull = data_ref[:, near] * own_ref[:, 0:128] - own_ref[:, (d + 1) * 128 : (d + 2) * 128]
        pull_ref[:, near] = coulomb_scale * data_ref[:, 384:512] * pull
    for turn in range(EARLY, SWEEPS):
        held, other = pad.at[turn % 2], pad.at[1 - turn % 2]
        last = turn == SWEEPS - 1
        other = pot_ref if last else other
        sweep(turn, held, other, resid, screen, total, last)
        for copy in halos:
            copy.wait()
        add_halos(turn, turn - EARLY, other, resid, screen, total, x_in, y_in, inside)
        halos = start_halos(0, [other], turn + 1 - EARLY, *exchange)
        halos = halos + start_halos(1, [other], turn + 1 - EARLY, *exchange)

    def field(i, carry):
        lo, hi = TOP, TOP + ny
        above, below = z_shifts(pot_ref[i + 1, lo:hi, :])
        spot = pl.ds(pl.multiple_of(i * ny, ny), ny)
        efield[0, spot, :] = -(pot_ref[i + 2, lo:hi, :] - pot_ref[i, lo:hi, :]) * 0.5
        efield[1, spot, :] = -(pot_ref[i + 1, lo + 1 : hi + 1, :] - pot_ref[i + 1, lo - 1 : hi - 1, :]) * 0.5
        efield[2, spot, :] = -(above - below) * 0.5
        return carry

    lax.fori_loop(0, nx, field, 0, unroll=2)
    for d in range(3):
        seen = select_rows(into_ref[...], efield[d], ((0,), (0,)), 2)
        push = field_scale * jnp.sum(seen * depth_ref[...], axis=1, keepdims=True)
        near = slice(d * 128, (d + 1) * 128)
        pull_ref[:, near] = pull_ref[:, near] + data_ref[:, 384:512] * push
    for copy in sends:
        copy.wait()
    pull_ref[...] = pull_ref[...] + coulomb_scale * select_rows(chooser, back[...])
    for copy in halos:
        copy.wait()
    place_halos(pot_ref, (SWEEPS - EARLY, 0), x_in, y_in, inside)


def final_kernel(
    data_ref,
    pull_ref,
    pot,
    ion,
    into_ref,
    edge_ref,
    depth_ref,
    force_hbm,
    pot_hbm,
    next_hbm,
    force,
    after,
    store,
):
    nx, ny, nz = pot_hbm.shape
    out = [
        pltpu.make_async_copy(pot.at[pl.ds(1, nx), pl.ds(TOP, ny), :], pot_hbm, store.at[0]),
        pltpu.make_async_copy(force, force_hbm, store.at[2]),
    ]
    half = nx // 2
    for k in range(2):
        span = pl.ds(k * half, half)
        out.append(pltpu.make_async_copy(after.at[span], next_hbm.at[span], store.at[2 * k + 1]))
    out[0].start()

    charge = field_scale * data_ref[:, 384:512]
    beside = 0.5 * jnp.concatenate([pot[0, TOP : TOP + ny, :], -pot[nx + 1, TOP : TOP + ny, :]], axis=0)
    across = 0.5 * jnp.concatenate(
        [pot[1 : nx + 1, TOP - 1, :], -pot[1 : nx + 1, TOP + ny, :]], axis=0
    )
    ends = jnp.concatenate([into_ref[0:ny, :], into_ref[(nx - 1) * ny :, :]], axis=0)
    for d, (chooser, halo) in enumerate(((ends, beside), (edge_ref[...], across))):
        seen = select_rows(chooser, halo, ((0,), (0,)), 2)
        push = jnp.sum(seen * depth_ref[...], axis=1, keepdims=True)
        force[:, d, :] = charge * push + pull_ref[:, d * 128 : (d + 1) * 128]
    force[:, 2, :] = pull_ref[:, 256:384]
    out[1].start()

    def finish(i, carry):
        lo, hi = TOP, TOP + ny
        p, n = pot[i + 1, lo:hi, :], ion[i + 1, lo:hi, :]
        px = (pot[i, lo:hi, :], pot[i + 2, lo:hi, :])
        py = (pot[i + 1, lo - 1 : hi - 1, :], pot[i + 1, lo + 1 : hi + 1, :])
        ix = (ion[i, lo:hi, :], ion[i + 2, lo:hi, :])
        iy = (ion[i + 1, lo - 1 : hi - 1, :], ion[i + 1, lo + 1 : hi + 1, :])
        pz = z_shifts(p)[::-1]
        iz = z_shifts(n)[::-1]
        change = jnp.zeros_like(p)
        for ps, ns in ((px, ix), (py, iy), (pz, iz)):
            change = change + (face_flux(p, ps[1], n, ns[1]) - face_flux(ps[0], p, ns[0], n))
        after[i] = n - time_step * change
        return carry

    for k in range(2):
        lax.fori_loop(k * half, (k + 1) * half, finish, 0, unroll=2)
        out[2 + k].start()
    for copy in out:
        copy.wait()


def features(data, base, row_feat, lane_feat, vals):
    @pl.loop(0, data.shape[0] // 8, unroll=4)
    def _(g):
        at = pl.multiple_of(g * 8, 8)
        feature_rows(data[pl.ds(at, 8), :], base + at, row_feat, lane_feat, vals)


def feature_rows(data, base, row_feat, lane_feat, vals):
    spots = [data[:, d * 128 : (d + 1) * 128] for d in range(3)]
    charge = data[:, 384:512]
    here = pl.ds(base, 8)
    one = jnp.ones_like(charge)
    square = jnp.zeros_like(charge)
    left, right, weighed = [], [], []
    for d in range(3):
        high, mid, low = split3(spots[d])
        left += [-2.0 * part for part in (high, high, mid, mid, high, low)]
        right += [high, mid, high, mid, low, high]
        square = square + spots[d] * spots[d]
    left += list(split3(square + softening)) + [one] * 3
    right += [one] * 3 + list(split3(square))
    parts = [split3(v) for v in (charge, charge * spots[0], charge * spots[1], charge * spots[2])]
    for f in range(3):
        weighed += [part[f] for part in parts]
    weighed += [jnp.zeros_like(charge)] * 4
    for rows, table in ((left, row_feat), (right, lane_feat)):
        for k in range(0, len(rows), 8):
            table[here, k : k + 8, :] = jnp.transpose(jnp.stack(rows[k : k + 8]), (1, 0, 2))
    halves = [jnp.transpose(jnp.stack(weighed[k : k + 8]), (1, 0, 2)) for k in (0, 8)]
    vals[here] = jnp.concatenate(halves, axis=1).astype(BF16)


def extent(data):
    charge = data[:, 384:512]
    lane = lax.broadcasted_iota(I32, charge.shape, 1).astype(F32) + 1.0
    return jnp.max(jnp.where(charge != 0.0, lane, 0.0), axis=1, keepdims=True)


def sort_pairs(local_ref, part_ids, own_extent, part_extent, order_ref):
    rows = local_ref.shape[0]
    clusters, partners = own_extent.shape[0], part_extent.shape[0]
    own_lines, part_lines = [], []
    for r in range(rows):
        for lines, ids, ext in (
            (own_lines, local_ref[r : r + 1, :], own_extent),
            (part_lines, part_ids[r : r + 1, :], part_extent),
        ):
            spot = lax.broadcasted_iota(I32, (ext.shape[0], 128), 0)
            lines.append(jnp.sum(jnp.where(spot == ids, ext, 0.0), axis=0, keepdims=True))
    own_len = jnp.concatenate(own_lines, axis=0)
    part_len = jnp.concatenate(part_lines, axis=0)
    short = jnp.minimum(own_len, part_len)
    blank = clusters + partners
    own_code = blank - local_ref[...]
    part_code = partners - part_ids
    swap = part_len < own_len
    row_code = jnp.where(swap, part_code, own_code)
    lane_code = jnp.where(swap, own_code, part_code)
    fields = [
        v.astype(F32)
        for v in (row_code & 255, row_code >> 8, lane_code & 255, lane_code >> 8)
    ]
    upto = jnp.where(
        lax.broadcasted_iota(I32, (128, 128), 0) <= lax.broadcasted_iota(I32, (128, 128), 1), 1.0, 0.0
    ).astype(BF16)
    before = jnp.where(
        lax.broadcasted_iota(I32, (rows, rows), 1) < lax.broadcasted_iota(I32, (rows, rows), 0), 1.0, 0.0
    ).astype(BF16)
    place = jnp.full((rows, 128), -1.0, F32)
    base = jnp.zeros((1, 1), F32)
    lane = lax.broadcasted_iota(I32, (1, 128), 1)
    spans = jnp.zeros((1, 128), F32)
    for blocks in ORDER:
        member = jnp.where((short > float(STEP) * (blocks - 1)) & (short <= float(STEP) * blocks), 1.0, 0.0)
        within = dot(member.astype(BF16), upto)
        total = jnp.sum(member, axis=1, keepdims=True)
        ahead = dot(before, jnp.broadcast_to(total, (rows, 128)).astype(BF16))
        place = jnp.where(member > 0.0, base + ahead + within - 1.0, place)
        batches = jnp.floor((jnp.sum(total, axis=0, keepdims=True) + (BATCH - 1.0)) / BATCH)
        spans = jnp.where(lane == len(ORDER) - blocks, batches, spans)
        base = base + batches * BATCH
    place = place.astype(I32)
    room = order_ref.shape[1] - 1
    found = jnp.zeros((4 * room, 128), F32)
    for r in range(rows):
        at = place[r : r + 1, :]
        here = jnp.where(lax.broadcasted_iota(I32, (128, 128), 0) == at & 127, 1.0, 0.0)
        ours = lax.broadcasted_iota(I32, (room, 128), 0) == at >> 7
        load = jnp.concatenate([jnp.where(ours, f[r : r + 1, :], 0.0) for f in fields], axis=0)
        found = found + dot(load.astype(BF16), here.astype(BF16), ((1,), (1,)))
    found = [found[i * room : (i + 1) * room, :] for i in range(4)]
    order_ref[0, 0:room, :] = blank - (found[0] + 256.0 * found[1]).astype(I32)
    order_ref[1, 0:room, :] = blank - (found[2] + 256.0 * found[3]).astype(I32)
    order_ref[0, room : room + 1, :] = spans.astype(I32)
    order_ref[1, room : room + 1, :] = spans.astype(I32)


def distances(row_ids, lane_ids, rows, row_feat, lane_feat, dist):
    blank = jnp.zeros((24, 128), F32)
    for k in range(0, len(row_ids), 2):
        left = jnp.concatenate([row_feat[o] for o in row_ids[k : k + 2]], axis=0)
        left = left[:, :rows].astype(BF16)
        a, b = (lane_feat[r] for r in lane_ids[k : k + 2])
        right = jnp.concatenate(
            [
                jnp.concatenate([a, blank], axis=0).astype(BF16),
                jnp.concatenate([blank, b], axis=0).astype(BF16),
            ],
            axis=1,
        )
        dist[k // 2, 0:rows, :] = dot(left, right, ((0,), (0,)))


def tile_sums(row_ids, lane_ids, rows, dist, vals, acc):
    sums = []
    for j in range(len(row_ids)):
        root = lax.rsqrt(dist[j // 2, 0:rows, (j % 2) * 128 : (j % 2) * 128 + 128])
        u = root * root * root
        high = u.astype(BF16)
        low = (u - high.astype(F32)).astype(BF16)
        mine = vals[row_ids[j]][:, :rows]
        theirs = vals[lane_ids[j]]
        if rows == 128:
            on_lane = dot(jnp.concatenate([mine, mine], axis=1), jnp.concatenate([high, low], axis=0))
        else:
            on_lane = dot(mine, high) + dot(mine, low)
        on_row = dot(
            jnp.concatenate([theirs, theirs], axis=1),
            jnp.concatenate([high, low], axis=1),
            ((1,), (1,)),
        )
        sums.append((on_row, on_lane))
    for j, (on_row, on_lane) in enumerate(sums):
        acc[row_ids[j], :, 0:rows] += on_row
        acc[lane_ids[j]] += on_lane


def pair_kernel(
    order,
    arrived_ref,
    row_feat,
    lane_feat,
    vals,
    own_ref,
    part_ref,
    acc,
    dist,
):
    clusters, partners = own_ref.shape[0], arrived_ref.shape[0]
    acc[...] = jnp.zeros_like(acc)
    room = order.shape[1] - 1
    spans = []
    base = 0
    for at in range(len(ORDER)):
        batches = order[0, room, at]
        spans.append((base, batches))
        base = base + batches * BATCH
    for blocks, (base, batches) in zip(ORDER, spans):
        rows = STEP * blocks

        def ids(turn, base=base):
            at = base + turn * BATCH
            line, first = at >> 7, at & 127
            return [[order[s, line, first + j] for j in range(BATCH)] for s in range(2)]

        @pl.when(batches > 0)
        def _(batches=batches, ids=ids, rows=rows):
            distances(*ids(0), rows, row_feat, lane_feat, dist)

            @pl.loop(0, batches)
            def _(turn):
                now = ids(turn)
                ahead = ids(jnp.minimum(turn + 1, batches - 1))
                tile_sums(*now, rows, dist, vals, acc)
                distances(*ahead, rows, row_feat, lane_feat, dist)

    def totals(first):
        parts = [
            jnp.transpose(acc[pl.ds(first, 8), f : f + 8, :], (1, 0, 2)) for f in (0, 8)
        ]
        return [parts[0][c] + (parts[0][4 + c] + parts[1][c]) for c in range(4)]

    @pl.loop(0, clusters // 8, unroll=4)
    def _(g):
        at = pl.multiple_of(g * 8, 8)
        for c, total in enumerate(totals(at)):
            own_ref[pl.ds(at, 8), c * 128 : (c + 1) * 128] = total

    @pl.loop(0, partners // 8, unroll=4)
    def _(g):
        at = pl.multiple_of(g * 8, 8)
        sums = totals(clusters + at)
        here = arrived_ref[pl.ds(at, 8), :]
        for d in range(3):
            near = slice(d * 128, (d + 1) * 128)
            part_ref[pl.ds(at, 8), near] = here[:, 384:512] * (here[:, near] * sums[0] - sums[d + 1])


def shards(
    groups,
    bricks,
    positions,
    charges,
    cluster_fill,
    cluster_cell,
    send_index,
    send_count,
    pair_local,
    pair_dir,
    pair_slot,
    ion_density,
    potential_prev,
    screening,
):
    clusters = cluster_fill.shape[0]
    psize = charges.shape[0] // clusters
    dirs, slots = send_index.shape
    nx, ny, nz = ion_density.shape
    placed = positions.reshape(3, clusters, psize).transpose(1, 0, 2)
    vmem = pl.BlockSpec(memory_space=pltpu.VMEM)
    smem = pl.BlockSpec(memory_space=pltpu.SMEM)
    hbm = pl.BlockSpec(memory_space=pltpu.HBM)
    shape = lambda *dims: jax.ShapeDtypeStruct(dims, F32)
    halo = lambda turns, fields, length: pltpu.VMEM((turns, 2, fields, length, nz), F32)
    block = shape(nx, ny, nz)
    rows = shape(dirs * slots, 4 * psize)
    padded = (nx + 2, ny + 2 * TOP, nz)
    cells = cluster_cell.reshape(clusters // 128, 128)
    late = SWEEPS + 1 - EARLY
    table = (clusters + dirs * slots + 8,)
    pairs = pair_local.shape[0]
    lines = lambda v: v.reshape(pairs // 128, 128)
    room = -(-(pairs + len(ORDER) * BATCH) // 1024) * 8
    still = lambda v: pltpu.with_memory_space_constraint(v, pltpu.HBM)
    ion_density, potential_prev, screening = map(still, (ion_density, potential_prev, screening))
    data, arrived, update, resid, total, ion, into, at_depth, edge, order, *tables = pl.pallas_call(
        functools.partial(send_kernel, groups, bricks),
        out_shape=(
            shape(clusters, 4 * psize),
            rows,
            block,
            block,
            block,
            shape(*padded),
            jax.ShapeDtypeStruct((nx * ny, clusters), BF16),
            shape(clusters, nz),
            jax.ShapeDtypeStruct((2 * nx, clusters), BF16),
            jax.ShapeDtypeStruct((2, room + 1, 128), I32),
            shape(*table, 24, psize),
            shape(*table, 24, psize),
            jax.ShapeDtypeStruct((*table, 16, psize), BF16),
        ),
        in_specs=[smem] + [hbm] * 11,
        out_specs=[vmem] * 13,
        scratch_shapes=[
            pltpu.VMEM((clusters, 3, psize), F32),
            pltpu.VMEM((clusters, psize), F32),
            pltpu.VMEM((clusters // 128, 128), I32),
            pltpu.VMEM((clusters // 128, 128), I32),
            pltpu.VMEM((dirs, slots), I32),
            pltpu.VMEM((pairs // 128, 128), I32),
            pltpu.VMEM((pairs // 128, 128), I32),
            pltpu.VMEM((pairs // 128, 128), I32),
            pltpu.VMEM((nx, ny, nz), F32),
            pltpu.VMEM((dirs * slots, 4 * psize), F32),
            pltpu.VMEM((dirs * slots, 4 * psize), F32),
            halo(EARLY + 1, 1, ny),
            halo(EARLY + 1, 1, ny),
            halo(EARLY + 1, 1, nx),
            halo(EARLY + 1, 1, nx),
            pltpu.VMEM((2, *padded), F32),
            pltpu.SemaphoreType.DMA((11,)),
            pltpu.SemaphoreType.DMA((dirs - 1,)),
            pltpu.SemaphoreType.DMA((dirs - 1,)),
            pltpu.SemaphoreType.DMA((EARLY + 1, 4)),
            pltpu.SemaphoreType.DMA((EARLY + 1, 4)),
        ],
        compiler_params=pltpu.CompilerParams(
            collective_id=0, has_side_effects=True, vmem_limit_bytes=32 << 20
        ),
        name="send",
    )(
        still(send_count),
        still(placed),
        still(charges.reshape(clusters, psize)),
        still(cluster_fill.reshape(clusters // 128, 128)),
        still(cells),
        still(send_index),
        still(lines(pair_local)),
        still(lines(pair_dir)),
        still(lines(pair_slot)),
        ion_density,
        potential_prev,
        screening,
    )
    own_sums, part_sums = pl.pallas_call(
        pair_kernel,
        out_shape=(shape(clusters, 4 * psize), shape(dirs * slots, 3 * psize)),
        in_specs=[smem] + [vmem] * 4,
        out_specs=[vmem] * 2,
        scratch_shapes=[
            pltpu.VMEM((*table, 16, psize), F32),
            pltpu.VMEM((BATCH // 2, psize, 2 * psize), F32),
        ],
        compiler_params=pltpu.CompilerParams(vmem_limit_bytes=28 << 20),
        name="pairs",
    )(order, arrived, *tables)
    padding = shape(*padded)
    pull, pot = pl.pallas_call(
        functools.partial(back_kernel, groups, bricks),
        out_shape=(shape(clusters, 3 * psize), padding),
        in_specs=[hbm] * 2 + [vmem] * 8,
        out_specs=[vmem] * 2,
        scratch_shapes=[
            pltpu.VMEM((dirs, slots), I32),
            pltpu.VMEM((nx, ny, nz), F32),
            pltpu.VMEM((dirs * slots, 3 * psize), F32),
            pltpu.VMEM((nx, ny, nz), F32),
            pltpu.VMEM((nx, ny, nz), F32),
            pltpu.VMEM((3, nx * ny, nz), F32),
            halo(late, 1, ny),
            halo(late, 1, ny),
            halo(late, 1, nx),
            halo(late, 1, nx),
            pltpu.VMEM((2, *padded), F32),
            pltpu.SemaphoreType.DMA((2,)),
            pltpu.SemaphoreType.DMA((dirs - 1,)),
            pltpu.SemaphoreType.DMA((dirs - 1,)),
            pltpu.SemaphoreType.DMA((late, 4)),
            pltpu.SemaphoreType.DMA((late, 4)),
        ],
        compiler_params=pltpu.CompilerParams(
            collective_id=1, has_side_effects=True, vmem_limit_bytes=28 << 20
        ),
        name="back",
    )(still(send_index), screening, data, into, at_depth, own_sums, part_sums, update, resid, total)
    forces, potential, ion_next = pl.pallas_call(
        final_kernel,
        out_shape=(shape(clusters, 3, psize), block, block),
        in_specs=[vmem] * 7,
        out_specs=[hbm] * 3,
        scratch_shapes=[
            pltpu.VMEM((clusters, 3, psize), F32),
            pltpu.VMEM((nx, ny, nz), F32),
            pltpu.SemaphoreType.DMA((4,)),
        ],
        compiler_params=pltpu.CompilerParams(vmem_limit_bytes=28 << 20),
        name="final",
    )(data, pull, pot, ion, into, edge, at_depth)
    return (forces.transpose(1, 0, 2).reshape(3, -1), potential, ion_next)


def solution(mesh):
    in_specs = (
        P(None, ("grp", "brick")),
        P(("grp", "brick")),
        P(("grp", "brick")),
        P(("grp", "brick")),
        P(("grp", "brick"), None),
        P(("grp", "brick"), None),
        P(("grp", "brick")),
        P(("grp", "brick")),
        P(("grp", "brick")),
        P("grp", "brick", None),
        P("grp", "brick", None),
        P("grp", "brick", None),
    )
    out_specs = (P(None, ("grp", "brick")), P("grp", "brick", None), P("grp", "brick", None))
    body = functools.partial(shards, mesh.shape["grp"], mesh.shape["brick"])
    return jax.shard_map(body, mesh=mesh, in_specs=in_specs, out_specs=out_specs, check_vma=False)
```
